32 devices in a mesh: slab: 4 (over x, core), grp: 8 (over z, y).
Axes of the slice: x: 2, y: 2, z: 4, core: 2. Of those that a mesh axis runs over, the one named last changes fastest.
Arguments:
- raw_frames: bfloat16 [256, 48, 10752], P('grp', 'slab'), may hold values from -700 to 700
- mask_index: int32 [57344], P(('slab', 'grp')), may hold values from 0 to 516095, as said below
- subspace: bfloat16 [1200, 57344], P(None, ('slab', 'grp')), may hold values from -6 to 6
- rotation: bfloat16 [1456, 1200], replicated, may hold values from -0.15625 to 0.15625
Outputs:
- gram: float32 [1456, 1456], P('grp')
- new_subspace: bfloat16 [1200, 57344], P(None, ('slab', 'grp'))
The draws below stay inside these ranges and needn't reach their ends.
Inputs may be any that keep to these rules, and one draw needn't show every extreme that they name: `mask_index`: entries are distinct flat grid positions that come in runs of 128 consecutive positions, each run starting at a multiple of 128; the 14336 entries of aligned block s lie in z planes s * 12 to (s + 1) * 12 - 1 and rise within the block; the first 3584 of a block lie in its lowest 3 planes, the last 3584 in its highest 3 planes, the others in the planes between.
All inputs are finite; a program needn't handle non-finite values.
Results may differ from the reference program's by a relative error of at most 0.006.
Values may be sent and summed in bfloat16 or wider, within the bound.
A program may use at most 192 MiB of HBM per device.

```python
import math
import jax
import jax.numpy as jnp
from jax import lax

NX = 96
NYX = 10752
RUN = 128
CZ = 12
NZ = 48
RAD = 3
FRAMES = 256
K = 1200
KX = 1456
MV_DEV = 1792
MASKED = 57344
SLAB_ROWS = 14336
RIM_ROWS = 3584


def pick_runs(run_key, run_total, run_count, first_cell):
    chosen = jnp.sort(jax.random.permutation(run_key, run_total)[:run_count]).astype(jnp.int32)
    within = jnp.arange(RUN, dtype=jnp.int32)
    return (chosen[:, None] * RUN + within[None, :]).reshape(-1) + first_cell


def draw_mask_index(key, part):
    slab_count = NZ // CZ
    slab_cells = CZ * NYX
    rim_runs = RAD * NYX // RUN
    middle_runs = (CZ - 2 * RAD) * NYX // RUN
    middle_rows = SLAB_ROWS - 2 * RIM_ROWS

    def per_slab(slab_number):
        slab_key = jax.random.fold_in(key, slab_number)
        lower = pick_runs(jax.random.fold_in(slab_key, 1), rim_runs, RIM_ROWS // RUN, 0)
        upper = pick_runs(jax.random.fold_in(slab_key, 2), rim_runs, RIM_ROWS // RUN, (CZ - RAD) * NYX)
        pieces = [lower]
        if middle_rows > 0:
            pieces.append(pick_runs(jax.random.fold_in(slab_key, 3), middle_runs, middle_rows // RUN, RAD * NYX))
        pieces.append(upper)
        return jnp.concatenate(pieces) + slab_number * slab_cells
    return jax.vmap(per_slab)(jnp.arange(slab_count, dtype=jnp.int32)).reshape(-1).astype(jnp.int32)


def draw_raw_frames(key, part):
    noise_key = jax.random.fold_in(key, 11)
    rough_key = jax.random.fold_in(key, 12)
    depth = jnp.arange(NZ, dtype=jnp.float32) / max(NZ - 1, 1)
    base = jax.random.truncated_normal(noise_key, -4.0, 4.0, (FRAMES, NZ, NYX), jnp.float32)
    depth_scale = jnp.exp(jnp.log(10.0) * depth)
    frame_scale = jnp.exp(jnp.log(3.0) * jnp.arange(FRAMES, dtype=jnp.float32) / max(FRAMES - 1, 1))
    rough = jnp.exp(jax.random.uniform(rough_key, (1, NZ, NYX), jnp.float32, -0.7, 0.7))
    values = base * rough * depth_scale[None, :, None] * frame_scale[:, None, None]
    return values.astype(jnp.bfloat16)


def spiked(result, own_key, source, target, parts, factor):
    owner, partner = [(jnp.arange(result.shape[position]) // (result.shape[position] // parts)).reshape([-1 if axis == position else 1 for axis in range(result.ndim)]) for position in (source, target)]
    chosen = jax.random.permutation(own_key, parts)[partner]
    strong = (owner == chosen) | (owner == (partner + parts // 2) % parts)
    return jnp.where(strong, factor * result, result)


def levels(rng, dims, cuts, smallest, top_value):
    def one(axis_at, blocks):
        steps = jax.random.uniform(jax.random.fold_in(jax.random.fold_in(rng, 6), axis_at), (blocks,), jnp.float32, smallest / len(cuts), top_value / len(cuts))
        return jnp.repeat(jnp.exp(steps), dims[axis_at] // blocks).reshape((-1,) + (1,) * (len(dims) - axis_at - 1))

    gain = one(*cuts[0])
    for cut in cuts[1:]:
        gain = gain * one(*cut)
    return gain


def centred(key, dims, scale, most, split=(), held_as=jnp.bfloat16):
    factor_of = levels(key, dims, split, -0.22, 0.18) if split else 1.0
    entries = jax.random.normal(key, dims, jnp.float32) * scale * factor_of
    return jnp.minimum(jnp.maximum(entries, -most), most).astype(held_as)


def bell_draw_with(key, shape, deviation, most, shards, heavy, kind=jnp.bfloat16):
    drawn = deviation * jax.random.normal(key, shape, jnp.float32)
    if shards:
        drawn = drawn * levels(key, shape, shards, -0.22, 0.18)
    return jnp.clip(spiked(drawn, jax.random.fold_in(key, 3), *heavy), -most, most).astype(kind)


def setup_inputs(seed: int = 0) -> dict:
    splits = jax.random.split(jax.random.key(seed), 5)
    return {
        "raw_frames": draw_raw_frames(jax.random.fold_in(splits[4], 71), 0),
        "mask_index": draw_mask_index(jax.random.fold_in(splits[4], 71), 0),
        "subspace": bell_draw_with(splits[2], (K, MASKED), 1.0, 6.0, ((1, 32),), (1, 0, 16, 2.0)),
        "rotation": centred(splits[3], (KX, K), KX ** -0.5, 0.15625),
    }


smooth_sigma = 1.0617
epsilon = 1e-06

def tap_weights():
    unscaled = [math.exp(-offset * offset / (2.0 * smooth_sigma * smooth_sigma)) for offset in range(-RAD, RAD + 1)]
    summed = sum(unscaled)
    return [weight / summed for weight in unscaled]

def along_rows(volume):
    weights = tap_weights()
    extent = volume.shape[-1]
    column = lax.broadcasted_iota(jnp.int32, (extent,), 0) % NX
    padded = jnp.pad(volume, [(0, 0)] * (volume.ndim - 1) + [(RAD, RAD)])
    summed = jnp.zeros(volume.shape, jnp.float32)
    for offset in range(-RAD, RAD + 1):
        shifted = lax.slice_in_dim(padded, RAD + offset, RAD + offset + extent, axis=volume.ndim - 1)
        inside = (column + offset >= 0) & (column + offset < NX)
        summed = summed + weights[offset + RAD] * jnp.where(inside, shifted, 0.0)
    return summed

def along_columns(volume):
    weights = tap_weights()
    extent = volume.shape[-1]
    reach_cells = RAD * NX
    padded = jnp.pad(volume, [(0, 0)] * (volume.ndim - 1) + [(reach_cells, reach_cells)])
    summed = jnp.zeros(volume.shape, jnp.float32)
    for offset in range(-RAD, RAD + 1):
        begin = reach_cells + offset * NX
        shifted = lax.slice_in_dim(padded, begin, begin + extent, axis=volume.ndim - 1)
        summed = summed + weights[offset + RAD] * shifted
    return summed

def along_depth(padded, slab_depth):
    weights = tap_weights()
    summed = None
    for offset in range(-RAD, RAD + 1):
        shifted = lax.slice_in_dim(padded, RAD + offset, RAD + offset + slab_depth, axis=padded.ndim - 2)
        term = weights[offset + RAD] * shifted
        summed = term if summed is None else summed + term
    return summed

def reference(raw_frames, mask_index, subspace, rotation):

    def one_frame(frame_data):
        planar = along_columns(along_rows(frame_data.astype(jnp.float32)))
        padded = jnp.pad(planar, [(RAD, RAD), (0, 0)])
        volume = along_depth(padded, NZ).reshape(-1)
        return jnp.take(volume, mask_index, axis=0).astype(jnp.bfloat16)
    smoothed = lax.map(one_frame, raw_frames)
    subject_frames = FRAMES // 2
    halves = smoothed.astype(jnp.float32).reshape(2, subject_frames, MASKED)
    centered = (halves - lax.optimization_barrier(jnp.mean(halves, axis=1, keepdims=True))).astype(jnp.bfloat16)
    widened = centered.astype(jnp.float32)
    power = lax.optimization_barrier(jnp.sum(widened * widened, axis=(1, 2)))
    scales = lax.rsqrt(power / (MASKED * subject_frames) + epsilon)
    centered = centered.reshape(FRAMES, MASKED)
    row_scale = jnp.concatenate([jnp.ones((K,), jnp.float32), jnp.repeat(scales, subject_frames)])
    rotation_wide = rotation.astype(jnp.float32)
    basis_rot = rotation_wide[:K]
    first_rot = rotation_wide[K:K + subject_frames]
    second_rot = rotation_wide[K + subject_frames:]
    highest = lax.Precision.HIGHEST
    block_count = MASKED // MV_DEV

    def accumulate(gram_raw, block_index):
        first_col = (block_index * MV_DEV).astype(jnp.int32)
        basis_cols = lax.dynamic_slice_in_dim(subspace, first_col, MV_DEV, 1).astype(jnp.float32)
        data_cols = lax.dynamic_slice_in_dim(centered, first_col, MV_DEV, 1).astype(jnp.float32)
        stacked = jnp.concatenate([basis_cols, data_cols], 0)
        gram_raw = gram_raw + jnp.dot(stacked, stacked.T, precision=highest)
        from_basis = jnp.dot(basis_rot.T, basis_cols, precision=highest)
        from_first = jnp.dot(first_rot.T, data_cols[:subject_frames], precision=highest)
        from_second = jnp.dot(second_rot.T, data_cols[subject_frames:], precision=highest)
        row_block = (from_basis + scales[0] * from_first + scales[1] * from_second).astype(jnp.bfloat16)
        return (gram_raw, row_block)
    gram_raw, pieces = lax.scan(accumulate, jnp.zeros((KX, KX), jnp.float32), jnp.arange(block_count, dtype=jnp.int32))
    new_subspace = jnp.transpose(pieces, (1, 0, 2)).reshape(K, MASKED)
    gram = gram_raw * (row_scale[:, None] * row_scale[None, :]) / MASKED
    return (gram, new_subspace)
```

```python
import functools
import math

import jax
import jax.numpy as jnp
import numpy as np
from jax import lax
from jax.experimental import pallas as pl
from jax.experimental.pallas import tpu as pltpu
from jax.sharding import PartitionSpec as P

NX = 96
RUN = 128
RAD = 3
K = 1200
MESH = pl.DeviceIdType.MESH

smooth_sigma = 1.0617
epsilon = 1e-06

WIDE = 2 * RUN
LEFT = 3 * RUN
SPAN = 8 * RUN


def tap_weights():
    unscaled = [
        math.exp(-offset * offset / (2.0 * smooth_sigma * smooth_sigma))
        for offset in range(-RAD, RAD + 1)
    ]
    summed = sum(unscaled)
    return [weight / summed for weight in unscaled]


def plane_weights():
    taps = np.array(tap_weights())
    kinds = NX // math.gcd(WIDE, NX)
    out = np.zeros((kinds, SPAN, WIDE))
    for kind in range(kinds):
        target = np.arange(WIDE)
        column = (kind * WIDE + target) % NX
        for dy in range(-RAD, RAD + 1):
            for dx in range(-RAD, RAD + 1):
                inside = (column + dx >= 0) & (column + dx < NX)
                source = target + LEFT + dy * NX + dx
                out[kind, source[inside], target[inside]] = taps[dy + RAD] * taps[dx + RAD]
    return out.astype(jnp.bfloat16)


def axes_of(groups, slabs):
    outer = 4 if groups % 4 == 0 else 1
    cores = 2 if slabs % 2 == 0 else 1
    return outer, groups // outer, slabs // cores, cores


def coordinates(sizes):
    slab, grp = lax.axis_index("slab"), lax.axis_index("grp")
    return [grp // sizes[1], lax.rem(grp, sizes[1]), slab // sizes[3], lax.rem(slab, sizes[3])]


def device_at(at, sizes):
    return (at[2] * sizes[3] + at[3], at[0] * sizes[1] + at[1])


def moved(at, sizes, axis, step):
    other = lax.rem(at[axis] + step, sizes[axis])
    return at[:axis] + [other] + at[axis + 1 :], other


class Scatter:
    def __init__(self, sizes, axis, left, src, landed, out, sems):
        self.sizes, self.axis, self.src, self.landed, self.out = sizes, axis, src, landed, out
        self.dim = left.index(axis)
        self.left = [other for other in left if other != axis]
        self.send_sem, self.recv_sem = sems
        self.at = coordinates(sizes)

    def part(self, where):
        return self.src.at[(slice(None),) * self.dim + (where,)]

    def copy(self, step):
        there, other = moved(self.at, self.sizes, self.axis, step)
        return pltpu.make_async_remote_copy(
            src_ref=self.part(other),
            dst_ref=self.landed.at[step - 1],
            send_sem=self.send_sem.at[self.axis, step],
            recv_sem=self.recv_sem.at[self.axis, step],
            device_id=device_at(there, self.sizes),
            device_id_type=MESH,
        )

    def start(self):
        for step in range(1, self.sizes[self.axis]):
            self.copy(step).start()

    def finish(self):
        for step in range(1, self.sizes[self.axis]):
            self.copy(step).wait()
        mine = self.part(self.at[self.axis])
        lead = [self.sizes[axis] for axis in self.left]
        total = math.prod(lead)

        def add(index, _):
            where = []
            for size in reversed(lead):
                where.insert(0, lax.rem(index, size))
                index = index // size
            where = tuple(where)
            value = mine[where].astype(jnp.float32)
            for step in range(self.sizes[self.axis] - 1):
                value = value + self.landed[(step,) + where].astype(jnp.float32)
            self.out[where] = value.astype(self.out.dtype)
            return 0

        lax.fori_loop(0, total, add, 0)


class Gather:
    def __init__(self, sizes, axis, full, first, sems):
        self.sizes, self.axis, self.full, self.first = sizes, axis, full, first
        self.send_sem, self.recv_sem = sems
        self.at = coordinates(sizes)

    def copy(self, step):
        there, _ = moved(self.at, self.sizes, self.axis, step)
        where = (slice(None),) * (self.axis - self.first) + tuple(self.at[self.axis :])
        return pltpu.make_async_remote_copy(
            src_ref=self.full.at[where],
            dst_ref=self.full.at[where],
            send_sem=self.send_sem.at[self.axis, step],
            recv_sem=self.recv_sem.at[self.axis, step],
            device_id=device_at(there, self.sizes),
            device_id_type=MESH,
        )

    def start(self):
        for step in range(1, self.sizes[self.axis]):
            self.copy(step).start()

    def finish(self):
        for step in range(1, self.sizes[self.axis]):
            self.copy(step).wait()


STAGES = (3, 1, 2, 0)


def stage_scratch(sizes, piece):
    out = []
    left = [axis for axis in range(4) if sizes[axis] > 1]
    for axis in STAGES:
        if sizes[axis] == 1:
            continue
        left.remove(axis)
        shape = tuple(sizes[other] for other in left) + piece
        out.append(pltpu.VMEM((sizes[axis] - 1,) + shape, jnp.bfloat16))
        if left:
            out.append(pltpu.VMEM(shape, jnp.bfloat16))
    return out


def stage_sems(sizes):
    most = max(sizes)
    return [pltpu.SemaphoreType.DMA((4, most)) for _ in range(4)]


def scatter_stages(sizes, src, bufs, result, sems):
    stages = []
    left = [0, 1, 2, 3]
    for axis in STAGES:
        if sizes[axis] == 1:
            src = src.at[(slice(None),) * left.index(axis) + (0,)]
            left = [other for other in left if other != axis]
    order = [axis for axis in STAGES if sizes[axis] > 1]
    for number, axis in enumerate(order):
        last = number == len(order) - 1
        out = result if last else bufs[2 * number + 1]
        stages.append(Scatter(sizes, axis, left, src, bufs[2 * number], out, sems))
        left = stages[-1].left
        src = out
    return stages


def place(peer, groups):
    return (peer // groups, lax.rem(peer, groups))


def group_kernel(dims, x_hbm, mask_ref, s_hbm, r_hbm, w_hbm,
                 rows_ref, data_ref, scale_ref, new_hbm,
                 stacked, gram, dpart, up_ref, down_ref, below, above, picked_ref,
                 regrouped, starts, starts_at, power_at, power_sum, w_ref,
                 load_sem, mask_send, mask_recv, rim_send, rim_recv, halo_send, halo_recv,
                 all_send, all_recv, p_send, p_recv, bs_send, bs_recv, bg_send, bg_recv,
                 ds_send, ds_recv, dg_send, dg_recv, *bufs):
    sizes, flat, depth, frames, extent, runs, share, masked, rows_here = dims
    groups, slabs = sizes[0] * sizes[1], sizes[2] * sizes[3]
    total = groups * slabs
    slab, grp = lax.axis_index("slab"), lax.axis_index("grp")
    me = slab * groups + grp
    at = coordinates(sizes)
    upper = lax.rem(slab + 1, slabs)
    lower = lax.rem(slab + slabs - 1, slabs)
    own = runs * groups
    rim_groups = groups * RAD // depth
    rim = rim_groups * runs
    places = extent // RUN
    padded = depth + RAD
    taps = tap_weights()
    data_rows = frames * groups
    order_rows = K + data_rows
    half_rows = data_rows // 2
    across = (((1,), (1,)), ((), ()))

    load_s = pltpu.make_async_copy(s_hbm, stacked.at[pl.ds(0, K)], load_sem.at[1])
    load_w = pltpu.make_async_copy(w_hbm, w_ref, load_sem.at[2])

    barrier = pltpu.get_barrier_semaphore()

    def greet(step, _):
        pl.semaphore_signal(
            barrier, inc=1, device_id=place(lax.rem(me + step, total), groups),
            device_id_type=MESH,
        )
        return 0

    def trade_starts(step):
        return pltpu.make_async_remote_copy(
            src_ref=starts.at[grp], dst_ref=starts.at[grp],
            send_sem=mask_send.at[step], recv_sem=mask_recv.at[step],
            device_id=(slab, lax.rem(grp + step, groups)), device_id_type=MESH,
        )

    def rim_starts(side, there, number, to):
        slot = groups + side * rim_groups + number
        return pltpu.make_async_remote_copy(
            src_ref=starts.at[grp], dst_ref=starts.at[slot],
            send_sem=rim_send.at[to], recv_sem=rim_recv.at[side * rim_groups + number],
            device_id=(there, to), device_id_type=MESH,
        )

    def for_peers(action):
        def one(step, _):
            action(step)
            return 0

        lax.fori_loop(1, groups, one, 0)

    def for_rim(action):
        def one(to, _):
            @pl.when(grp < rim_groups)
            def _():
                action(rim_starts(0, lower, grp, to))

            @pl.when(grp >= groups - rim_groups)
            def _():
                action(rim_starts(1, upper, grp - (groups - rim_groups), to))

            return 0

        lax.fori_loop(0, groups, one, 0)

    def send_starts():
        lane = lax.broadcasted_iota(jnp.int32, (1, RUN), 1)
        first = jnp.zeros((1, RUN), jnp.int32)
        for run in range(runs):
            first = jnp.where(lane == run, mask_ref[run : run + 1, :] - run, first)
        cell = lax.shift_right_arithmetic(first, 7) - slab * (depth * places)
        plane = jnp.zeros((1, RUN), jnp.int32)
        for number in range(1, depth):
            plane = plane + jnp.where(cell >= number * places, 1, 0)
        row = (cell - plane * places) * padded + plane
        row = jnp.minimum(jnp.maximum(row, 0), (places - 1) * padded + depth - 1)
        starts[grp] = jnp.where(lane < runs, row, 0)
        for_peers(lambda step: trade_starts(step).start())
        for_rim(lambda copy: copy.start())

    def await_starts():
        for_peers(lambda step: trade_starts(step).wait())
        for_rim(lambda copy: copy.wait_send())
        for number in range(rim_groups):
            rim_starts(0, lower, number, grp).wait_recv()
            rim_starts(1, upper, number, grp).wait_recv()
        copy = pltpu.make_async_copy(starts, starts_at, load_sem.at[0])
        copy.start()
        copy.wait()

    def halo(src, dst, number, other):
        return pltpu.make_async_remote_copy(
            src_ref=src, dst_ref=dst, send_sem=halo_send.at[number], recv_sem=halo_recv.at[number],
            device_id=(other, grp), device_id_type=MESH,
        )

    halo_up = halo(up_ref, below, 0, upper)
    halo_down = halo(down_ref, above, 1, lower)

    def trade(step):
        other = lax.rem(grp + step, groups)
        return pltpu.make_async_remote_copy(
            src_ref=picked_ref.at[pl.ds(other * runs, runs)], dst_ref=regrouped.at[grp],
            send_sem=all_send.at[step], recv_sem=all_recv.at[step],
            device_id=(slab, other), device_id_type=MESH,
        )

    def start_trades(at_rim):
        for step in range(1, groups):
            other = lax.rem(grp + step, groups)
            inside = (other >= rim_groups) & (other < groups - rim_groups)
            pl.when(jnp.logical_not(inside) if at_rim else inside)(trade(step).start)

    def smooth(x_ref, y_ref):
        load_x = pltpu.make_async_copy(
            x_hbm, x_ref.at[:, :, pl.ds(LEFT, extent)], load_sem.at[3]
        )
        load_x.start()
        load_w.start()
        load_s.start()
        lax.fori_loop(1, total, greet, 0)
        right = x_ref.shape[2] - LEFT - extent
        x_ref[:, :, :LEFT] = jnp.zeros((depth, frames, LEFT), x_ref.dtype)
        x_ref[:, :, LEFT + extent :] = jnp.zeros((depth, frames, right), x_ref.dtype)
        rest = stacked.shape[0] - K
        stacked[K:] = jnp.zeros((rest, stacked.shape[1]), stacked.dtype)

        def blank(number, _):
            y_ref[pl.ds(number * padded, RAD)] = jnp.zeros((RAD, frames, RUN), jnp.float32)
            return 0

        lax.fori_loop(0, places + 1, blank, 0)
        pl.semaphore_wait(barrier, total - 1)
        send_starts()
        load_w.wait()
        load_x.wait()
        kinds = w_ref.shape[0]

        def planar(step, _):
            for kind in range(kinds):
                number = step * kinds + kind
                begin = pl.multiple_of(number * WIDE, WIDE)
                found = jnp.dot(
                    x_ref[:, :, pl.ds(begin, SPAN)].reshape(depth * frames, SPAN),
                    w_ref[kind],
                    preferred_element_type=jnp.float32,
                )
                for side in range(2):
                    y_ref[pl.ds((2 * number + side) * padded + RAD, depth)] = found[
                        :, side * RUN : (side + 1) * RUN
                    ].reshape(depth, frames, RUN)
            return 0

        lax.fori_loop(0, extent // (WIDE * kinds), planar, 0)
        await_starts()

        def pick(slot, run, shift, used):
            row = starts_at[slot, 0, run]
            if shift > 0:
                row = jnp.minimum(row + shift, places * padded)
            if shift < 0:
                row = jnp.maximum(row + shift, -(RAD + 1))
            found = None
            for tap in used:
                term = taps[tap] * y_ref[row + tap]
                found = term if found is None else found + term
            return found

        def over(count, action):
            def one(number, _):
                for run in range(runs):
                    action(number, run)
                return 0

            lax.fori_loop(0, count, one, 0)

        every = range(2 * RAD + 1)

        def one_up(number, run):
            up_ref[number * runs + run] = pick(
                groups + number, run, depth, range(RAD)
            ).astype(up_ref.dtype)

        over(rim_groups, one_up)
        halo_up.start()

        def one_down(number, run):
            down_ref[number * runs + run] = pick(
                groups + rim_groups + number, run, -depth, range(RAD + 1, 2 * RAD + 1)
            ).astype(down_ref.dtype)

        over(rim_groups, one_down)
        halo_down.start()

        def one_inner(number, run):
            slot = number + rim_groups
            picked_ref[slot * runs + run] = pick(slot, run, 0, every).astype(picked_ref.dtype)

        over(groups - 2 * rim_groups, one_inner)
        start_trades(False)
        halo_up.wait()
        halo_down.wait()
        low_part = jnp.where(slab > 0, 1.0, 0.0)
        high_part = jnp.where(slab < slabs - 1, 1.0, 0.0)

        def one_edge(number, run):
            where = number * runs + run
            picked_ref[where] = (
                pick(number, run, 0, every) + low_part * below[where].astype(jnp.float32)
            ).astype(picked_ref.dtype)
            slot = number + groups - rim_groups
            picked_ref[slot * runs + run] = (
                pick(slot, run, 0, every) + high_part * above[where].astype(jnp.float32)
            ).astype(picked_ref.dtype)

        over(rim_groups, one_edge)
        start_trades(True)

    pl.run_scoped(
        smooth,
        pltpu.VMEM((depth, frames, extent + SPAN - WIDE), jnp.bfloat16),
        pltpu.VMEM((places * padded + RAD, frames, RUN), jnp.float32),
    )

    b_bufs, d_bufs = split_bufs(sizes, flat, bufs)
    b_steps = scatter_stages(sizes, gram, b_bufs, rows_ref.at[at[2], at[3]], (bs_send, bs_recv))
    b_steps += [Gather(sizes, axis, rows_ref, 2, (bg_send, bg_recv)) for axis in (2, 3)]
    flat_at = [0, grp, at[2], at[3]]
    d_steps = scatter_stages(flat, dpart, d_bufs, data_ref.at[tuple(flat_at)], (ds_send, ds_recv))
    d_steps += [
        Gather(flat, axis, data_ref, 0, (dg_send, dg_recv)) for axis in range(4) if flat[axis] > 1
    ]

    load_s.wait()
    for group in range(groups):
        first = group * rows_here
        where = (group // sizes[1], group % sizes[1])
        low = first // 16 * 16
        if first < K:
            found = lax.dot_general(
                stacked[low : low + slabs * share + 16], stacked[:K], across,
                preferred_element_type=jnp.float32,
            )
        for number in range(slabs):
            begin = first - low + number * share
            gram[where + (number // sizes[3], number % sizes[3])] = (
                found[begin : begin + share] if first < K else jnp.zeros((share, K), jnp.float32)
            ).astype(gram.dtype)
    b_steps[0].start()

    def finish(regrouped_rows):
        r_ref, out_ref = regrouped_rows
        load_r = pltpu.make_async_copy(r_hbm, r_ref, load_sem.at[4])
        load_r.start()
        regrouped[grp] = picked_ref[pl.ds(grp * runs, runs)]
        for_peers(lambda step: trade(step).wait())
        b_steps[0].finish()
        b_steps[1].start()

        half = groups // 2
        squares = [jnp.zeros((1, RUN), jnp.float32) for _ in range(2)]
        for run in range(runs):
            lanes = slice(run * RUN, (run + 1) * RUN)
            for subject in range(2):
                block = regrouped[subject * half : (subject + 1) * half, run].astype(jnp.float32)
                block = block.reshape(half * frames, RUN)
                mean = jnp.sum(block, axis=0, keepdims=True) * (1.0 / (half * frames))
                rounded = (block - mean).astype(stacked.dtype)
                begin = K + subject * half_rows
                stacked[begin : begin + half_rows, lanes] = rounded
                wide = rounded.astype(jnp.float32)
                squares[subject] = squares[subject] + jnp.sum(wide * wide, axis=0, keepdims=True)
        power_sum[0:1, :] = squares[0]
        power_sum[1:2, :] = squares[1]

        def share_power(axis, count, other):
            first = 0 if axis == 0 else groups

            def copy(step):
                return pltpu.make_async_remote_copy(
                    src_ref=power_sum, dst_ref=power_at.at[first + step],
                    send_sem=p_send.at[first + step], recv_sem=p_recv.at[first + step],
                    device_id=other(step), device_id_type=MESH,
                )

            def start():
                for step in range(1, count):
                    copy(step).start()

            def wait():
                found = power_sum[...]
                for step in range(1, count):
                    copy(step).wait()
                for step in range(1, count):
                    found = found + power_at[first + step]
                power_sum[...] = found

            return start, wait

        start_p, wait_p = share_power(0, groups, lambda step: (slab, lax.rem(grp + step, groups)))
        start_q, wait_q = share_power(1, slabs, lambda step: (lax.rem(slab + step, slabs), grp))
        start_p()

        found = lax.dot_general(
            stacked[K:order_rows], stacked[:order_rows], across,
            preferred_element_type=jnp.float32,
        )
        piece = data_rows // total
        for number in range(total):
            group, part = number // slabs, number % slabs
            dpart[0, group, part // sizes[3], part % sizes[3]] = found[
                number * piece : (number + 1) * piece
            ].astype(dpart.dtype)
        d_steps[0].start()
        wait_p()
        start_q()
        d_steps[0].finish()
        d_steps[1].start()
        b_steps[1].finish()
        b_steps[2].start()
        wait_q()
        power = jnp.sum(power_sum[...], axis=1, keepdims=True)
        scales = lax.rsqrt(power * (1.0 / (masked * half_rows)) + epsilon)
        scale_ref[...] = jnp.broadcast_to(scales, scale_ref.shape)

        load_r.wait()
        edge = K // RUN * RUN
        lane = lax.broadcasted_iota(jnp.int32, (1, order_rows - edge), 1) + edge
        factor = jnp.where(
            lane < K, 1.0, jnp.where(lane < K + half_rows, scales[0:1], scales[1:2])
        )
        r_ref[:, edge:] = (r_ref[:, edge:].astype(jnp.float32) * factor).astype(r_ref.dtype)

        chunk = out_ref.shape[1]
        copies = []

        def rotate(number):
            slot = number % 2
            if number >= 2:
                copies[number - 2].wait()
            rows = slice(number * chunk, (number + 1) * chunk)
            out_ref[slot] = jnp.dot(
                r_ref[rows], stacked[:order_rows], preferred_element_type=jnp.float32
            ).astype(out_ref.dtype)
            copy = pltpu.make_async_copy(
                out_ref.at[slot], new_hbm.at[pl.ds(number * chunk, chunk)], load_sem.at[5 + slot]
            )
            copy.start()
            copies.append(copy)

        count = K // chunk
        rotate(0)
        todo = list(range(1, count))
        d_left, b_left = d_steps[1:], b_steps[2:]
        while d_left or b_left:
            for left in (d_left, b_left):
                if left:
                    left.pop(0).finish()
                    if left:
                        left[0].start()
            if todo:
                rotate(todo.pop(0))
        while todo:
            rotate(todo.pop(0))
        for copy in copies[-2:]:
            copy.wait()

    pl.run_scoped(
        lambda r_ref, out_ref: finish((r_ref, out_ref)),
        pltpu.VMEM((K, order_rows), jnp.bfloat16),
        pltpu.VMEM((2, K // 5, runs * RUN), jnp.bfloat16),
    )


def split_bufs(sizes, flat, bufs):
    count = len(stage_scratch(sizes, (16, RUN)))
    return bufs[:count], bufs[count:]


def run_group(cells, mask, subspace, turned, weights, sizes, flat, masked, rows_here, share):
    depth, frames, extent = cells.shape
    vmem = pl.BlockSpec(memory_space=pltpu.VMEM)
    hbm = pl.BlockSpec(memory_space=pl.ANY)
    groups, slabs = sizes[0] * sizes[1], sizes[2] * sizes[3]
    total = groups * slabs
    runs = mask.shape[0]
    own = groups * runs
    rim_groups = groups * RAD // depth
    rim = rim_groups * runs
    data_rows = frames * groups
    order_rows = K + data_rows
    piece = (share, K)
    d_piece = (data_rows // total, order_rows)
    last = (groups - 1) * rows_here // 16 * 16 + slabs * share + 16
    stacked_rows = max(order_rows, last)
    rim_shape = pltpu.VMEM((rim, frames, RUN), jnp.bfloat16)
    dma = pltpu.SemaphoreType.DMA
    dims = (sizes, flat, depth, frames, extent, runs, share, masked, rows_here)
    slots = groups + 2 * rim_groups
    return pl.pallas_call(
        functools.partial(group_kernel, dims),
        out_shape=(
            jax.ShapeDtypeStruct(tuple(sizes[2:]) + piece, jnp.bfloat16),
            jax.ShapeDtypeStruct(tuple(flat) + d_piece, jnp.bfloat16),
            jax.ShapeDtypeStruct((2, RUN), jnp.float32),
            jax.ShapeDtypeStruct(subspace.shape, jnp.bfloat16),
        ),
        in_specs=[hbm, vmem, hbm, hbm, hbm],
        out_specs=(vmem, vmem, vmem, hbm),
        scratch_shapes=[
            pltpu.VMEM((stacked_rows, runs * RUN), jnp.bfloat16),
            pltpu.VMEM(tuple(sizes) + piece, jnp.bfloat16),
            pltpu.VMEM(tuple(flat) + d_piece, jnp.bfloat16),
            rim_shape, rim_shape, rim_shape, rim_shape,
            pltpu.VMEM((own, frames, RUN), jnp.bfloat16),
            pltpu.VMEM((groups, runs, frames, RUN), jnp.bfloat16),
            pltpu.VMEM((slots, 1, RUN), jnp.int32),
            pltpu.SMEM((slots, 1, RUN), jnp.int32),
            pltpu.VMEM((groups + slabs, 2, RUN), jnp.float32),
            pltpu.VMEM((2, RUN), jnp.float32),
            pltpu.VMEM(weights.shape, jnp.bfloat16),
            dma((7,)),
            dma((groups,)), dma((groups,)),
            dma((groups,)), dma((2 * rim_groups,)),
            dma((2,)), dma((2,)),
            dma((groups,)), dma((groups,)),
            dma((groups + slabs,)), dma((groups + slabs,)),
        ]
        + stage_sems(sizes)
        + stage_sems(flat)
        + stage_scratch(sizes, piece)
        + stage_scratch(flat, d_piece),
        compiler_params=pltpu.CompilerParams(
            collective_id=1, has_side_effects=True, vmem_limit_bytes=62 * 1024 * 1024
        ),
    )(cells, mask, subspace, turned, weights)


def body(raw_frames, mask_index, subspace, rotation):
    frames_here, slab_depth, extent = raw_frames.shape
    per_device = subspace.shape[1]
    group_count = lax.axis_size("grp")
    slab_count = lax.axis_size("slab")
    sizes = axes_of(group_count, slab_count)
    masked = per_device * slab_count * group_count
    frame_count = frames_here * group_count
    subject_frames = frame_count // 2
    order_rows = K + frame_count
    rows_here = order_rows // group_count
    first_row = lax.axis_index("grp") * rows_here
    share = -(-rows_here // (16 * slab_count)) * 16
    flat = (1, group_count) + tuple(sizes[2:])

    basis_rows, data, scales, new_subspace = run_group(
        raw_frames.transpose(1, 0, 2), mask_index.reshape(-1, RUN), subspace, rotation.T,
        jnp.asarray(plane_weights()), sizes, flat, masked, rows_here, share,
    )
    basis_rows = basis_rows.reshape(share * slab_count, K)[:rows_here].astype(jnp.float32)
    data = data.reshape(frame_count, order_rows).astype(jnp.float32)
    row_scale = jnp.concatenate(
        [jnp.ones((K,), jnp.float32), jnp.repeat(scales[:, 0], subject_frames)]
    )
    right = lax.dynamic_slice_in_dim(data, first_row, rows_here, 1).T
    low = jnp.pad(data[:, :K], ((rows_here, rows_here), (0, 0)))
    low = lax.dynamic_slice_in_dim(low, jnp.maximum(first_row - K + rows_here, 0), rows_here, 0)
    owned = jnp.concatenate([basis_rows + low, right], 1)
    owned_scale = lax.dynamic_slice_in_dim(row_scale, first_row, rows_here, 0)
    gram_rows = owned * (owned_scale[:, None] * row_scale[None, :]) / masked
    return (gram_rows, new_subspace)


def solution(mesh):
    placed = (P("grp", "slab", None), P(("slab", "grp")), P(None, ("slab", "grp")), P())
    return jax.shard_map(
        body,
        mesh=mesh,
        in_specs=placed,
        out_specs=(P("grp", None), P(None, ("slab", "grp"))),
        check_vma=False,
    )
```

```python
import functools
import math

import jax
import jax.numpy as jnp
import numpy as np
from jax import lax
from jax.experimental import pallas as pl
from jax.experimental.pallas import tpu as pltpu
from jax.sharding import PartitionSpec as P

NX = 96
RUN = 128
RAD = 3
K = 1200
MESH = pl.DeviceIdType.MESH

smooth_sigma = 1.0617
epsilon = 1e-06

WIDE = 2 * RUN
LEFT = 3 * RUN
SPAN = 8 * RUN


def tap_weights():
    unscaled = [
        math.exp(-offset * offset / (2.0 * smooth_sigma * smooth_sigma))
        for offset in range(-RAD, RAD + 1)
    ]
    summed = sum(unscaled)
    return [weight / summed for weight in unscaled]


def plane_weights():
    taps = np.array(tap_weights())
    kinds = NX // math.gcd(WIDE, NX)
    out = np.zeros((kinds, SPAN, WIDE))
    for kind in range(kinds):
        target = np.arange(WIDE)
        column = (kind * WIDE + target) % NX
        for dy in range(-RAD, RAD + 1):
            for dx in range(-RAD, RAD + 1):
                inside = (column + dx >= 0) & (column + dx < NX)
                source = target + LEFT + dy * NX + dx
                out[kind, source[inside], target[inside]] = taps[dy + RAD] * taps[dx + RAD]
    return out.astype(jnp.bfloat16)


def axes_of(groups, slabs):
    outer = 4 if groups % 4 == 0 else 1
    cores = 2 if slabs % 2 == 0 else 1
    return outer, groups // outer, slabs // cores, cores


def coordinates(sizes):
    slab, grp = lax.axis_index("slab"), lax.axis_index("grp")
    return [grp // sizes[1], lax.rem(grp, sizes[1]), slab // sizes[3], lax.rem(slab, sizes[3])]


def device_at(at, sizes):
    return (at[2] * sizes[3] + at[3], at[0] * sizes[1] + at[1])


def moved(at, sizes, axis, step):
    other = lax.rem(at[axis] + step, sizes[axis])
    return at[:axis] + [other] + at[axis + 1 :], other


class Scatter:
    def __init__(self, sizes, axis, left, src, landed, out, sems):
        self.sizes, self.axis, self.src, self.landed, self.out = sizes, axis, src, landed, out
        self.dim = left.index(axis)
        self.left = [other for other in left if other != axis]
        self.send_sem, self.recv_sem = sems
        self.at = coordinates(sizes)

    def part(self, where):
        return self.src.at[(slice(None),) * self.dim + (where,)]

    def copy(self, step):
        there, other = moved(self.at, self.sizes, self.axis, step)
        return pltpu.make_async_remote_copy(
            src_ref=self.part(other),
            dst_ref=self.landed.at[step - 1],
            send_sem=self.send_sem.at[self.axis, step],
            recv_sem=self.recv_sem.at[self.axis, step],
            device_id=device_at(there, self.sizes),
            device_id_type=MESH,
        )

    def start(self):
        for step in range(1, self.sizes[self.axis]):
            self.copy(step).start()

    def finish(self):
        for step in range(1, self.sizes[self.axis]):
            self.copy(step).wait()
        mine = self.part(self.at[self.axis])
        lead = [self.sizes[axis] for axis in self.left]
        total = math.prod(lead)

        def add(index, _):
            where = []
            for size in reversed(lead):
                where.insert(0, lax.rem(index, size))
                index = index // size
            where = tuple(where)
            value = mine[where].astype(jnp.float32)
            for step in range(self.sizes[self.axis] - 1):
                value = value + self.landed[(step,) + where].astype(jnp.float32)
            self.out[where] = value.astype(self.out.dtype)
            return 0

        lax.fori_loop(0, total, add, 0)


class Gather:
    def __init__(self, sizes, axis, full, first, sems):
        self.sizes, self.axis, self.full, self.first = sizes, axis, full, first
        self.send_sem, self.recv_sem = sems
        self.at = coordinates(sizes)

    def copy(self, step):
        there, _ = moved(self.at, self.sizes, self.axis, step)
        where = (slice(None),) * (self.axis - self.first) + tuple(self.at[self.axis :])
        return pltpu.make_async_remote_copy(
            src_ref=self.full.at[where],
            dst_ref=self.full.at[where],
            send_sem=self.send_sem.at[self.axis, step],
            recv_sem=self.recv_sem.at[self.axis, step],
            device_id=device_at(there, self.sizes),
            device_id_type=MESH,
        )

    def start(self):
        for step in range(1, self.sizes[self.axis]):
            self.copy(step).start()

    def finish(self):
        for step in range(1, self.sizes[self.axis]):
            self.copy(step).wait()


STAGES = (3, 1, 2, 0)


def stage_scratch(sizes, piece):
    out = []
    left = [axis for axis in range(4) if sizes[axis] > 1]
    for axis in STAGES:
        if sizes[axis] == 1:
            continue
        left.remove(axis)
        shape = tuple(sizes[other] for other in left) + piece
        out.append(pltpu.VMEM((sizes[axis] - 1,) + shape, jnp.bfloat16))
        if left:
            out.append(pltpu.VMEM(shape, jnp.bfloat16))
    return out


def stage_sems(sizes):
    most = max(sizes)
    return [pltpu.SemaphoreType.DMA((4, most)) for _ in range(4)]


def scatter_stages(sizes, src, bufs, result, sems):
    stages = []
    left = [0, 1, 2, 3]
    for axis in STAGES:
        if sizes[axis] == 1:
            src = src.at[(slice(None),) * left.index(axis) + (0,)]
            left = [other for other in left if other != axis]
    order = [axis for axis in STAGES if sizes[axis] > 1]
    for number, axis in enumerate(order):
        last = number == len(order) - 1
        out = result if last else bufs[2 * number + 1]
        stages.append(Scatter(sizes, axis, left, src, bufs[2 * number], out, sems))
        left = stages[-1].left
        src = out
    return stages


def place(peer, groups):
    return (peer // groups, lax.rem(peer, groups))


def group_kernel(dims, x_hbm, mask_ref, s_hbm, r_hbm, w_hbm,
                 rows_ref, data_ref, scale_ref, new_hbm,
                 stacked, gram, dpart, up_ref, down_ref, below, above, picked_ref,
                 regrouped, starts, starts_at, power_at, power_sum, w_ref,
                 load_sem, mask_send, mask_recv, rim_send, rim_recv, halo_send, halo_recv,
                 all_send, all_recv, p_send, p_recv, bs_send, bs_recv, bg_send, bg_recv,
                 ds_send, ds_recv, dg_send, dg_recv, *bufs):
    sizes, flat, depth, frames, extent, runs, share, masked, rows_here = dims
    groups, slabs = sizes[0] * sizes[1], sizes[2] * sizes[3]
    total = groups * slabs
    slab, grp = lax.axis_index("slab"), lax.axis_index("grp")
    me = slab * groups + grp
    at = coordinates(sizes)
    upper = lax.rem(slab + 1, slabs)
    lower = lax.rem(slab + slabs - 1, slabs)
    own = runs * groups
    rim_groups = groups * RAD // depth
    rim = rim_groups * runs
    places = extent // RUN
    padded = depth + RAD
    taps = tap_weights()
    data_rows = frames * groups
    order_rows = K + data_rows
    half_rows = data_rows // 2
    across = (((1,), (1,)), ((), ()))

    load_s = pltpu.make_async_copy(s_hbm, stacked.at[pl.ds(0, K)], load_sem.at[1])
    load_w = pltpu.make_async_copy(w_hbm, w_ref, load_sem.at[2])

    barrier = pltpu.get_barrier_semaphore()

    def greet(step, _):
        pl.semaphore_signal(
            barrier, inc=1, device_id=place(lax.rem(me + step, total), groups),
            device_id_type=MESH,
        )
        return 0

    def trade_starts(step):
        return pltpu.make_async_remote_copy(
            src_ref=starts.at[grp], dst_ref=starts.at[grp],
            send_sem=mask_send.at[step], recv_sem=mask_recv.at[step],
            device_id=(slab, lax.rem(grp + step, groups)), device_id_type=MESH,
        )

    def rim_starts(side, there, number, to):
        slot = groups + side * rim_groups + number
        return pltpu.make_async_remote_copy(
            src_ref=starts.at[grp], dst_ref=starts.at[slot],
            send_sem=rim_send.at[to], recv_sem=rim_recv.at[side * rim_groups + number],
            device_id=(there, to), device_id_type=MESH,
        )

    def for_peers(action):
        def one(step, _):
            action(step)
            return 0

        lax.fori_loop(1, groups, one, 0)

    def for_rim(action):
        def one(to, _):
            @pl.when(grp < rim_groups)
            def _():
                action(rim_starts(0, lower, grp, to))

            @pl.when(grp >= groups - rim_groups)
            def _():
                action(rim_starts(1, upper, grp - (groups - rim_groups), to))

            return 0

        lax.fori_loop(0, groups, one, 0)

    def send_starts():
        lane = lax.broadcasted_iota(jnp.int32, (1, RUN), 1)
        first = jnp.zeros((1, RUN), jnp.int32)
        for run in range(runs):
            first = jnp.where(lane == run, mask_ref[run : run + 1, :] - run, first)
        cell = lax.shift_right_arithmetic(first, 7) - slab * (depth * places)
        plane = jnp.zeros((1, RUN), jnp.int32)
        for number in range(1, depth):
            plane = plane + jnp.where(cell >= number * places, 1, 0)
        row = (cell - plane * places) * padded + plane
        row = jnp.minimum(jnp.maximum(row, 0), (places - 1) * padded + depth - 1)
        starts[grp] = jnp.where(lane < runs, row, 0)
        for_peers(lambda step: trade_starts(step).start())
        for_rim(lambda copy: copy.start())

    def await_starts():
        for_peers(lambda step: trade_starts(step).wait())
        for_rim(lambda copy: copy.wait_send())
        for number in range(rim_groups):
            rim_starts(0, lower, number, grp).wait_recv()
            rim_starts(1, upper, number, grp).wait_recv()
        copy = pltpu.make_async_copy(starts, starts_at, load_sem.at[0])
        copy.start()
        copy.wait()

    def halo(src, dst, number, other):
        return pltpu.make_async_remote_copy(
            src_ref=src, dst_ref=dst, send_sem=halo_send.at[number], recv_sem=halo_recv.at[number],
            device_id=(other, grp), device_id_type=MESH,
        )

    halo_up = halo(up_ref, below, 0, upper)
    halo_down = halo(down_ref, above, 1, lower)

    def trade(step):
        other = lax.rem(grp + step, groups)
        return pltpu.make_async_remote_copy(
            src_ref=picked_ref.at[pl.ds(other * runs, runs)], dst_ref=regrouped.at[grp],
            send_sem=all_send.at[step], recv_sem=all_recv.at[step],
            device_id=(slab, other), device_id_type=MESH,
        )

    def start_trades(at_rim):
        for step in range(1, groups):
            other = lax.rem(grp + step, groups)
            inside = (other >= rim_groups) & (other < groups - rim_groups)
            pl.when(jnp.logical_not(inside) if at_rim else inside)(trade(step).start)

    b_bufs, d_bufs = split_bufs(sizes, flat, bufs)
    b_steps = scatter_stages(sizes, gram, b_bufs, rows_ref.at[at[2], at[3]], (bs_send, bs_recv))
    b_steps += [Gather(sizes, axis, rows_ref, 2, (bg_send, bg_recv)) for axis in (2, 3)]
    flat_at = [0, grp, at[2], at[3]]
    d_steps = scatter_stages(flat, dpart, d_bufs, data_ref.at[tuple(flat_at)], (ds_send, ds_recv))
    d_steps += [
        Gather(flat, axis, data_ref, 0, (dg_send, dg_recv)) for axis in range(4) if flat[axis] > 1
    ]

    def basis_gram():
        load_s.wait()
        for group in range(groups):
            first = group * rows_here
            where = (group // sizes[1], group % sizes[1])
            low = first // 16 * 16
            if first < K:
                found = lax.dot_general(
                    stacked[low : low + slabs * share + 16], stacked[:K], across,
                    preferred_element_type=jnp.float32,
                )
            for number in range(slabs):
                begin = first - low + number * share
                gram[where + (number // sizes[3], number % sizes[3])] = (
                    found[begin : begin + share] if first < K else jnp.zeros((share, K), jnp.float32)
                ).astype(gram.dtype)

    def smooth(x_ref, y_ref):
        load_x = pltpu.make_async_copy(
            x_hbm, x_ref.at[:, :, pl.ds(LEFT, extent)], load_sem.at[3]
        )
        load_s.start()
        load_x.start()
        load_w.start()
        lax.fori_loop(1, total, greet, 0)
        right = x_ref.shape[2] - LEFT - extent
        x_ref[:, :, :LEFT] = jnp.zeros((depth, frames, LEFT), x_ref.dtype)
        x_ref[:, :, LEFT + extent :] = jnp.zeros((depth, frames, right), x_ref.dtype)
        rest = stacked.shape[0] - K
        stacked[K:] = jnp.zeros((rest, stacked.shape[1]), stacked.dtype)

        def blank(number, _):
            y_ref[pl.ds(number * padded, RAD)] = jnp.zeros((RAD, frames, RUN), jnp.float32)
            return 0

        lax.fori_loop(0, places + 1, blank, 0)
        basis_gram()
        pl.semaphore_wait(barrier, total - 1)
        b_steps[0].start()
        send_starts()
        load_w.wait()
        load_x.wait()
        kinds = w_ref.shape[0]

        def planar(step, _):
            for kind in range(kinds):
                number = step * kinds + kind
                begin = pl.multiple_of(number * WIDE, WIDE)
                found = jnp.dot(
                    x_ref[:, :, pl.ds(begin, SPAN)].reshape(depth * frames, SPAN),
                    w_ref[kind],
                    preferred_element_type=jnp.float32,
                )
                for side in range(2):
                    y_ref[pl.ds((2 * number + side) * padded + RAD, depth)] = found[
                        :, side * RUN : (side + 1) * RUN
                    ].reshape(depth, frames, RUN)
            return 0

        steps = extent // (WIDE * kinds)
        early = steps // 3
        lax.fori_loop(0, early, planar, 0)
        b_steps[0].finish()
        b_steps[1].start()
        lax.fori_loop(early, steps, planar, 0)
        await_starts()

        def pick(slot, run, shift, used):
            row = starts_at[slot, 0, run]
            if shift > 0:
                row = jnp.minimum(row + shift, places * padded)
            if shift < 0:
                row = jnp.maximum(row + shift, -(RAD + 1))
            found = None
            for tap in used:
                term = taps[tap] * y_ref[row + tap]
                found = term if found is None else found + term
            return found

        def over(count, action):
            def one(number, _):
                for run in range(runs):
                    action(number, run)
                return 0

            lax.fori_loop(0, count, one, 0)

        every = range(2 * RAD + 1)

        def one_up(number, run):
            up_ref[number * runs + run] = pick(
                groups + number, run, depth, range(RAD)
            ).astype(up_ref.dtype)

        over(rim_groups, one_up)
        halo_up.start()

        def one_down(number, run):
            down_ref[number * runs + run] = pick(
                groups + rim_groups + number, run, -depth, range(RAD + 1, 2 * RAD + 1)
            ).astype(down_ref.dtype)

        over(rim_groups, one_down)
        halo_down.start()

        def one_inner(number, run):
            slot = number + rim_groups
            picked_ref[slot * runs + run] = pick(slot, run, 0, every).astype(picked_ref.dtype)

        over(groups - 2 * rim_groups, one_inner)
        start_trades(False)
        halo_up.wait()
        halo_down.wait()
        low_part = jnp.where(slab > 0, 1.0, 0.0)
        high_part = jnp.where(slab < slabs - 1, 1.0, 0.0)

        def one_edge(number, run):
            where = number * runs + run
            picked_ref[where] = (
                pick(number, run, 0, every) + low_part * below[where].astype(jnp.float32)
            ).astype(picked_ref.dtype)
            slot = number + groups - rim_groups
            picked_ref[slot * runs + run] = (
                pick(slot, run, 0, every) + high_part * above[where].astype(jnp.float32)
            ).astype(picked_ref.dtype)

        over(rim_groups, one_edge)
        start_trades(True)

    pl.run_scoped(
        smooth,
        pltpu.VMEM((depth, frames, extent + SPAN - WIDE), jnp.bfloat16),
        pltpu.VMEM((places * padded + RAD, frames, RUN), jnp.float32),
    )

    def finish(regrouped_rows):
        r_ref, rd_ref, sum_ref, out_ref = regrouped_rows
        chunk = out_ref.shape[1]
        count = K // chunk
        load_r = pltpu.make_async_copy(r_hbm, r_ref, load_sem.at[4])
        load_r.start()
        regrouped[grp] = picked_ref[pl.ds(grp * runs, runs)]
        load_r.wait()
        for number in range(count):
            rows = slice(number * chunk, (number + 1) * chunk)
            sum_ref[rows] = jnp.dot(
                r_ref[rows, :K], stacked[:K], preferred_element_type=jnp.float32
            )
            if number == count // 2:
                b_steps[1].finish()
                b_steps[2].start()
        b_steps[2].finish()
        b_steps[3].start()
        for_peers(lambda step: trade(step).wait())

        half = groups // 2
        squares = [jnp.zeros((1, RUN), jnp.float32) for _ in range(2)]
        for run in range(runs):
            lanes = slice(run * RUN, (run + 1) * RUN)
            for subject in range(2):
                block = regrouped[subject * half : (subject + 1) * half, run].astype(jnp.float32)
                block = block.reshape(half * frames, RUN)
                mean = jnp.sum(block, axis=0, keepdims=True) * (1.0 / (half * frames))
                rounded = (block - mean).astype(stacked.dtype)
                begin = K + subject * half_rows
                stacked[begin : begin + half_rows, lanes] = rounded
                wide = rounded.astype(jnp.float32)
                squares[subject] = squares[subject] + jnp.sum(wide * wide, axis=0, keepdims=True)
        power_sum[0:1, :] = squares[0]
        power_sum[1:2, :] = squares[1]

        def share_power(axis, count, other):
            first = 0 if axis == 0 else groups

            def copy(step):
                return pltpu.make_async_remote_copy(
                    src_ref=power_sum, dst_ref=power_at.at[first + step],
                    send_sem=p_send.at[first + step], recv_sem=p_recv.at[first + step],
                    device_id=other(step), device_id_type=MESH,
                )

            def start():
                for step in range(1, count):
                    copy(step).start()

            def wait():
                found = power_sum[...]
                for step in range(1, count):
                    copy(step).wait()
                for step in range(1, count):
                    found = found + power_at[first + step]
                power_sum[...] = found

            return start, wait

        start_p, wait_p = share_power(0, groups, lambda step: (slab, lax.rem(grp + step, groups)))
        start_q, wait_q = share_power(1, slabs, lambda step: (lax.rem(slab + step, slabs), grp))
        start_p()

        found = lax.dot_general(
            stacked[K:order_rows], stacked[:order_rows], across,
            preferred_element_type=jnp.float32,
        )
        piece = data_rows // total
        for number in range(total):
            group, part = number // slabs, number % slabs
            dpart[0, group, part // sizes[3], part % sizes[3]] = found[
                number * piece : (number + 1) * piece
            ].astype(dpart.dtype)
        d_steps[0].start()
        wait_p()
        start_q()
        d_steps[0].finish()
        d_steps[1].start()
        wait_q()
        power = jnp.sum(power_sum[...], axis=1, keepdims=True)
        scales = lax.rsqrt(power * (1.0 / (masked * half_rows)) + epsilon)
        scale_ref[...] = jnp.broadcast_to(scales, scale_ref.shape)

        edge = K // RUN * RUN
        lane = lax.broadcasted_iota(jnp.int32, (1, order_rows - edge), 1) + edge
        factor = jnp.where(
            lane < K, 1.0, jnp.where(lane < K + half_rows, scales[0:1], scales[1:2])
        )
        scaled = r_ref[:, edge:].astype(jnp.float32) * factor
        rd_ref[...] = scaled[:, K - edge :].astype(rd_ref.dtype)

        copies = []

        def rotate(number):
            slot = number % 2
            if number >= 2:
                copies[number - 2].wait()
            rows = slice(number * chunk, (number + 1) * chunk)
            out_ref[slot] = (
                sum_ref[rows]
                + jnp.dot(
                    rd_ref[rows], stacked[K:order_rows], preferred_element_type=jnp.float32
                )
            ).astype(out_ref.dtype)
            copy = pltpu.make_async_copy(
                out_ref.at[slot], new_hbm.at[pl.ds(number * chunk, chunk)], load_sem.at[5 + slot]
            )
            copy.start()
            copies.append(copy)

        rotate(0)
        todo = list(range(1, count))
        d_left, b_left = d_steps[1:], b_steps[3:]
        while d_left or b_left:
            for left in (d_left, b_left):
                if left:
                    left.pop(0).finish()
                    if left:
                        left[0].start()
            if todo:
                rotate(todo.pop(0))
        while todo:
            rotate(todo.pop(0))
        for copy in copies[-2:]:
            copy.wait()

    pl.run_scoped(
        lambda *refs: finish(refs),
        pltpu.VMEM((K, order_rows), jnp.bfloat16),
        pltpu.VMEM((K, data_rows), jnp.bfloat16),
        pltpu.VMEM((K, runs * RUN), jnp.float32),
        pltpu.VMEM((2, K // 5, runs * RUN), jnp.bfloat16),
    )


def split_bufs(sizes, flat, bufs):
    count = len(stage_scratch(sizes, (16, RUN)))
    return bufs[:count], bufs[count:]


def run_group(cells, mask, subspace, turned, weights, sizes, flat, masked, rows_here, share):
    depth, frames, extent = cells.shape
    vmem = pl.BlockSpec(memory_space=pltpu.VMEM)
    hbm = pl.BlockSpec(memory_space=pl.ANY)
    groups, slabs = sizes[0] * sizes[1], sizes[2] * sizes[3]
    total = groups * slabs
    runs = mask.shape[0]
    own = groups * runs
    rim_groups = groups * RAD // depth
    rim = rim_groups * runs
    data_rows = frames * groups
    order_rows = K + data_rows
    piece = (share, K)
    d_piece = (data_rows // total, order_rows)
    last = (groups - 1) * rows_here // 16 * 16 + slabs * share + 16
    stacked_rows = max(order_rows, last)
    rim_shape = pltpu.VMEM((rim, frames, RUN), jnp.bfloat16)
    dma = pltpu.SemaphoreType.DMA
    dims = (sizes, flat, depth, frames, extent, runs, share, masked, rows_here)
    slots = groups + 2 * rim_groups
    return pl.pallas_call(
        functools.partial(group_kernel, dims),
        out_shape=(
            jax.ShapeDtypeStruct(tuple(sizes[2:]) + piece, jnp.bfloat16),
            jax.ShapeDtypeStruct(tuple(flat) + d_piece, jnp.bfloat16),
            jax.ShapeDtypeStruct((2, RUN), jnp.float32),
            jax.ShapeDtypeStruct(subspace.shape, jnp.bfloat16),
        ),
        in_specs=[hbm, vmem, hbm, hbm, hbm],
        out_specs=(vmem, vmem, vmem, hbm),
        scratch_shapes=[
            pltpu.VMEM((stacked_rows, runs * RUN), jnp.bfloat16),
            pltpu.VMEM(tuple(sizes) + piece, jnp.bfloat16),
            pltpu.VMEM(tuple(flat) + d_piece, jnp.bfloat16),
            rim_shape, rim_shape, rim_shape, rim_shape,
            pltpu.VMEM((own, frames, RUN), jnp.bfloat16),
            pltpu.VMEM((groups, runs, frames, RUN), jnp.bfloat16),
            pltpu.VMEM((slots, 1, RUN), jnp.int32),
            pltpu.SMEM((slots, 1, RUN), jnp.int32),
            pltpu.VMEM((groups + slabs, 2, RUN), jnp.float32),
            pltpu.VMEM((2, RUN), jnp.float32),
            pltpu.VMEM(weights.shape, jnp.bfloat16),
            dma((7,)),
            dma((groups,)), dma((groups,)),
            dma((groups,)), dma((2 * rim_groups,)),
            dma((2,)), dma((2,)),
            dma((groups,)), dma((groups,)),
            dma((groups + slabs,)), dma((groups + slabs,)),
        ]
        + stage_sems(sizes)
        + stage_sems(flat)
        + stage_scratch(sizes, piece)
        + stage_scratch(flat, d_piece),
        compiler_params=pltpu.CompilerParams(
            collective_id=1, has_side_effects=True, vmem_limit_bytes=62 * 1024 * 1024
        ),
    )(cells, mask, subspace, turned, weights)


def close_kernel(rows_here, masked, rows_ref, data_ref, scale_ref, new_hbm, gram_ref, out_hbm,
                 wide, turned, low, sem):
    first = lax.axis_index("grp") * rows_here
    data_rows, order_rows = data_ref.shape
    parts = 5
    chunk = K // parts
    copies = [
        pltpu.make_async_copy(
            new_hbm.at[pl.ds(part * chunk, chunk)], out_hbm.at[pl.ds(part * chunk, chunk)],
            sem.at[part],
        )
        for part in range(parts)
    ]
    for copy in copies:
        copy.start()

    def rows_from(ref, start):
        size = -(-rows_here // 8) * 8 + 8
        held = ref[pl.ds(pl.multiple_of(start // 8 * 8, 8), size)]
        return pltpu.roll(held, lax.rem(size - lax.rem(start, 8), size), 0)[:rows_here]

    window = turned.shape[0]
    data = data_ref[...].astype(jnp.float32)
    wide[:, :order_rows] = data
    begin = pl.multiple_of(first // RUN * RUN, RUN)
    turned[...] = wide[:, pl.ds(begin, window)].T
    right = rows_from(turned, first - begin)
    low[:rows_here] = jnp.zeros((rows_here, K), jnp.float32)
    rest = low.shape[0] - rows_here - data_rows
    low[rows_here + data_rows :] = jnp.zeros((rest, K), jnp.float32)
    low[rows_here : rows_here + data_rows] = data[:, :K]
    below = rows_from(low, jnp.maximum(first - K + rows_here, 0))

    half = data_rows // 2
    scales = scale_ref[:, :1]

    def scale_of(index):
        return jnp.where(
            index < K, 1.0, jnp.where(index < K + half, scales[0:1], scales[1:2])
        )

    row = scale_of(lax.broadcasted_iota(jnp.int32, (rows_here, 1), 0) + first)
    row = row * (1.0 / masked)
    column = scale_of(lax.broadcasted_iota(jnp.int32, (1, data_rows), 1) + K)
    basis = rows_ref[...].astype(jnp.float32)[:rows_here]
    gram_ref[:, :K] = (basis + below) * row
    gram_ref[:, K:] = right * (row * column)
    for copy in copies:
        copy.wait()


def close_up(rows, data, scales, new_subspace, rows_here, masked):
    vmem = pl.BlockSpec(memory_space=pltpu.VMEM)
    hbm = pl.BlockSpec(memory_space=pl.ANY)
    data_rows, order_rows = data.shape
    window = -(-(rows_here + RUN) // RUN) * RUN
    wide = (order_rows // RUN) * RUN + window
    return pl.pallas_call(
        functools.partial(close_kernel, rows_here, masked),
        out_shape=(
            jax.ShapeDtypeStruct((rows_here, order_rows), jnp.float32),
            jax.ShapeDtypeStruct(new_subspace.shape, new_subspace.dtype),
        ),
        in_specs=[vmem, vmem, vmem, hbm],
        out_specs=(vmem, hbm),
        scratch_shapes=[
            pltpu.VMEM((data_rows, wide), jnp.float32),
            pltpu.VMEM((window, data_rows), jnp.float32),
            pltpu.VMEM((2 * rows_here + data_rows + 16, K), jnp.float32),
            pltpu.SemaphoreType.DMA((5,)),
        ],
        compiler_params=pltpu.CompilerParams(vmem_limit_bytes=40 * 1024 * 1024),
    )(rows, data, scales, new_subspace)


def body(raw_frames, mask_index, subspace, rotation):
    frames_here, slab_depth, extent = raw_frames.shape
    per_device = subspace.shape[1]
    group_count = lax.axis_size("grp")
    slab_count = lax.axis_size("slab")
    sizes = axes_of(group_count, slab_count)
    masked = per_device * slab_count * group_count
    frame_count = frames_here * group_count
    order_rows = K + frame_count
    rows_here = order_rows // group_count
    share = -(-rows_here // (16 * slab_count)) * 16
    flat = (1, group_count) + tuple(sizes[2:])

    basis_rows, data, scales, new_subspace = run_group(
        raw_frames.transpose(1, 0, 2), mask_index.reshape(-1, RUN), subspace, rotation.T,
        jnp.asarray(plane_weights()), sizes, flat, masked, rows_here, share,
    )
    return close_up(
        basis_rows.reshape(share * slab_count, K), data.reshape(frame_count, order_rows),
        scales, new_subspace, rows_here, masked,
    )


def solution(mesh):
    placed = (P("grp", "slab", None), P(("slab", "grp")), P(None, ("slab", "grp")), P())
    return jax.shard_map(
        body,
        mesh=mesh,
        in_specs=placed,
        out_specs=(P("grp", None), P(None, ("slab", "grp"))),
        check_vma=False,
    )
```

```python
import functools
import math

import jax
import jax.numpy as jnp
import numpy as np
from jax import lax
from jax.experimental import pallas as pl
from jax.experimental.pallas import tpu as pltpu
from jax.sharding import PartitionSpec as P

NX = 96
RUN = 128
RAD = 3
K = 1200
MESH = pl.DeviceIdType.MESH

smooth_sigma = 1.0617
epsilon = 1e-06

WIDE = 2 * RUN
LEFT = 3 * RUN
SPAN = 8 * RUN


def tap_weights():
    unscaled = [
        math.exp(-offset * offset / (2.0 * smooth_sigma * smooth_sigma))
        for offset in range(-RAD, RAD + 1)
    ]
    summed = sum(unscaled)
    return [weight / summed for weight in unscaled]


def plane_weights():
    taps = np.array(tap_weights())
    kinds = NX // math.gcd(WIDE, NX)
    out = np.zeros((kinds, SPAN, WIDE))
    for kind in range(kinds):
        target = np.arange(WIDE)
        column = (kind * WIDE + target) % NX
        for dy in range(-RAD, RAD + 1):
            for dx in range(-RAD, RAD + 1):
                inside = (column + dx >= 0) & (column + dx < NX)
                source = target + LEFT + dy * NX + dx
                out[kind, source[inside], target[inside]] = taps[dy + RAD] * taps[dx + RAD]
    return out.astype(jnp.bfloat16)


def axes_of(groups, slabs):
    outer = 4 if groups % 4 == 0 else 1
    cores = 2 if slabs % 2 == 0 else 1
    return outer, groups // outer, slabs // cores, cores


class Grid:
    def __init__(self, sizes, planes):
        self.full, self.planes = sizes, planes
        z, y, x, cores = sizes
        self.sizes = (z, y * x, cores) if planes else tuple(sizes)

    def here(self):
        _, ys, xs, cores = self.full
        slab, grp = lax.axis_index("slab"), lax.axis_index("grp")
        z, y, x, core = grp // ys, lax.rem(grp, ys), slab // cores, lax.rem(slab, cores)
        return [z, y * xs + x, core] if self.planes else [z, y, x, core]

    def device(self, at):
        _, ys, xs, cores = self.full
        if self.planes:
            at = [at[0], at[1] // xs, lax.rem(at[1], xs), at[2]]
        return (at[2] * cores + at[3], at[0] * ys + at[1])

    def moved(self, at, axis, step):
        other = lax.rem(at[axis] + step, self.sizes[axis])
        return at[:axis] + [other] + at[axis + 1 :], other


class Scatter:
    def __init__(self, grid, axis, left, src, landed, out, sems):
        self.grid, self.axis, self.src, self.landed, self.out = grid, axis, src, landed, out
        self.sizes = grid.sizes
        self.dim = left.index(axis)
        self.left = [other for other in left if other != axis]
        self.send_sem, self.recv_sem = sems
        self.at = grid.here()

    def part(self, where):
        return self.src.at[(slice(None),) * self.dim + (where,)]

    def copy(self, step):
        there, other = self.grid.moved(self.at, self.axis, step)
        return pltpu.make_async_remote_copy(
            src_ref=self.part(other),
            dst_ref=self.landed.at[step - 1],
            send_sem=self.send_sem.at[self.axis, step],
            recv_sem=self.recv_sem.at[self.axis, step],
            device_id=self.grid.device(there),
            device_id_type=MESH,
        )

    def start(self):
        for step in range(1, self.sizes[self.axis]):
            self.copy(step).start()

    def finish(self):
        for step in range(1, self.sizes[self.axis]):
            self.copy(step).wait()
        mine = self.part(self.at[self.axis])
        lead = [self.sizes[axis] for axis in self.left]
        total = math.prod(lead)

        def add(index, _):
            where = []
            for size in reversed(lead):
                where.insert(0, lax.rem(index, size))
                index = index // size
            where = tuple(where)
            value = mine[where].astype(jnp.float32)
            for step in range(self.sizes[self.axis] - 1):
                value = value + self.landed[(step,) + where].astype(jnp.float32)
            self.out[where] = value.astype(self.out.dtype)
            return 0

        lax.fori_loop(0, total, add, 0)


class Gather:
    def __init__(self, grid, axis, done, full, first, sems):
        self.grid, self.sizes, self.axis, self.full = grid, grid.sizes, axis, full
        self.send_sem, self.recv_sem = sems
        self.at = grid.here()
        self.where = tuple(
            slice(None) if other in done else self.at[other] for other in range(first, len(self.sizes))
        )

    def copy(self, step):
        there, _ = self.grid.moved(self.at, self.axis, step)
        return pltpu.make_async_remote_copy(
            src_ref=self.full.at[self.where],
            dst_ref=self.full.at[self.where],
            send_sem=self.send_sem.at[self.axis, step],
            recv_sem=self.recv_sem.at[self.axis, step],
            device_id=self.grid.device(there),
            device_id_type=MESH,
        )

    def start(self):
        for step in range(1, self.sizes[self.axis]):
            self.copy(step).start()

    def finish(self):
        for step in range(1, self.sizes[self.axis]):
            self.copy(step).wait()


def gather_stages(grid, order, full, first, sems):
    stages, done = [], []
    for axis in order:
        if grid.sizes[axis] > 1:
            stages.append(Gather(grid, axis, list(done), full, first, sems))
        done.append(axis)
    return stages


def stage_scratch(sizes, order, piece):
    out = []
    left = [axis for axis in range(len(sizes)) if sizes[axis] > 1]
    for axis in order:
        if sizes[axis] == 1:
            continue
        left.remove(axis)
        shape = tuple(sizes[other] for other in left) + piece
        out.append(pltpu.VMEM((sizes[axis] - 1,) + shape, jnp.bfloat16))
        if left:
            out.append(pltpu.VMEM(shape, jnp.bfloat16))
    return out


def stage_sems(sizes):
    most = max(sizes)
    return [pltpu.SemaphoreType.DMA((4, most)) for _ in range(4)]


def scatter_stages(grid, order, src, bufs, result, sems):
    stages, sizes = [], grid.sizes
    left = list(range(len(sizes)))
    for axis in order:
        if sizes[axis] == 1:
            src = src.at[(slice(None),) * left.index(axis) + (0,)]
            left = [other for other in left if other != axis]
    order = [axis for axis in order if sizes[axis] > 1]
    for number, axis in enumerate(order):
        last = number == len(order) - 1
        out = result if last else bufs[2 * number + 1]
        stages.append(Scatter(grid, axis, left, src, bufs[2 * number], out, sems))
        left = stages[-1].left
        src = out
    return stages


def place(peer, groups):
    return (peer // groups, lax.rem(peer, groups))


def group_kernel(dims, x_hbm, mask_ref, s_hbm, r_hbm, w_hbm,
                 rows_a, rows_b, data_ref, scale_ref, new_hbm,
                 stacked, gram_a, gram_b, dpart, up_ref, down_ref, below, above, picked_ref,
                 regrouped, starts, starts_at, power_at, power_sum, w_ref,
                 load_sem, mask_send, mask_recv, rim_send, rim_recv, halo_send, halo_recv,
                 all_send, all_recv, p_send, p_recv, *bufs):
    sizes, cut, depth, frames, extent, runs, share, masked, rows_here = dims
    groups, slabs = sizes[0] * sizes[1], sizes[2] * sizes[3]
    total = groups * slabs
    slab, grp = lax.axis_index("slab"), lax.axis_index("grp")
    me = slab * groups + grp
    grid, planes = Grid(sizes, False), Grid(sizes, True)
    at, plane_at = grid.here(), planes.here()
    bufs = list(bufs)
    upper = lax.rem(slab + 1, slabs)
    lower = lax.rem(slab + slabs - 1, slabs)
    own = runs * groups
    rim_groups = groups * RAD // depth
    rim = rim_groups * runs
    places = extent // RUN
    padded = depth + RAD
    taps = tap_weights()
    data_rows = frames * groups
    order_rows = K + data_rows
    half_rows = data_rows // 2
    across = (((1,), (1,)), ((), ()))

    load_s = pltpu.make_async_copy(s_hbm, stacked.at[pl.ds(0, K)], load_sem.at[1])
    load_w = pltpu.make_async_copy(w_hbm, w_ref, load_sem.at[2])

    barrier = pltpu.get_barrier_semaphore()

    def greet(step, _):
        pl.semaphore_signal(
            barrier, inc=1, device_id=place(lax.rem(me + step, total), groups),
            device_id_type=MESH,
        )
        return 0

    def trade_starts(step):
        return pltpu.make_async_remote_copy(
            src_ref=starts.at[grp], dst_ref=starts.at[grp],
            send_sem=mask_send.at[step], recv_sem=mask_recv.at[step],
            device_id=(slab, lax.rem(grp + step, groups)), device_id_type=MESH,
        )

    def rim_starts(side, there, number, to):
        slot = groups + side * rim_groups + number
        return pltpu.make_async_remote_copy(
            src_ref=starts.at[grp], dst_ref=starts.at[slot],
            send_sem=rim_send.at[to], recv_sem=rim_recv.at[side * rim_groups + number],
            device_id=(there, to), device_id_type=MESH,
        )

    def for_peers(action):
        def one(step, _):
            action(step)
            return 0

        lax.fori_loop(1, groups, one, 0)

    def for_rim(action):
        def one(to, _):
            @pl.when(grp < rim_groups)
            def _():
                action(rim_starts(0, lower, grp, to))

            @pl.when(grp >= groups - rim_groups)
            def _():
                action(rim_starts(1, upper, grp - (groups - rim_groups), to))

            return 0

        lax.fori_loop(0, groups, one, 0)

    def send_starts():
        lane = lax.broadcasted_iota(jnp.int32, (1, RUN), 1)
        first = jnp.zeros((1, RUN), jnp.int32)
        for run in range(runs):
            first = jnp.where(lane == run, mask_ref[run : run + 1, :] - run, first)
        cell = lax.shift_right_arithmetic(first, 7) - slab * (depth * places)
        plane = jnp.zeros((1, RUN), jnp.int32)
        for number in range(1, depth):
            plane = plane + jnp.where(cell >= number * places, 1, 0)
        row = (cell - plane * places) * padded + plane
        row = jnp.minimum(jnp.maximum(row, 0), (places - 1) * padded + depth - 1)
        starts[grp] = jnp.where(lane < runs, row, 0)
        for_peers(lambda step: trade_starts(step).start())
        for_rim(lambda copy: copy.start())

    def await_starts():
        for_peers(lambda step: trade_starts(step).wait())
        for_rim(lambda copy: copy.wait_send())
        for number in range(rim_groups):
            rim_starts(0, lower, number, grp).wait_recv()
            rim_starts(1, upper, number, grp).wait_recv()
        copy = pltpu.make_async_copy(starts, starts_at, load_sem.at[0])
        copy.start()
        copy.wait()

    def halo(src, dst, number, other):
        return pltpu.make_async_remote_copy(
            src_ref=src, dst_ref=dst, send_sem=halo_send.at[number], recv_sem=halo_recv.at[number],
            device_id=(other, grp), device_id_type=MESH,
        )

    halo_up = halo(up_ref, below, 0, upper)
    halo_down = halo(down_ref, above, 1, lower)

    def trade(step):
        other = lax.rem(grp + step, groups)
        return pltpu.make_async_remote_copy(
            src_ref=picked_ref.at[pl.ds(other * runs, runs)], dst_ref=regrouped.at[grp],
            send_sem=all_send.at[step], recv_sem=all_recv.at[step],
            device_id=(slab, other), device_id_type=MESH,
        )

    def start_trades(at_rim):
        for step in range(1, groups):
            other = lax.rem(grp + step, groups)
            inside = (other >= rim_groups) & (other < groups - rim_groups)
            pl.when(jnp.logical_not(inside) if at_rim else inside)(trade(step).start)

    def take(count):
        taken = bufs[:count]
        del bufs[:count]
        return taken

    def chain(grid, order, back, src, full, first, piece):
        sems = take(4)
        scratch = take(len(stage_scratch(grid.sizes, order, piece)))
        where = tuple((plane_at if grid.planes else at)[first:])
        return scatter_stages(grid, order, src, scratch, full.at[where], sems[:2]) + gather_stages(
            grid, back, full, first, sems[2:]
        )

    a_steps = chain(grid, ORDER_A, (2, 3), gram_a, rows_a, 2, (share, cut))
    b_steps = chain(grid, ORDER_B, (2, 3), gram_b, rows_b, 2, (share, K - cut))
    d_steps = chain(planes, ORDER_D, (0, 1, 2), dpart, data_ref, 0, dpart.shape[3:])

    def advance(steps):
        if steps:
            steps.pop(0).finish()
        if steps:
            steps[0].start()

    def basis_gram(gram, low_column, high_column):
        width = high_column - low_column
        for group in range(groups):
            first = group * rows_here
            where = (group // sizes[1], group % sizes[1])
            low = first // 16 * 16
            if first < K:
                found = lax.dot_general(
                    stacked[low : low + slabs * share + 16], stacked[low_column:high_column],
                    across, preferred_element_type=jnp.float32,
                )
            for number in range(slabs):
                begin = first - low + number * share
                gram[where + (number // sizes[3], number % sizes[3])] = (
                    found[begin : begin + share]
                    if first < K
                    else jnp.zeros((share, width), jnp.float32)
                ).astype(gram.dtype)

    def smooth(x_ref, y_ref):
        load_x = pltpu.make_async_copy(
            x_hbm, x_ref.at[:, :, pl.ds(LEFT, extent)], load_sem.at[3]
        )
        load_s.start()
        load_x.start()
        load_w.start()
        lax.fori_loop(1, total, greet, 0)
        right = x_ref.shape[2] - LEFT - extent
        x_ref[:, :, :LEFT] = jnp.zeros((depth, frames, LEFT), x_ref.dtype)
        x_ref[:, :, LEFT + extent :] = jnp.zeros((depth, frames, right), x_ref.dtype)
        rest = stacked.shape[0] - K
        stacked[K:] = jnp.zeros((rest, stacked.shape[1]), stacked.dtype)

        def blank(number, _):
            y_ref[pl.ds(number * padded, RAD)] = jnp.zeros((RAD, frames, RUN), jnp.float32)
            return 0

        lax.fori_loop(0, places + 1, blank, 0)
        load_s.wait()
        basis_gram(gram_a, 0, cut)
        pl.semaphore_wait(barrier, total - 1)
        a_steps[0].start()
        send_starts()
        load_w.wait()
        load_x.wait()
        kinds = w_ref.shape[0]

        def planar(step, _):
            for kind in range(kinds):
                number = step * kinds + kind
                begin = pl.multiple_of(number * WIDE, WIDE)
                found = jnp.dot(
                    x_ref[:, :, pl.ds(begin, SPAN)].reshape(depth * frames, SPAN),
                    w_ref[kind],
                    preferred_element_type=jnp.float32,
                )
                for side in range(2):
                    y_ref[pl.ds((2 * number + side) * padded + RAD, depth)] = found[
                        :, side * RUN : (side + 1) * RUN
                    ].reshape(depth, frames, RUN)
            return 0

        steps = extent // (WIDE * kinds)
        early = steps // 3
        lax.fori_loop(0, early, planar, 0)
        advance(a_steps)
        lax.fori_loop(early, steps, planar, 0)
        await_starts()

        def pick(slot, run, shift, used):
            row = starts_at[slot, 0, run]
            if shift > 0:
                row = jnp.minimum(row + shift, places * padded)
            if shift < 0:
                row = jnp.maximum(row + shift, -(RAD + 1))
            found = None
            for tap in used:
                term = taps[tap] * y_ref[row + tap]
                found = term if found is None else found + term
            return found

        def over(count, action):
            def one(number, _):
                for run in range(runs):
                    action(number, run)
                return 0

            lax.fori_loop(0, count, one, 0)

        every = range(2 * RAD + 1)

        def one_up(number, run):
            up_ref[number * runs + run] = pick(
                groups + number, run, depth, range(RAD)
            ).astype(up_ref.dtype)

        over(rim_groups, one_up)
        halo_up.start()

        def one_down(number, run):
            down_ref[number * runs + run] = pick(
                groups + rim_groups + number, run, -depth, range(RAD + 1, 2 * RAD + 1)
            ).astype(down_ref.dtype)

        over(rim_groups, one_down)
        halo_down.start()

        def one_inner(number, run):
            slot = number + rim_groups
            picked_ref[slot * runs + run] = pick(slot, run, 0, every).astype(picked_ref.dtype)

        over(groups - 2 * rim_groups, one_inner)
        start_trades(False)
        halo_up.wait()
        halo_down.wait()
        low_part = jnp.where(slab > 0, 1.0, 0.0)
        high_part = jnp.where(slab < slabs - 1, 1.0, 0.0)

        def one_edge(number, run):
            where = number * runs + run
            picked_ref[where] = (
                pick(number, run, 0, every) + low_part * below[where].astype(jnp.float32)
            ).astype(picked_ref.dtype)
            slot = number + groups - rim_groups
            picked_ref[slot * runs + run] = (
                pick(slot, run, 0, every) + high_part * above[where].astype(jnp.float32)
            ).astype(picked_ref.dtype)

        over(rim_groups, one_edge)
        start_trades(True)

    pl.run_scoped(
        smooth,
        pltpu.VMEM((depth, frames, extent + SPAN - WIDE), jnp.bfloat16),
        pltpu.VMEM((places * padded + RAD, frames, RUN), jnp.float32),
    )

    def finish(regrouped_rows):
        r_ref, out_ref = regrouped_rows
        load_r = pltpu.make_async_copy(r_hbm, r_ref, load_sem.at[4])
        load_r.start()
        regrouped[grp] = picked_ref[pl.ds(grp * runs, runs)]
        advance(a_steps)
        basis_gram(gram_b, cut, K)
        b_steps[0].start()
        advance(a_steps)
        advance(b_steps)
        for_peers(lambda step: trade(step).wait())

        half = groups // 2
        squares = [jnp.zeros((1, RUN), jnp.float32) for _ in range(2)]
        for run in range(runs):
            lanes = slice(run * RUN, (run + 1) * RUN)
            for subject in range(2):
                block = regrouped[subject * half : (subject + 1) * half, run].astype(jnp.float32)
                block = block.reshape(half * frames, RUN)
                mean = jnp.sum(block, axis=0, keepdims=True) * (1.0 / (half * frames))
                rounded = (block - mean).astype(stacked.dtype)
                begin = K + subject * half_rows
                stacked[begin : begin + half_rows, lanes] = rounded
                wide = rounded.astype(jnp.float32)
                squares[subject] = squares[subject] + jnp.sum(wide * wide, axis=0, keepdims=True)
        power_sum[0:1, :] = squares[0]
        power_sum[1:2, :] = squares[1]

        def share_power(axis, count, other):
            first = 0 if axis == 0 else groups

            def copy(step):
                return pltpu.make_async_remote_copy(
                    src_ref=power_sum, dst_ref=power_at.at[first + step],
                    send_sem=p_send.at[first + step], recv_sem=p_recv.at[first + step],
                    device_id=other(step), device_id_type=MESH,
                )

            def start():
                for step in range(1, count):
                    copy(step).start()

            def wait():
                found = power_sum[...]
                for step in range(1, count):
                    copy(step).wait()
                for step in range(1, count):
                    found = found + power_at[first + step]
                power_sum[...] = found

            return start, wait

        start_p, wait_p = share_power(0, groups, lambda step: (slab, lax.rem(grp + step, groups)))
        start_q, wait_q = share_power(1, slabs, lambda step: (lax.rem(slab + step, slabs), grp))
        start_p()

        found = lax.dot_general(
            stacked[K:order_rows], stacked[:order_rows], across,
            preferred_element_type=jnp.float32,
        )
        piece = data_rows // total
        for number in range(total):
            line, core = number // sizes[3], number % sizes[3]
            dpart[line // planes.sizes[1], line % planes.sizes[1], core] = found[
                number * piece : (number + 1) * piece
            ].astype(dpart.dtype)
        d_steps[0].start()
        wait_p()
        start_q()
        advance(d_steps)
        advance(a_steps)
        wait_q()
        power = jnp.sum(power_sum[...], axis=1, keepdims=True)
        scales = lax.rsqrt(power * (1.0 / (masked * half_rows)) + epsilon)
        scale_ref[...] = jnp.broadcast_to(scales, scale_ref.shape)

        load_r.wait()
        edge = K // RUN * RUN
        lane = lax.broadcasted_iota(jnp.int32, (1, order_rows - edge), 1) + edge
        factor = jnp.where(
            lane < K, 1.0, jnp.where(lane < K + half_rows, scales[0:1], scales[1:2])
        )
        r_ref[:, edge:] = (r_ref[:, edge:].astype(jnp.float32) * factor).astype(r_ref.dtype)

        chunk = out_ref.shape[1]
        copies = []

        def rotate(number):
            slot = number % 2
            if number >= 2:
                copies[number - 2].wait()
            rows = slice(number * chunk, (number + 1) * chunk)
            out_ref[slot] = jnp.dot(
                r_ref[rows], stacked[:order_rows], preferred_element_type=jnp.float32
            ).astype(out_ref.dtype)
            copy = pltpu.make_async_copy(
                out_ref.at[slot], new_hbm.at[pl.ds(number * chunk, chunk)], load_sem.at[5 + slot]
            )
            copy.start()
            copies.append(copy)

        count = K // chunk
        rotate(0)
        todo = list(range(1, count))
        while d_steps or a_steps or b_steps:
            for steps in (d_steps, a_steps, b_steps):
                advance(steps)
            if todo:
                rotate(todo.pop(0))
        while todo:
            rotate(todo.pop(0))
        for copy in copies[-2:]:
            copy.wait()

    pl.run_scoped(
        lambda r_ref, out_ref: finish((r_ref, out_ref)),
        pltpu.VMEM((K, order_rows), jnp.bfloat16),
        pltpu.VMEM((2, K // 5, runs * RUN), jnp.bfloat16),
    )


ORDER_A, ORDER_B, ORDER_D = (3, 1, 2, 0), (3, 2, 1, 0), (2, 1, 0)


def run_group(cells, mask, subspace, turned, weights, sizes, masked, rows_here, share):
    depth, frames, extent = cells.shape
    vmem = pl.BlockSpec(memory_space=pltpu.VMEM)
    hbm = pl.BlockSpec(memory_space=pl.ANY)
    groups, slabs = sizes[0] * sizes[1], sizes[2] * sizes[3]
    total = groups * slabs
    runs = mask.shape[0]
    own = groups * runs
    rim_groups = groups * RAD // depth
    rim = rim_groups * runs
    data_rows = frames * groups
    order_rows = K + data_rows
    cut = -(-K // (2 * RUN)) * RUN
    planes = Grid(sizes, True)
    flat = planes.sizes
    d_piece = (data_rows // total, order_rows)
    last = (groups - 1) * rows_here // 16 * 16 + slabs * share + 16
    stacked_rows = max(order_rows, last)
    rim_shape = pltpu.VMEM((rim, frames, RUN), jnp.bfloat16)
    dma = pltpu.SemaphoreType.DMA
    dims = (sizes, cut, depth, frames, extent, runs, share, masked, rows_here)
    slots = groups + 2 * rim_groups
    return pl.pallas_call(
        functools.partial(group_kernel, dims),
        out_shape=(
            jax.ShapeDtypeStruct(tuple(sizes[2:]) + (share, cut), jnp.bfloat16),
            jax.ShapeDtypeStruct(tuple(sizes[2:]) + (share, K - cut), jnp.bfloat16),
            jax.ShapeDtypeStruct(tuple(flat) + d_piece, jnp.bfloat16),
            jax.ShapeDtypeStruct((2, RUN), jnp.float32),
            jax.ShapeDtypeStruct(subspace.shape, jnp.bfloat16),
        ),
        in_specs=[hbm, vmem, hbm, hbm, hbm],
        out_specs=(vmem, vmem, vmem, vmem, hbm),
        scratch_shapes=[
            pltpu.VMEM((stacked_rows, runs * RUN), jnp.bfloat16),
            pltpu.VMEM(tuple(sizes) + (share, cut), jnp.bfloat16),
            pltpu.VMEM(tuple(sizes) + (share, K - cut), jnp.bfloat16),
            pltpu.VMEM(tuple(flat) + d_piece, jnp.bfloat16),
            rim_shape, rim_shape, rim_shape, rim_shape,
            pltpu.VMEM((own, frames, RUN), jnp.bfloat16),
            pltpu.VMEM((groups, runs, frames, RUN), jnp.bfloat16),
            pltpu.VMEM((slots, 1, RUN), jnp.int32),
            pltpu.SMEM((slots, 1, RUN), jnp.int32),
            pltpu.VMEM((groups + slabs, 2, RUN), jnp.float32),
            pltpu.VMEM((2, RUN), jnp.float32),
            pltpu.VMEM(weights.shape, jnp.bfloat16),
            dma((7,)),
            dma((groups,)), dma((groups,)),
            dma((groups,)), dma((2 * rim_groups,)),
            dma((2,)), dma((2,)),
            dma((groups,)), dma((groups,)),
            dma((groups + slabs,)), dma((groups + slabs,)),
        ]
        + stage_sems(sizes)
        + stage_scratch(sizes, ORDER_A, (share, cut))
        + stage_sems(sizes)
        + stage_scratch(sizes, ORDER_B, (share, K - cut))
        + stage_sems(flat)
        + stage_scratch(flat, ORDER_D, d_piece),
        compiler_params=pltpu.CompilerParams(
            collective_id=1, has_side_effects=True, vmem_limit_bytes=62 * 1024 * 1024
        ),
    )(cells, mask, subspace, turned, weights)


def close_kernel(rows_here, masked, a_hbm, b_hbm, data_hbm, scale_hbm, new_hbm, gram_ref,
                 out_hbm, a_ref, b_ref, data_ref, scale_ref, wide, turned, low, sem):
    first = lax.axis_index("grp") * rows_here
    data_rows, order_rows = data_ref.shape
    parts = 5
    chunk = K // parts
    copies = [
        pltpu.make_async_copy(
            new_hbm.at[pl.ds(part * chunk, chunk)], out_hbm.at[pl.ds(part * chunk, chunk)],
            sem.at[part],
        )
        for part in range(parts)
    ]
    loads = [
        pltpu.make_async_copy(source, target, sem.at[parts + number])
        for number, (source, target) in enumerate(
            ((data_hbm, data_ref), (scale_hbm, scale_ref), (a_hbm, a_ref), (b_hbm, b_ref))
        )
    ]
    for copy in loads + copies:
        copy.start()
    for copy in loads:
        copy.wait()

    def rows_from(ref, start):
        size = -(-rows_here // 8) * 8 + 8
        held = ref[pl.ds(pl.multiple_of(start // 8 * 8, 8), size)]
        return pltpu.roll(held, lax.rem(size - lax.rem(start, 8), size), 0)[:rows_here]

    window = turned.shape[0]
    data = data_ref[...].astype(jnp.float32)
    wide[:, :order_rows] = data
    begin = pl.multiple_of(first // RUN * RUN, RUN)
    turned[...] = wide[:, pl.ds(begin, window)].T
    right = rows_from(turned, first - begin)
    low[:rows_here] = jnp.zeros((rows_here, K), jnp.float32)
    rest = low.shape[0] - rows_here - data_rows
    low[rows_here + data_rows :] = jnp.zeros((rest, K), jnp.float32)
    low[rows_here : rows_here + data_rows] = data[:, :K]
    below = rows_from(low, jnp.maximum(first - K + rows_here, 0))

    half = data_rows // 2
    scales = scale_ref[:, :1]

    def scale_of(index):
        return jnp.where(
            index < K, 1.0, jnp.where(index < K + half, scales[0:1], scales[1:2])
        )

    row = scale_of(lax.broadcasted_iota(jnp.int32, (rows_here, 1), 0) + first)
    row = row * (1.0 / masked)
    column = scale_of(lax.broadcasted_iota(jnp.int32, (1, data_rows), 1) + K)
    cut = a_ref.shape[1]
    gram_ref[:, :cut] = (a_ref[...].astype(jnp.float32)[:rows_here] + below[:, :cut]) * row
    gram_ref[:, cut:K] = (b_ref[...].astype(jnp.float32)[:rows_here] + below[:, cut:]) * row
    gram_ref[:, K:] = right * (row * column)
    for copy in copies:
        copy.wait()


def close_up(rows_a, rows_b, data, scales, new_subspace, rows_here, masked):
    vmem = pl.BlockSpec(memory_space=pltpu.VMEM)
    hbm = pl.BlockSpec(memory_space=pl.ANY)
    data_rows, order_rows = data.shape
    window = -(-(rows_here + RUN) // RUN) * RUN
    wide = (order_rows // RUN) * RUN + window
    return pl.pallas_call(
        functools.partial(close_kernel, rows_here, masked),
        out_shape=(
            jax.ShapeDtypeStruct((rows_here, order_rows), jnp.float32),
            jax.ShapeDtypeStruct(new_subspace.shape, new_subspace.dtype),
        ),
        in_specs=[hbm] * 5,
        out_specs=(vmem, hbm),
        scratch_shapes=[
            pltpu.VMEM(rows_a.shape, rows_a.dtype),
            pltpu.VMEM(rows_b.shape, rows_b.dtype),
            pltpu.VMEM(data.shape, data.dtype),
            pltpu.VMEM(scales.shape, scales.dtype),
            pltpu.VMEM((data_rows, wide), jnp.float32),
            pltpu.VMEM((window, data_rows), jnp.float32),
            pltpu.VMEM((2 * rows_here + data_rows + 16, K), jnp.float32),
            pltpu.SemaphoreType.DMA((9,)),
        ],
        compiler_params=pltpu.CompilerParams(vmem_limit_bytes=62 * 1024 * 1024),
    )(rows_a, rows_b, data, scales, new_subspace)


def body(raw_frames, mask_index, subspace, rotation):
    frames_here, slab_depth, extent = raw_frames.shape
    per_device = subspace.shape[1]
    group_count = lax.axis_size("grp")
    slab_count = lax.axis_size("slab")
    sizes = axes_of(group_count, slab_count)
    masked = per_device * slab_count * group_count
    frame_count = frames_here * group_count
    order_rows = K + frame_count
    rows_here = order_rows // group_count
    share = -(-rows_here // (16 * slab_count)) * 16

    rows_a, rows_b, data, scales, new_subspace = run_group(
        raw_frames.transpose(1, 0, 2), mask_index.reshape(-1, RUN), subspace, rotation.T,
        jnp.asarray(plane_weights()), sizes, masked, rows_here, share,
    )
    return close_up(
        rows_a.reshape(share * slab_count, -1), rows_b.reshape(share * slab_count, -1),
        data.reshape(frame_count, order_rows), scales, new_subspace, rows_here, masked,
    )


def solution(mesh):
    placed = (P("grp", "slab", None), P(("slab", "grp")), P(None, ("slab", "grp")), P())
    return jax.shard_map(
        body,
        mesh=mesh,
        in_specs=placed,
        out_specs=(P("grp", None), P(None, ("slab", "grp"))),
        check_vma=False,
    )
```

```python
import functools
import math

import jax
import jax.numpy as jnp
import numpy as np
from jax import lax
from jax.experimental import pallas as pl
from jax.experimental.pallas import tpu as pltpu
from jax.sharding import PartitionSpec as P

NX = 96
RUN = 128
RAD = 3
K = 1200
MESH = pl.DeviceIdType.MESH

smooth_sigma = 1.0617
epsilon = 1e-06

WIDE = 2 * RUN
LEFT = 3 * RUN
SPAN = 8 * RUN


def tap_weights():
    unscaled = [
        math.exp(-offset * offset / (2.0 * smooth_sigma * smooth_sigma))
        for offset in range(-RAD, RAD + 1)
    ]
    summed = sum(unscaled)
    return [weight / summed for weight in unscaled]


def plane_weights():
    taps = np.array(tap_weights())
    kinds = NX // math.gcd(WIDE, NX)
    out = np.zeros((kinds, SPAN, WIDE))
    for kind in range(kinds):
        target = np.arange(WIDE)
        column = (kind * WIDE + target) % NX
        for dy in range(-RAD, RAD + 1):
            for dx in range(-RAD, RAD + 1):
                inside = (column + dx >= 0) & (column + dx < NX)
                source = target + LEFT + dy * NX + dx
                out[kind, source[inside], target[inside]] = taps[dy + RAD] * taps[dx + RAD]
    return out.astype(jnp.bfloat16)


def axes_of(groups, slabs):
    outer = 4 if groups % 4 == 0 else 1
    cores = 2 if slabs % 2 == 0 else 1
    return outer, groups // outer, slabs // cores, cores


class Grid:
    def __init__(self, sizes, planes):
        self.full, self.planes = sizes, planes
        z, y, x, cores = sizes
        self.sizes = (z, y * x, cores) if planes else tuple(sizes)

    def here(self):
        _, ys, xs, cores = self.full
        slab, grp = lax.axis_index("slab"), lax.axis_index("grp")
        z, y, x, core = grp // ys, lax.rem(grp, ys), slab // cores, lax.rem(slab, cores)
        return [z, y * xs + x, core] if self.planes else [z, y, x, core]

    def device(self, at):
        _, ys, xs, cores = self.full
        if self.planes:
            at = [at[0], at[1] // xs, lax.rem(at[1], xs), at[2]]
        return (at[2] * cores + at[3], at[0] * ys + at[1])

    def moved(self, at, axis, step):
        other = lax.rem(at[axis] + step, self.sizes[axis])
        return at[:axis] + [other] + at[axis + 1 :], other


class Scatter:
    def __init__(self, grid, axis, left, src, landed, out, sems):
        self.grid, self.axis, self.src, self.landed, self.out = grid, axis, src, landed, out
        self.sizes = grid.sizes
        self.dim = left.index(axis)
        self.left = [other for other in left if other != axis]
        self.send_sem, self.recv_sem = sems
        self.at = grid.here()

    def part(self, where):
        return self.src.at[(slice(None),) * self.dim + (where,)]

    def copy(self, step):
        there, other = self.grid.moved(self.at, self.axis, step)
        return pltpu.make_async_remote_copy(
            src_ref=self.part(other),
            dst_ref=self.landed.at[step - 1],
            send_sem=self.send_sem.at[self.axis, step],
            recv_sem=self.recv_sem.at[self.axis, step],
            device_id=self.grid.device(there),
            device_id_type=MESH,
        )

    def start(self):
        for step in range(1, self.sizes[self.axis]):
            self.copy(step).start()

    def finish(self):
        for step in range(1, self.sizes[self.axis]):
            self.copy(step).wait()
        mine = self.part(self.at[self.axis])
        lead = [self.sizes[axis] for axis in self.left]
        total = math.prod(lead)

        def add(index, _):
            where = []
            for size in reversed(lead):
                where.insert(0, lax.rem(index, size))
                index = index // size
            where = tuple(where)
            value = mine[where].astype(jnp.float32)
            for step in range(self.sizes[self.axis] - 1):
                value = value + self.landed[(step,) + where].astype(jnp.float32)
            self.out[where] = value.astype(self.out.dtype)
            return 0

        lax.fori_loop(0, total, add, 0)


class Gather:
    def __init__(self, grid, axis, done, full, first, sems):
        self.grid, self.sizes, self.axis, self.full = grid, grid.sizes, axis, full
        self.send_sem, self.recv_sem = sems
        self.at = grid.here()
        self.where = tuple(
            slice(None) if other in done else self.at[other] for other in range(first, len(self.sizes))
        )

    def copy(self, step):
        there, _ = self.grid.moved(self.at, self.axis, step)
        return pltpu.make_async_remote_copy(
            src_ref=self.full.at[self.where],
            dst_ref=self.full.at[self.where],
            send_sem=self.send_sem.at[self.axis, step],
            recv_sem=self.recv_sem.at[self.axis, step],
            device_id=self.grid.device(there),
            device_id_type=MESH,
        )

    def start(self):
        for step in range(1, self.sizes[self.axis]):
            self.copy(step).start()

    def finish(self):
        for step in range(1, self.sizes[self.axis]):
            self.copy(step).wait()


def gather_stages(grid, order, full, first, sems):
    stages, done = [], []
    for axis in order:
        if grid.sizes[axis] > 1:
            stages.append(Gather(grid, axis, list(done), full, first, sems))
        done.append(axis)
    return stages


def stage_scratch(sizes, order, piece):
    out = []
    left = [axis for axis in range(len(sizes)) if sizes[axis] > 1]
    for axis in order:
        if sizes[axis] == 1:
            continue
        left.remove(axis)
        shape = tuple(sizes[other] for other in left) + piece
        out.append(pltpu.VMEM((sizes[axis] - 1,) + shape, jnp.bfloat16))
        if left:
            out.append(pltpu.VMEM(shape, jnp.bfloat16))
    return out


def stage_sems(sizes):
    most = max(sizes)
    return [pltpu.SemaphoreType.DMA((4, most)) for _ in range(4)]


def scatter_stages(grid, order, src, bufs, result, sems):
    stages, sizes = [], grid.sizes
    left = list(range(len(sizes)))
    for axis in order:
        if sizes[axis] == 1:
            src = src.at[(slice(None),) * left.index(axis) + (0,)]
            left = [other for other in left if other != axis]
    order = [axis for axis in order if sizes[axis] > 1]
    for number, axis in enumerate(order):
        last = number == len(order) - 1
        out = result if last else bufs[2 * number + 1]
        stages.append(Scatter(grid, axis, left, src, bufs[2 * number], out, sems))
        left = stages[-1].left
        src = out
    return stages


def place(peer, groups):
    return (peer // groups, lax.rem(peer, groups))


def group_kernel(dims, x_hbm, mask_ref, s_hbm, r_hbm, w_hbm,
                 rows_a, rows_b, data_ref, scale_ref, new_hbm,
                 stacked, gram_a, gram_b, dpart, up_ref, down_ref, below, above, picked_ref,
                 regrouped, starts, starts_at, power_at, power_sum, w_ref,
                 load_sem, mask_send, mask_recv, rim_send, rim_recv, halo_send, halo_recv,
                 all_send, all_recv, p_send, p_recv, *bufs):
    sizes, cut, depth, frames, extent, runs, share, masked, rows_here = dims
    groups, slabs = sizes[0] * sizes[1], sizes[2] * sizes[3]
    total = groups * slabs
    slab, grp = lax.axis_index("slab"), lax.axis_index("grp")
    me = slab * groups + grp
    grid, planes = Grid(sizes, False), Grid(sizes, True)
    at, plane_at = grid.here(), planes.here()
    bufs = list(bufs)
    upper = lax.rem(slab + 1, slabs)
    lower = lax.rem(slab + slabs - 1, slabs)
    own = runs * groups
    rim_groups = groups * RAD // depth
    rim = rim_groups * runs
    places = extent // RUN
    padded = depth + RAD
    taps = tap_weights()
    data_rows = frames * groups
    order_rows = K + data_rows
    half_rows = data_rows // 2
    some = frames // HALVES
    across = (((1,), (1,)), ((), ()))

    load_s = pltpu.make_async_copy(s_hbm, stacked.at[pl.ds(0, K)], load_sem.at[1])
    load_w = pltpu.make_async_copy(w_hbm, w_ref, load_sem.at[2])

    barrier = pltpu.get_barrier_semaphore()

    def greet(step, _):
        pl.semaphore_signal(
            barrier, inc=1, device_id=place(lax.rem(me + step, total), groups),
            device_id_type=MESH,
        )
        return 0

    def trade_starts(step):
        return pltpu.make_async_remote_copy(
            src_ref=starts.at[grp], dst_ref=starts.at[grp],
            send_sem=mask_send.at[step], recv_sem=mask_recv.at[step],
            device_id=(slab, lax.rem(grp + step, groups)), device_id_type=MESH,
        )

    def rim_starts(side, there, number, to):
        slot = groups + side * rim_groups + number
        return pltpu.make_async_remote_copy(
            src_ref=starts.at[grp], dst_ref=starts.at[slot],
            send_sem=rim_send.at[to], recv_sem=rim_recv.at[side * rim_groups + number],
            device_id=(there, to), device_id_type=MESH,
        )

    def for_peers(action):
        def one(step, _):
            action(step)
            return 0

        lax.fori_loop(1, groups, one, 0)

    def for_rim(action):
        def one(to, _):
            @pl.when(grp < rim_groups)
            def _():
                action(rim_starts(0, lower, grp, to))

            @pl.when(grp >= groups - rim_groups)
            def _():
                action(rim_starts(1, upper, grp - (groups - rim_groups), to))

            return 0

        lax.fori_loop(0, groups, one, 0)

    def send_starts():
        lane = lax.broadcasted_iota(jnp.int32, (1, RUN), 1)
        first = jnp.zeros((1, RUN), jnp.int32)
        for run in range(runs):
            first = jnp.where(lane == run, mask_ref[run : run + 1, :] - run, first)
        cell = lax.shift_right_arithmetic(first, 7) - slab * (depth * places)
        plane = jnp.zeros((1, RUN), jnp.int32)
        for number in range(1, depth):
            plane = plane + jnp.where(cell >= number * places, 1, 0)
        row = (cell - plane * places) * padded + plane
        row = jnp.minimum(jnp.maximum(row, 0), (places - 1) * padded + depth - 1)
        starts[grp] = jnp.where(lane < runs, row, 0)
        for_peers(lambda step: trade_starts(step).start())
        for_rim(lambda copy: copy.start())

    def await_starts():
        for_peers(lambda step: trade_starts(step).wait())
        for_rim(lambda copy: copy.wait_send())
        for number in range(rim_groups):
            rim_starts(0, lower, number, grp).wait_recv()
            rim_starts(1, upper, number, grp).wait_recv()
        copy = pltpu.make_async_copy(starts, starts_at, load_sem.at[0])
        copy.start()
        copy.wait()

    def halo(src, dst, number, other):
        return pltpu.make_async_remote_copy(
            src_ref=src, dst_ref=dst, send_sem=halo_send.at[number], recv_sem=halo_recv.at[number],
            device_id=(other, grp), device_id_type=MESH,
        )

    halos_up = [halo(up_ref.at[h], below.at[h], h, upper) for h in range(HALVES)]
    halos_down = [halo(down_ref.at[h], above.at[h], HALVES + h, lower) for h in range(HALVES)]

    def trade(h, step):
        other = lax.rem(grp + step, groups)
        return pltpu.make_async_remote_copy(
            src_ref=picked_ref.at[h, pl.ds(other * runs, runs)], dst_ref=regrouped.at[grp, h],
            send_sem=all_send.at[h, step], recv_sem=all_recv.at[h, step],
            device_id=(slab, other), device_id_type=MESH,
        )

    def start_trades(h, at_rim):
        for step in range(1, groups):
            other = lax.rem(grp + step, groups)
            inside = (other >= rim_groups) & (other < groups - rim_groups)
            pl.when(jnp.logical_not(inside) if at_rim else inside)(trade(h, step).start)

    def take(count):
        taken = bufs[:count]
        del bufs[:count]
        return taken

    def chain(grid, order, back, src, full, first, piece):
        sems = take(4)
        scratch = take(len(stage_scratch(grid.sizes, order, piece)))
        where = tuple((plane_at if grid.planes else at)[first:])
        return scatter_stages(grid, order, src, scratch, full.at[where], sems[:2]) + gather_stages(
            grid, back, full, first, sems[2:]
        )

    a_steps = chain(grid, ORDER_A, (2, 3), gram_a, rows_a, 2, (share, cut))
    b_steps = chain(grid, ORDER_B, (2, 3), gram_b, rows_b, 2, (share, K - cut))
    d_steps = chain(planes, ORDER_D, (0, 1, 2), dpart, data_ref, 0, dpart.shape[3:])

    def advance(steps):
        if steps:
            steps.pop(0).finish()
        if steps:
            steps[0].start()

    def basis_gram(gram, low_column, high_column):
        width = high_column - low_column
        for group in range(groups):
            first = group * rows_here
            where = (group // sizes[1], group % sizes[1])
            low = first // 16 * 16
            if first < K:
                found = lax.dot_general(
                    stacked[low : low + slabs * share + 16], stacked[low_column:high_column],
                    across, preferred_element_type=jnp.float32,
                )
            for number in range(slabs):
                begin = first - low + number * share
                gram[where + (number // sizes[3], number % sizes[3])] = (
                    found[begin : begin + share]
                    if first < K
                    else jnp.zeros((share, width), jnp.float32)
                ).astype(gram.dtype)

    def smooth(x_ref, y_ref):
        load_x = pltpu.make_async_copy(
            x_hbm, x_ref.at[:, :, pl.ds(LEFT, extent)], load_sem.at[3]
        )
        load_s.start()
        load_x.start()
        load_w.start()
        lax.fori_loop(1, total, greet, 0)
        right = x_ref.shape[2] - LEFT - extent
        x_ref[:, :, :LEFT] = jnp.zeros((depth, frames, LEFT), x_ref.dtype)
        x_ref[:, :, LEFT + extent :] = jnp.zeros((depth, frames, right), x_ref.dtype)
        rest = stacked.shape[0] - K
        stacked[K:] = jnp.zeros((rest, stacked.shape[1]), stacked.dtype)

        def blank(number, _):
            for h in range(HALVES):
                y_ref[h, pl.ds(number * padded, RAD)] = jnp.zeros((RAD, some, RUN), jnp.float32)
            return 0

        lax.fori_loop(0, places + 1, blank, 0)
        load_s.wait()
        basis_gram(gram_a, 0, cut)
        pl.semaphore_wait(barrier, total - 1)
        a_steps[0].start()
        send_starts()
        load_w.wait()
        load_x.wait()
        kinds = w_ref.shape[0]

        def planar(h, begin_step, end_step):
            def one(step, _):
                for kind in range(kinds):
                    number = step * kinds + kind
                    begin = pl.multiple_of(number * WIDE, WIDE)
                    cells = x_ref[:, h * some : (h + 1) * some, pl.ds(begin, SPAN)]
                    found = jnp.dot(
                        cells.reshape(depth * some, SPAN), w_ref[kind],
                        preferred_element_type=jnp.float32,
                    )
                    for side in range(2):
                        y_ref[h, pl.ds((2 * number + side) * padded + RAD, depth)] = found[
                            :, side * RUN : (side + 1) * RUN
                        ].reshape(depth, some, RUN)
                return 0

            lax.fori_loop(begin_step, end_step, one, 0)

        def pick(h, slot, run, shift, used):
            row = starts_at[slot, 0, run]
            if shift > 0:
                row = jnp.minimum(row + shift, places * padded)
            if shift < 0:
                row = jnp.maximum(row + shift, -(RAD + 1))
            found = None
            for tap in used:
                term = taps[tap] * y_ref[h, row + tap]
                found = term if found is None else found + term
            return found

        def over(count, action):
            def one(number, _):
                for run in range(runs):
                    action(number, run)
                return 0

            lax.fori_loop(0, count, one, 0)

        every = range(2 * RAD + 1)
        low_part = jnp.where(slab > 0, 1.0, 0.0)
        high_part = jnp.where(slab < slabs - 1, 1.0, 0.0)

        def pick_halos(h):
            def one_up(number, run):
                up_ref[h, number * runs + run] = pick(
                    h, groups + number, run, depth, range(RAD)
                ).astype(up_ref.dtype)

            def one_down(number, run):
                down_ref[h, number * runs + run] = pick(
                    h, groups + rim_groups + number, run, -depth, range(RAD + 1, 2 * RAD + 1)
                ).astype(down_ref.dtype)

            over(rim_groups, one_up)
            halos_up[h].start()
            over(rim_groups, one_down)
            halos_down[h].start()

        def pick_inner(h):
            def one(number, run):
                slot = number + rim_groups
                picked_ref[h, slot * runs + run] = pick(h, slot, run, 0, every).astype(
                    picked_ref.dtype
                )

            over(groups - 2 * rim_groups, one)
            start_trades(h, False)

        def pick_edges(h):
            halos_up[h].wait()
            halos_down[h].wait()

            def one(number, run):
                where = number * runs + run
                picked_ref[h, where] = (
                    pick(h, number, run, 0, every)
                    + low_part * below[h, where].astype(jnp.float32)
                ).astype(picked_ref.dtype)
                slot = number + groups - rim_groups
                picked_ref[h, slot * runs + run] = (
                    pick(h, slot, run, 0, every)
                    + high_part * above[h, where].astype(jnp.float32)
                ).astype(picked_ref.dtype)

            over(rim_groups, one)
            start_trades(h, True)

        steps = extent // (WIDE * kinds)
        part = -(-steps // 3)
        planar(0, 0, part)
        advance(a_steps)
        planar(0, part, steps)
        await_starts()
        pick_halos(0)
        pick_inner(0)
        planar(1, 0, part)
        pick_edges(0)
        planar(1, part, steps)
        pick_halos(1)
        pick_inner(1)
        pick_edges(1)

    pl.run_scoped(
        smooth,
        pltpu.VMEM((depth, frames, extent + SPAN - WIDE), jnp.bfloat16),
        pltpu.VMEM((HALVES, places * padded + RAD, some, RUN), jnp.float32),
    )

    def finish(regrouped_rows):
        r_ref, out_ref = regrouped_rows
        load_r = pltpu.make_async_copy(r_hbm, r_ref, load_sem.at[4])
        load_r.start()
        for h in range(HALVES):
            regrouped[grp, h] = picked_ref[h, pl.ds(grp * runs, runs)]
        advance(a_steps)
        basis_gram(gram_b, cut, K)
        b_steps[0].start()
        advance(a_steps)
        advance(b_steps)
        for h in range(HALVES):
            for_peers(lambda step, h=h: trade(h, step).wait())

        half = groups // 2
        squares = [jnp.zeros((1, RUN), jnp.float32) for _ in range(2)]
        for run in range(runs):
            lanes = slice(run * RUN, (run + 1) * RUN)
            for subject in range(2):
                block = regrouped[subject * half : (subject + 1) * half, :, run]
                block = block.astype(jnp.float32)
                block = block.reshape(half * frames, RUN)
                mean = jnp.sum(block, axis=0, keepdims=True) * (1.0 / (half * frames))
                rounded = (block - mean).astype(stacked.dtype)
                begin = K + subject * half_rows
                stacked[begin : begin + half_rows, lanes] = rounded
                wide = rounded.astype(jnp.float32)
                squares[subject] = squares[subject] + jnp.sum(wide * wide, axis=0, keepdims=True)
        power_sum[0:1, :] = squares[0]
        power_sum[1:2, :] = squares[1]

        def share_power(axis, count, other):
            first = 0 if axis == 0 else groups

            def copy(step):
                return pltpu.make_async_remote_copy(
                    src_ref=power_sum, dst_ref=power_at.at[first + step],
                    send_sem=p_send.at[first + step], recv_sem=p_recv.at[first + step],
                    device_id=other(step), device_id_type=MESH,
                )

            def start():
                for step in range(1, count):
                    copy(step).start()

            def wait():
                found = power_sum[...]
                for step in range(1, count):
                    copy(step).wait()
                for step in range(1, count):
                    found = found + power_at[first + step]
                power_sum[...] = found

            return start, wait

        start_p, wait_p = share_power(0, groups, lambda step: (slab, lax.rem(grp + step, groups)))
        start_q, wait_q = share_power(1, slabs, lambda step: (lax.rem(slab + step, slabs), grp))
        start_p()

        found = lax.dot_general(
            stacked[K:order_rows], stacked[:order_rows], across,
            preferred_element_type=jnp.float32,
        )
        piece = data_rows // total
        for number in range(total):
            line, core = number // sizes[3], number % sizes[3]
            dpart[line // planes.sizes[1], line % planes.sizes[1], core] = found[
                number * piece : (number + 1) * piece
            ].astype(dpart.dtype)
        d_steps[0].start()
        wait_p()
        start_q()
        advance(d_steps)
        advance(a_steps)
        wait_q()
        power = jnp.sum(power_sum[...], axis=1, keepdims=True)
        scales = lax.rsqrt(power * (1.0 / (masked * half_rows)) + epsilon)
        scale_ref[...] = jnp.broadcast_to(scales, scale_ref.shape)

        load_r.wait()
        edge = K // RUN * RUN
        lane = lax.broadcasted_iota(jnp.int32, (1, order_rows - edge), 1) + edge
        factor = jnp.where(
            lane < K, 1.0, jnp.where(lane < K + half_rows, scales[0:1], scales[1:2])
        )
        r_ref[:, edge:] = (r_ref[:, edge:].astype(jnp.float32) * factor).astype(r_ref.dtype)

        chunk = out_ref.shape[1]
        copies = []

        def rotate(number):
            slot = number % 2
            if number >= 2:
                copies[number - 2].wait()
            rows = slice(number * chunk, (number + 1) * chunk)
            out_ref[slot] = jnp.dot(
                r_ref[rows], stacked[:order_rows], preferred_element_type=jnp.float32
            ).astype(out_ref.dtype)
            copy = pltpu.make_async_copy(
                out_ref.at[slot], new_hbm.at[pl.ds(number * chunk, chunk)], load_sem.at[5 + slot]
            )
            copy.start()
            copies.append(copy)

        count = K // chunk
        rotate(0)
        todo = list(range(1, count))
        turn = 0
        while d_steps or a_steps or b_steps:
            for steps in (d_steps, a_steps) if turn == 1 else (d_steps, a_steps, b_steps):
                advance(steps)
            if todo:
                rotate(todo.pop(0))
            turn += 1
        while todo:
            rotate(todo.pop(0))
        for copy in copies[-2:]:
            copy.wait()

    pl.run_scoped(
        lambda r_ref, out_ref: finish((r_ref, out_ref)),
        pltpu.VMEM((K, order_rows), jnp.bfloat16),
        pltpu.VMEM((2, K // 5, runs * RUN), jnp.bfloat16),
    )


HALVES = 2
ORDER_A, ORDER_B, ORDER_D = (3, 1, 2, 0), (3, 2, 1, 0), (2, 1, 0)


def run_group(cells, mask, subspace, turned, weights, sizes, masked, rows_here, share):
    depth, frames, extent = cells.shape
    vmem = pl.BlockSpec(memory_space=pltpu.VMEM)
    hbm = pl.BlockSpec(memory_space=pl.ANY)
    groups, slabs = sizes[0] * sizes[1], sizes[2] * sizes[3]
    total = groups * slabs
    runs = mask.shape[0]
    own = groups * runs
    rim_groups = groups * RAD // depth
    rim = rim_groups * runs
    data_rows = frames * groups
    order_rows = K + data_rows
    cut = -(-K // (2 * RUN)) * RUN
    planes = Grid(sizes, True)
    flat = planes.sizes
    d_piece = (data_rows // total, order_rows)
    last = (groups - 1) * rows_here // 16 * 16 + slabs * share + 16
    stacked_rows = max(order_rows, last)
    some = frames // HALVES
    rim_shape = pltpu.VMEM((HALVES, rim, some, RUN), jnp.bfloat16)
    dma = pltpu.SemaphoreType.DMA
    dims = (sizes, cut, depth, frames, extent, runs, share, masked, rows_here)
    slots = groups + 2 * rim_groups
    return pl.pallas_call(
        functools.partial(group_kernel, dims),
        out_shape=(
            jax.ShapeDtypeStruct(tuple(sizes[2:]) + (share, cut), jnp.bfloat16),
            jax.ShapeDtypeStruct(tuple(sizes[2:]) + (share, K - cut), jnp.bfloat16),
            jax.ShapeDtypeStruct(tuple(flat) + d_piece, jnp.bfloat16),
            jax.ShapeDtypeStruct((2, RUN), jnp.float32),
            jax.ShapeDtypeStruct(subspace.shape, jnp.bfloat16),
        ),
        in_specs=[hbm, vmem, hbm, hbm, hbm],
        out_specs=(vmem, vmem, vmem, vmem, hbm),
        scratch_shapes=[
            pltpu.VMEM((stacked_rows, runs * RUN), jnp.bfloat16),
            pltpu.VMEM(tuple(sizes) + (share, cut), jnp.bfloat16),
            pltpu.VMEM(tuple(sizes) + (share, K - cut), jnp.bfloat16),
            pltpu.VMEM(tuple(flat) + d_piece, jnp.bfloat16),
            rim_shape, rim_shape, rim_shape, rim_shape,
            pltpu.VMEM((HALVES, own, some, RUN), jnp.bfloat16),
            pltpu.VMEM((groups, HALVES, runs, some, RUN), jnp.bfloat16),
            pltpu.VMEM((slots, 1, RUN), jnp.int32),
            pltpu.SMEM((slots, 1, RUN), jnp.int32),
            pltpu.VMEM((groups + slabs, 2, RUN), jnp.float32),
            pltpu.VMEM((2, RUN), jnp.float32),
            pltpu.VMEM(weights.shape, jnp.bfloat16),
            dma((7,)),
            dma((groups,)), dma((groups,)),
            dma((groups,)), dma((2 * rim_groups,)),
            dma((2 * HALVES,)), dma((2 * HALVES,)),
            dma((HALVES, groups)), dma((HALVES, groups)),
            dma((groups + slabs,)), dma((groups + slabs,)),
        ]
        + stage_sems(sizes)
        + stage_scratch(sizes, ORDER_A, (share, cut))
        + stage_sems(sizes)
        + stage_scratch(sizes, ORDER_B, (share, K - cut))
        + stage_sems(flat)
        + stage_scratch(flat, ORDER_D, d_piece),
        compiler_params=pltpu.CompilerParams(
            collective_id=1, has_side_effects=True, vmem_limit_bytes=62 * 1024 * 1024
        ),
    )(cells, mask, subspace, turned, weights)


def close_kernel(rows_here, masked, a_hbm, b_hbm, data_hbm, scale_hbm, new_hbm, gram_ref,
                 out_hbm, held, a_ref, b_ref, data_ref, scale_ref, wide, turned, low, sem):
    first = lax.axis_index("grp") * rows_here
    data_rows, order_rows = data_ref.shape
    parts = 5
    chunk = K // parts
    fetches = [
        pltpu.make_async_copy(
            new_hbm.at[pl.ds(part * chunk, chunk)], held.at[part], sem.at[part]
        )
        for part in range(parts)
    ]
    copies = [
        pltpu.make_async_copy(
            held.at[part], out_hbm.at[pl.ds(part * chunk, chunk)], sem.at[parts + part]
        )
        for part in range(parts)
    ]
    loads = [
        pltpu.make_async_copy(source, target, sem.at[2 * parts + number])
        for number, (source, target) in enumerate(
            ((data_hbm, data_ref), (scale_hbm, scale_ref), (a_hbm, a_ref), (b_hbm, b_ref))
        )
    ]
    for copy in loads + fetches:
        copy.start()
    for fetch, copy in zip(fetches, copies):
        fetch.wait()
        copy.start()
    for copy in loads:
        copy.wait()

    def rows_from(ref, start):
        size = -(-rows_here // 8) * 8 + 8
        held = ref[pl.ds(pl.multiple_of(start // 8 * 8, 8), size)]
        return pltpu.roll(held, lax.rem(size - lax.rem(start, 8), size), 0)[:rows_here]

    window = turned.shape[0]
    data = data_ref[...].astype(jnp.float32)
    wide[:, :order_rows] = data
    begin = pl.multiple_of(first // RUN * RUN, RUN)
    turned[...] = wide[:, pl.ds(begin, window)].T
    right = rows_from(turned, first - begin)
    low[:rows_here] = jnp.zeros((rows_here, K), jnp.float32)
    rest = low.shape[0] - rows_here - data_rows
    low[rows_here + data_rows :] = jnp.zeros((rest, K), jnp.float32)
    low[rows_here : rows_here + data_rows] = data[:, :K]
    below = rows_from(low, jnp.maximum(first - K + rows_here, 0))

    half = data_rows // 2
    scales = scale_ref[:, :1]

    def scale_of(index):
        return jnp.where(
            index < K, 1.0, jnp.where(index < K + half, scales[0:1], scales[1:2])
        )

    row = scale_of(lax.broadcasted_iota(jnp.int32, (rows_here, 1), 0) + first)
    row = row * (1.0 / masked)
    column = scale_of(lax.broadcasted_iota(jnp.int32, (1, data_rows), 1) + K)
    cut = a_ref.shape[1]
    gram_ref[:, :cut] = (a_ref[...].astype(jnp.float32)[:rows_here] + below[:, :cut]) * row
    gram_ref[:, cut:K] = (b_ref[...].astype(jnp.float32)[:rows_here] + below[:, cut:]) * row
    gram_ref[:, K:] = right * (row * column)
    for copy in copies:
        copy.wait()


def close_up(rows_a, rows_b, data, scales, new_subspace, rows_here, masked):
    vmem = pl.BlockSpec(memory_space=pltpu.VMEM)
    hbm = pl.BlockSpec(memory_space=pl.ANY)
    data_rows, order_rows = data.shape
    window = -(-(rows_here + RUN) // RUN) * RUN
    wide = (order_rows // RUN) * RUN + window
    return pl.pallas_call(
        functools.partial(close_kernel, rows_here, masked),
        out_shape=(
            jax.ShapeDtypeStruct((rows_here, order_rows), jnp.float32),
            jax.ShapeDtypeStruct(new_subspace.shape, new_subspace.dtype),
        ),
        in_specs=[hbm] * 5,
        out_specs=(vmem, hbm),
        scratch_shapes=[
            pltpu.VMEM((5, K // 5, new_subspace.shape[1]), new_subspace.dtype),
            pltpu.VMEM(rows_a.shape, rows_a.dtype),
            pltpu.VMEM(rows_b.shape, rows_b.dtype),
            pltpu.VMEM(data.shape, data.dtype),
            pltpu.VMEM(scales.shape, scales.dtype),
            pltpu.VMEM((data_rows, wide), jnp.float32),
            pltpu.VMEM((window, data_rows), jnp.float32),
            pltpu.VMEM((2 * rows_here + data_rows + 16, K), jnp.float32),
            pltpu.SemaphoreType.DMA((14,)),
        ],
        compiler_params=pltpu.CompilerParams(vmem_limit_bytes=62 * 1024 * 1024),
    )(rows_a, rows_b, data, scales, new_subspace)


def body(raw_frames, mask_index, subspace, rotation):
    frames_here, slab_depth, extent = raw_frames.shape
    per_device = subspace.shape[1]
    group_count = lax.axis_size("grp")
    slab_count = lax.axis_size("slab")
    sizes = axes_of(group_count, slab_count)
    masked = per_device * slab_count * group_count
    frame_count = frames_here * group_count
    order_rows = K + frame_count
    rows_here = order_rows // group_count
    share = -(-rows_here // (16 * slab_count)) * 16

    rows_a, rows_b, data, scales, new_subspace = run_group(
        raw_frames.transpose(1, 0, 2), mask_index.reshape(-1, RUN), subspace, rotation.T,
        jnp.asarray(plane_weights()), sizes, masked, rows_here, share,
    )
    return close_up(
        rows_a.reshape(share * slab_count, -1), rows_b.reshape(share * slab_count, -1),
        data.reshape(frame_count, order_rows), scales, new_subspace, rows_here, masked,
    )


def solution(mesh):
    placed = (P("grp", "slab", None), P(("slab", "grp")), P(None, ("slab", "grp")), P())
    return jax.shard_map(
        body,
        mesh=mesh,
        in_specs=placed,
        out_specs=(P("grp", None), P(None, ("slab", "grp"))),
        check_vma=False,
    )
```

```python
import functools
import math

import jax
import jax.numpy as jnp
import numpy as np
from jax import lax
from jax.experimental import pallas as pl
from jax.experimental.pallas import tpu as pltpu
from jax.sharding import PartitionSpec as P

NX = 96
RUN = 128
RAD = 3
K = 1200
MESH = pl.DeviceIdType.MESH

smooth_sigma = 1.0617
epsilon = 1e-06

WIDE = 2 * RUN
LEFT = 3 * RUN
SPAN = 8 * RUN


def tap_weights():
    unscaled = [
        math.exp(-offset * offset / (2.0 * smooth_sigma * smooth_sigma))
        for offset in range(-RAD, RAD + 1)
    ]
    summed = sum(unscaled)
    return [weight / summed for weight in unscaled]


def plane_weights():
    taps = np.array(tap_weights())
    kinds = NX // math.gcd(WIDE, NX)
    out = np.zeros((kinds, SPAN, WIDE))
    for kind in range(kinds):
        target = np.arange(WIDE)
        column = (kind * WIDE + target) % NX
        for dy in range(-RAD, RAD + 1):
            for dx in range(-RAD, RAD + 1):
                inside = (column + dx >= 0) & (column + dx < NX)
                source = target + LEFT + dy * NX + dx
                out[kind, source[inside], target[inside]] = taps[dy + RAD] * taps[dx + RAD]
    return out.astype(jnp.bfloat16)


def axes_of(groups, slabs):
    outer = 4 if groups % 4 == 0 else 1
    cores = 2 if slabs % 2 == 0 else 1
    return outer, groups // outer, slabs // cores, cores


class Grid:
    def __init__(self, sizes, planes):
        self.full, self.planes = sizes, planes
        z, y, x, cores = sizes
        self.sizes = (z, y * x, cores) if planes else tuple(sizes)

    def here(self):
        _, ys, xs, cores = self.full
        slab, grp = lax.axis_index("slab"), lax.axis_index("grp")
        z, y, x, core = grp // ys, lax.rem(grp, ys), slab // cores, lax.rem(slab, cores)
        return [z, y * xs + x, core] if self.planes else [z, y, x, core]

    def device(self, at):
        _, ys, xs, cores = self.full
        if self.planes:
            at = [at[0], at[1] // xs, lax.rem(at[1], xs), at[2]]
        return (at[2] * cores + at[3], at[0] * ys + at[1])

    def moved(self, at, axis, step):
        other = lax.rem(at[axis] + step, self.sizes[axis])
        return at[:axis] + [other] + at[axis + 1 :], other


class Scatter:
    def __init__(self, grid, axis, left, src, landed, out, sems):
        self.grid, self.axis, self.src, self.landed, self.out = grid, axis, src, landed, out
        self.sizes = grid.sizes
        self.dim = left.index(axis)
        self.left = [other for other in left if other != axis]
        self.send_sem, self.recv_sem = sems
        self.at = grid.here()

    def part(self, where):
        return self.src.at[(slice(None),) * self.dim + (where,)]

    def copy(self, step):
        there, other = self.grid.moved(self.at, self.axis, step)
        return pltpu.make_async_remote_copy(
            src_ref=self.part(other),
            dst_ref=self.landed.at[step - 1],
            send_sem=self.send_sem.at[self.axis, step],
            recv_sem=self.recv_sem.at[self.axis, step],
            device_id=self.grid.device(there),
            device_id_type=MESH,
        )

    def start(self):
        for step in range(1, self.sizes[self.axis]):
            self.copy(step).start()

    def finish(self):
        for step in range(1, self.sizes[self.axis]):
            self.copy(step).wait()
        mine = self.part(self.at[self.axis])
        lead = [self.sizes[axis] for axis in self.left]
        total = math.prod(lead)

        def add(index, _):
            where = []
            for size in reversed(lead):
                where.insert(0, lax.rem(index, size))
                index = index // size
            where = tuple(where)
            value = mine[where].astype(jnp.float32)
            for step in range(self.sizes[self.axis] - 1):
                value = value + self.landed[(step,) + where].astype(jnp.float32)
            self.out[where] = value.astype(self.out.dtype)
            return 0

        lax.fori_loop(0, total, add, 0)


class Gather:
    def __init__(self, grid, axis, done, full, first, sems):
        self.grid, self.sizes, self.axis, self.full = grid, grid.sizes, axis, full
        self.send_sem, self.recv_sem = sems
        self.at = grid.here()
        self.where = tuple(
            slice(None) if other in done else self.at[other] for other in range(first, len(self.sizes))
        )

    def copy(self, step):
        there, _ = self.grid.moved(self.at, self.axis, step)
        return pltpu.make_async_remote_copy(
            src_ref=self.full.at[self.where],
            dst_ref=self.full.at[self.where],
            send_sem=self.send_sem.at[self.axis, step],
            recv_sem=self.recv_sem.at[self.axis, step],
            device_id=self.grid.device(there),
            device_id_type=MESH,
        )

    def start(self):
        for step in range(1, self.sizes[self.axis]):
            self.copy(step).start()

    def finish(self):
        for step in range(1, self.sizes[self.axis]):
            self.copy(step).wait()


def gather_stages(grid, order, full, first, sems):
    stages, done = [], []
    for axis in order:
        if grid.sizes[axis] > 1:
            stages.append(Gather(grid, axis, list(done), full, first, sems))
        done.append(axis)
    return stages


def stage_scratch(sizes, order, piece):
    out = []
    left = [axis for axis in range(len(sizes)) if sizes[axis] > 1]
    for axis in order:
        if sizes[axis] == 1:
            continue
        left.remove(axis)
        shape = tuple(sizes[other] for other in left) + piece
        out.append(pltpu.VMEM((sizes[axis] - 1,) + shape, jnp.bfloat16))
        if left:
            out.append(pltpu.VMEM(shape, jnp.bfloat16))
    return out


def stage_sems(sizes):
    most = max(sizes)
    return [pltpu.SemaphoreType.DMA((4, most)) for _ in range(4)]


def scatter_stages(grid, order, src, bufs, result, sems):
    stages, sizes = [], grid.sizes
    left = list(range(len(sizes)))
    for axis in order:
        if sizes[axis] == 1:
            src = src.at[(slice(None),) * left.index(axis) + (0,)]
            left = [other for other in left if other != axis]
    order = [axis for axis in order if sizes[axis] > 1]
    for number, axis in enumerate(order):
        last = number == len(order) - 1
        out = result if last else bufs[2 * number + 1]
        stages.append(Scatter(grid, axis, left, src, bufs[2 * number], out, sems))
        left = stages[-1].left
        src = out
    return stages


def place(peer, groups):
    return (peer // groups, lax.rem(peer, groups))


def group_kernel(dims, x_hbm, mask_ref, s_hbm, r_hbm, w_hbm,
                 rows_a, rows_b, data_ref, scale_ref, new_hbm,
                 stacked, gram_a, gram_b, dpart, up_ref, down_ref, below, above, picked_ref,
                 regrouped, starts, starts_at, power_at, power_sum, w_ref,
                 load_sem, mask_send, mask_recv, rim_send, rim_recv, halo_send, halo_recv,
                 all_send, all_recv, p_send, p_recv, *bufs):
    sizes, cut, depth, frames, extent, runs, share, masked, rows_here = dims
    groups, slabs = sizes[0] * sizes[1], sizes[2] * sizes[3]
    total = groups * slabs
    slab, grp = lax.axis_index("slab"), lax.axis_index("grp")
    me = slab * groups + grp
    grid, planes = Grid(sizes, False), Grid(sizes, True)
    at, plane_at = grid.here(), planes.here()
    bufs = list(bufs)
    upper = lax.rem(slab + 1, slabs)
    lower = lax.rem(slab + slabs - 1, slabs)
    own = runs * groups
    rim_groups = groups * RAD // depth
    rim = rim_groups * runs
    places = extent // RUN
    padded = depth + RAD
    taps = tap_weights()
    data_rows = frames * groups
    order_rows = K + data_rows
    half_rows = data_rows // 2
    some = frames // HALVES
    across = (((1,), (1,)), ((), ()))

    load_s = pltpu.make_async_copy(s_hbm, stacked.at[pl.ds(0, K)], load_sem.at[1])
    load_w = pltpu.make_async_copy(w_hbm, w_ref, load_sem.at[2])

    barrier = pltpu.get_barrier_semaphore()

    def greet(step, _):
        pl.semaphore_signal(
            barrier, inc=1, device_id=place(lax.rem(me + step, total), groups),
            device_id_type=MESH,
        )
        return 0

    def trade_starts(step):
        return pltpu.make_async_remote_copy(
            src_ref=starts.at[grp], dst_ref=starts.at[grp],
            send_sem=mask_send.at[step], recv_sem=mask_recv.at[step],
            device_id=(slab, lax.rem(grp + step, groups)), device_id_type=MESH,
        )

    def rim_starts(side, there, number, to):
        slot = groups + side * rim_groups + number
        return pltpu.make_async_remote_copy(
            src_ref=starts.at[grp], dst_ref=starts.at[slot],
            send_sem=rim_send.at[to], recv_sem=rim_recv.at[side * rim_groups + number],
            device_id=(there, to), device_id_type=MESH,
        )

    def for_peers(action):
        def one(step, _):
            action(step)
            return 0

        lax.fori_loop(1, groups, one, 0)

    def for_rim(action):
        def one(to, _):
            @pl.when(grp < rim_groups)
            def _():
                action(rim_starts(0, lower, grp, to))

            @pl.when(grp >= groups - rim_groups)
            def _():
                action(rim_starts(1, upper, grp - (groups - rim_groups), to))

            return 0

        lax.fori_loop(0, groups, one, 0)

    def send_starts():
        lane = lax.broadcasted_iota(jnp.int32, (1, RUN), 1)
        first = jnp.zeros((1, RUN), jnp.int32)
        for run in range(runs):
            first = jnp.where(lane == run, mask_ref[run : run + 1, :] - run, first)
        cell = lax.shift_right_arithmetic(first, 7) - slab * (depth * places)
        plane = jnp.zeros((1, RUN), jnp.int32)
        for number in range(1, depth):
            plane = plane + jnp.where(cell >= number * places, 1, 0)
        row = (cell - plane * places) * padded + plane
        row = jnp.minimum(jnp.maximum(row, 0), (places - 1) * padded + depth - 1)
        starts[grp] = jnp.where(lane < runs, row, 0)
        for_peers(lambda step: trade_starts(step).start())
        for_rim(lambda copy: copy.start())

    def await_starts():
        for_peers(lambda step: trade_starts(step).wait())
        for_rim(lambda copy: copy.wait_send())
        for number in range(rim_groups):
            rim_starts(0, lower, number, grp).wait_recv()
            rim_starts(1, upper, number, grp).wait_recv()
        copy = pltpu.make_async_copy(starts, starts_at, load_sem.at[0])
        copy.start()
        copy.wait()

    def halo(src, dst, number, other):
        return pltpu.make_async_remote_copy(
            src_ref=src, dst_ref=dst, send_sem=halo_send.at[number], recv_sem=halo_recv.at[number],
            device_id=(other, grp), device_id_type=MESH,
        )

    halos_up = [halo(up_ref.at[h], below.at[h], h, upper) for h in range(HALVES)]
    halos_down = [halo(down_ref.at[h], above.at[h], HALVES + h, lower) for h in range(HALVES)]

    def trade(h, step):
        other = lax.rem(grp + step, groups)
        return pltpu.make_async_remote_copy(
            src_ref=picked_ref.at[h, pl.ds(other * runs, runs)], dst_ref=regrouped.at[grp, h],
            send_sem=all_send.at[h, step], recv_sem=all_recv.at[h, step],
            device_id=(slab, other), device_id_type=MESH,
        )

    def start_trades(h, at_rim):
        for step in range(1, groups):
            other = lax.rem(grp + step, groups)
            inside = (other >= rim_groups) & (other < groups - rim_groups)
            pl.when(jnp.logical_not(inside) if at_rim else inside)(trade(h, step).start)

    def take(count):
        taken = bufs[:count]
        del bufs[:count]
        return taken

    def chain(grid, order, back, src, full, first, piece):
        sems = take(4)
        scratch = take(len(stage_scratch(grid.sizes, order, piece)))
        where = tuple((plane_at if grid.planes else at)[first:])
        return scatter_stages(grid, order, src, scratch, full.at[where], sems[:2]) + gather_stages(
            grid, back, full, first, sems[2:]
        )

    a_steps = chain(grid, ORDER_A, (2, 3), gram_a, rows_a, 2, (share, cut))
    b_steps = chain(grid, ORDER_B, (2, 3), gram_b, rows_b, 2, (share, K - cut))
    d_steps = chain(planes, ORDER_D, (0, 1, 2), dpart, data_ref, 0, dpart.shape[3:])

    def advance(steps):
        if steps:
            steps.pop(0).finish()
        if steps:
            steps[0].start()

    def basis_gram(gram, low_column, high_column):
        width = high_column - low_column
        used = [group for group in range(groups) if group * rows_here < K]
        top = -(-(used[-1] * rows_here + slabs * share) // 16) * 16
        found = lax.dot_general(
            stacked[:top], stacked[low_column:high_column], across,
            preferred_element_type=jnp.float32,
        )
        for group in range(groups):
            where = (group // sizes[1], group % sizes[1])
            for number in range(slabs):
                begin = group * rows_here + number * share
                gram[where + (number // sizes[3], number % sizes[3])] = (
                    found[begin : begin + share]
                    if group in used
                    else jnp.zeros((share, width), jnp.float32)
                ).astype(gram.dtype)

    def smooth(x_ref, y_ref):
        load_x = pltpu.make_async_copy(
            x_hbm, x_ref.at[:, :, pl.ds(LEFT, extent)], load_sem.at[3]
        )
        load_s.start()
        load_x.start()
        load_w.start()
        lax.fori_loop(1, total, greet, 0)
        right = x_ref.shape[2] - LEFT - extent
        x_ref[:, :, :LEFT] = jnp.zeros((depth, frames, LEFT), x_ref.dtype)
        x_ref[:, :, LEFT + extent :] = jnp.zeros((depth, frames, right), x_ref.dtype)
        rest = stacked.shape[0] - K
        stacked[K:] = jnp.zeros((rest, stacked.shape[1]), stacked.dtype)

        def blank(number, _):
            for h in range(HALVES):
                y_ref[h, pl.ds(number * padded, RAD)] = jnp.zeros((RAD, some, RUN), jnp.float32)
            return 0

        lax.fori_loop(0, places + 1, blank, 0)
        load_s.wait()
        basis_gram(gram_a, 0, cut)
        pl.semaphore_wait(barrier, total - 1)
        a_steps[0].start()
        send_starts()
        load_w.wait()
        load_x.wait()
        kinds = w_ref.shape[0]

        blocks = 2
        steps = extent // (WIDE * kinds * blocks)

        def planar(h, block):
            def one(kind, _):
                numbers = [(block * steps + step) * kinds + kind for step in range(steps)]
                cells = [
                    x_ref[
                        :, h * some : (h + 1) * some, pl.ds(pl.multiple_of(at * WIDE, WIDE), SPAN)
                    ].reshape(depth * some, SPAN)
                    for at in numbers
                ]
                found = jnp.dot(
                    jnp.concatenate(cells, 0), w_ref[kind], preferred_element_type=jnp.float32
                )
                found = found.reshape(steps, depth, some, WIDE)
                for step, number in enumerate(numbers):
                    for side in range(2):
                        y_ref[h, pl.ds((2 * number + side) * padded + RAD, depth)] = found[
                            step, :, :, side * RUN : (side + 1) * RUN
                        ]
                return 0

            lax.fori_loop(0, kinds, one, 0)

        def pick(h, slot, run, shift, used):
            row = starts_at[slot, 0, run]
            if shift > 0:
                row = jnp.minimum(row + shift, places * padded)
            if shift < 0:
                row = jnp.maximum(row + shift, -(RAD + 1))
            found = None
            for tap in used:
                term = taps[tap] * y_ref[h, row + tap]
                found = term if found is None else found + term
            return found

        def over(count, action):
            def one(number, _):
                for run in range(runs):
                    action(number, run)
                return 0

            lax.fori_loop(0, count, one, 0)

        every = range(2 * RAD + 1)
        low_part = jnp.where(slab > 0, 1.0, 0.0)
        high_part = jnp.where(slab < slabs - 1, 1.0, 0.0)

        def pick_halos(h):
            def one_up(number, run):
                up_ref[h, number * runs + run] = pick(
                    h, groups + number, run, depth, range(RAD)
                ).astype(up_ref.dtype)

            def one_down(number, run):
                down_ref[h, number * runs + run] = pick(
                    h, groups + rim_groups + number, run, -depth, range(RAD + 1, 2 * RAD + 1)
                ).astype(down_ref.dtype)

            over(rim_groups, one_up)
            halos_up[h].start()
            over(rim_groups, one_down)
            halos_down[h].start()

        def pick_inner(h):
            def one(number, run):
                slot = number + rim_groups
                picked_ref[h, slot * runs + run] = pick(h, slot, run, 0, every).astype(
                    picked_ref.dtype
                )

            over(groups - 2 * rim_groups, one)
            start_trades(h, False)

        def pick_edges(h):
            halos_up[h].wait()
            halos_down[h].wait()

            def one(number, run):
                where = number * runs + run
                picked_ref[h, where] = (
                    pick(h, number, run, 0, every)
                    + low_part * below[h, where].astype(jnp.float32)
                ).astype(picked_ref.dtype)
                slot = number + groups - rim_groups
                picked_ref[h, slot * runs + run] = (
                    pick(h, slot, run, 0, every)
                    + high_part * above[h, where].astype(jnp.float32)
                ).astype(picked_ref.dtype)

            over(rim_groups, one)
            start_trades(h, True)

        planar(0, 0)
        advance(a_steps)
        planar(0, 1)
        await_starts()
        pick_halos(0)
        pick_inner(0)
        planar(1, 0)
        pick_edges(0)
        planar(1, 1)
        pick_halos(1)
        pick_inner(1)
        pick_edges(1)

    pl.run_scoped(
        smooth,
        pltpu.VMEM((depth, frames, extent + SPAN - WIDE), jnp.bfloat16),
        pltpu.VMEM((HALVES, places * padded + RAD, some, RUN), jnp.float32),
    )

    def finish(regrouped_rows):
        r_ref, out_ref = regrouped_rows
        load_r = pltpu.make_async_copy(r_hbm, r_ref, load_sem.at[4])
        load_r.start()
        for h in range(HALVES):
            regrouped[grp, h] = picked_ref[h, pl.ds(grp * runs, runs)]
        advance(a_steps)
        basis_gram(gram_b, cut, K)
        b_steps[0].start()
        advance(a_steps)
        advance(b_steps)
        for h in range(HALVES):
            for_peers(lambda step, h=h: trade(h, step).wait())

        half = groups // 2
        squares = [jnp.zeros((1, RUN), jnp.float32) for _ in range(2)]
        for run in range(runs):
            lanes = slice(run * RUN, (run + 1) * RUN)
            for subject in range(2):
                block = regrouped[subject * half : (subject + 1) * half, :, run]
                block = block.astype(jnp.float32)
                block = block.reshape(half * frames, RUN)
                mean = jnp.sum(block, axis=0, keepdims=True) * (1.0 / (half * frames))
                rounded = (block - mean).astype(stacked.dtype)
                begin = K + subject * half_rows
                stacked[begin : begin + half_rows, lanes] = rounded
                wide = rounded.astype(jnp.float32)
                squares[subject] = squares[subject] + jnp.sum(wide * wide, axis=0, keepdims=True)
        power_sum[0:1, :] = squares[0]
        power_sum[1:2, :] = squares[1]

        def share_power(axis, count, other):
            first = 0 if axis == 0 else groups

            def copy(step):
                return pltpu.make_async_remote_copy(
                    src_ref=power_sum, dst_ref=power_at.at[first + step],
                    send_sem=p_send.at[first + step], recv_sem=p_recv.at[first + step],
                    device_id=other(step), device_id_type=MESH,
                )

            def start():
                for step in range(1, count):
                    copy(step).start()

            def wait():
                found = power_sum[...]
                for step in range(1, count):
                    copy(step).wait()
                for step in range(1, count):
                    found = found + power_at[first + step]
                power_sum[...] = found

            return start, wait

        start_p, wait_p = share_power(0, groups, lambda step: (slab, lax.rem(grp + step, groups)))
        start_q, wait_q = share_power(1, slabs, lambda step: (lax.rem(slab + step, slabs), grp))
        start_p()

        found = lax.dot_general(
            stacked[K:order_rows], stacked[:order_rows], across,
            preferred_element_type=jnp.float32,
        )
        piece = data_rows // total
        for number in range(total):
            line, core = number // sizes[3], number % sizes[3]
            dpart[line // planes.sizes[1], line % planes.sizes[1], core] = found[
                number * piece : (number + 1) * piece
            ].astype(dpart.dtype)
        d_steps[0].start()
        wait_p()
        start_q()
        advance(d_steps)
        advance(a_steps)
        wait_q()
        power = jnp.sum(power_sum[...], axis=1, keepdims=True)
        scales = lax.rsqrt(power * (1.0 / (masked * half_rows)) + epsilon)
        scale_ref[...] = jnp.broadcast_to(scales, scale_ref.shape)

        load_r.wait()
        edge = K // RUN * RUN
        lane = lax.broadcasted_iota(jnp.int32, (1, order_rows - edge), 1) + edge
        factor = jnp.where(
            lane < K, 1.0, jnp.where(lane < K + half_rows, scales[0:1], scales[1:2])
        )
        r_ref[:, edge:] = (r_ref[:, edge:].astype(jnp.float32) * factor).astype(r_ref.dtype)

        chunk = out_ref.shape[1]
        copies = []

        def rotate(number):
            slot = number % 2
            if number >= 2:
                copies[number - 2].wait()
            rows = slice(number * chunk, (number + 1) * chunk)
            out_ref[slot] = jnp.dot(
                r_ref[rows], stacked[:order_rows], preferred_element_type=jnp.float32
            ).astype(out_ref.dtype)
            copy = pltpu.make_async_copy(
                out_ref.at[slot], new_hbm.at[pl.ds(number * chunk, chunk)], load_sem.at[5 + slot]
            )
            copy.start()
            copies.append(copy)

        count = K // chunk
        rotate(0)
        todo = list(range(1, count))
        turn = 0
        while d_steps or a_steps or b_steps:
            for steps in (d_steps, a_steps) if turn == 1 else (d_steps, a_steps, b_steps):
                advance(steps)
            if todo:
                rotate(todo.pop(0))
            turn += 1
        while todo:
            rotate(todo.pop(0))
        for copy in copies[-2:]:
            copy.wait()

    pl.run_scoped(
        lambda r_ref, out_ref: finish((r_ref, out_ref)),
        pltpu.VMEM((K, order_rows), jnp.bfloat16),
        pltpu.VMEM((2, K // 5, runs * RUN), jnp.bfloat16),
    )


HALVES = 2
ORDER_A, ORDER_B, ORDER_D = (3, 1, 2, 0), (3, 2, 1, 0), (2, 1, 0)


def run_group(cells, mask, subspace, turned, weights, sizes, masked, rows_here, share):
    depth, frames, extent = cells.shape
    vmem = pl.BlockSpec(memory_space=pltpu.VMEM)
    hbm = pl.BlockSpec(memory_space=pl.ANY)
    groups, slabs = sizes[0] * sizes[1], sizes[2] * sizes[3]
    total = groups * slabs
    runs = mask.shape[0]
    own = groups * runs
    rim_groups = groups * RAD // depth
    rim = rim_groups * runs
    data_rows = frames * groups
    order_rows = K + data_rows
    cut = -(-K // (2 * RUN)) * RUN
    planes = Grid(sizes, True)
    flat = planes.sizes
    d_piece = (data_rows // total, order_rows)
    last = (groups - 1) * rows_here // 16 * 16 + slabs * share + 16
    stacked_rows = max(order_rows, last)
    some = frames // HALVES
    rim_shape = pltpu.VMEM((HALVES, rim, some, RUN), jnp.bfloat16)
    dma = pltpu.SemaphoreType.DMA
    dims = (sizes, cut, depth, frames, extent, runs, share, masked, rows_here)
    slots = groups + 2 * rim_groups
    return pl.pallas_call(
        functools.partial(group_kernel, dims),
        out_shape=(
            jax.ShapeDtypeStruct(tuple(sizes[2:]) + (share, cut), jnp.bfloat16),
            jax.ShapeDtypeStruct(tuple(sizes[2:]) + (share, K - cut), jnp.bfloat16),
            jax.ShapeDtypeStruct(tuple(flat) + d_piece, jnp.bfloat16),
            jax.ShapeDtypeStruct((2, RUN), jnp.float32),
            jax.ShapeDtypeStruct(subspace.shape, jnp.bfloat16),
        ),
        in_specs=[hbm, vmem, hbm, hbm, hbm],
        out_specs=(vmem, vmem, vmem, vmem, hbm),
        scratch_shapes=[
            pltpu.VMEM((stacked_rows, runs * RUN), jnp.bfloat16),
            pltpu.VMEM(tuple(sizes) + (share, cut), jnp.bfloat16),
            pltpu.VMEM(tuple(sizes) + (share, K - cut), jnp.bfloat16),
            pltpu.VMEM(tuple(flat) + d_piece, jnp.bfloat16),
            rim_shape, rim_shape, rim_shape, rim_shape,
            pltpu.VMEM((HALVES, own, some, RUN), jnp.bfloat16),
            pltpu.VMEM((groups, HALVES, runs, some, RUN), jnp.bfloat16),
            pltpu.VMEM((slots, 1, RUN), jnp.int32),
            pltpu.SMEM((slots, 1, RUN), jnp.int32),
            pltpu.VMEM((groups + slabs, 2, RUN), jnp.float32),
            pltpu.VMEM((2, RUN), jnp.float32),
            pltpu.VMEM(weights.shape, jnp.bfloat16),
            dma((7,)),
            dma((groups,)), dma((groups,)),
            dma((groups,)), dma((2 * rim_groups,)),
            dma((2 * HALVES,)), dma((2 * HALVES,)),
            dma((HALVES, groups)), dma((HALVES, groups)),
            dma((groups + slabs,)), dma((groups + slabs,)),
        ]
        + stage_sems(sizes)
        + stage_scratch(sizes, ORDER_A, (share, cut))
        + stage_sems(sizes)
        + stage_scratch(sizes, ORDER_B, (share, K - cut))
        + stage_sems(flat)
        + stage_scratch(flat, ORDER_D, d_piece),
        compiler_params=pltpu.CompilerParams(
            collective_id=1, has_side_effects=True, vmem_limit_bytes=63 * 1024 * 1024
        ),
    )(cells, mask, subspace, turned, weights)


def close_kernel(rows_here, masked, a_hbm, b_hbm, data_hbm, scale_hbm, new_hbm, gram_ref,
                 out_hbm, held, a_ref, b_ref, data_ref, scale_ref, wide, turned, low, sem):
    first = lax.axis_index("grp") * rows_here
    data_rows, order_rows = data_ref.shape
    parts = 5
    chunk = K // parts
    fetches = [
        pltpu.make_async_copy(
            new_hbm.at[pl.ds(part * chunk, chunk)], held.at[part], sem.at[part]
        )
        for part in range(parts)
    ]
    copies = [
        pltpu.make_async_copy(
            held.at[part], out_hbm.at[pl.ds(part * chunk, chunk)], sem.at[parts + part]
        )
        for part in range(parts)
    ]
    loads = [
        pltpu.make_async_copy(source, target, sem.at[2 * parts + number])
        for number, (source, target) in enumerate(
            ((data_hbm, data_ref), (scale_hbm, scale_ref), (a_hbm, a_ref), (b_hbm, b_ref))
        )
    ]
    for copy in loads + fetches:
        copy.start()
    for copy in loads:
        copy.wait()

    def rows_from(ref, start):
        size = -(-rows_here // 8) * 8 + 8
        held = ref[pl.ds(pl.multiple_of(start // 8 * 8, 8), size)]
        return pltpu.roll(held, lax.rem(size - lax.rem(start, 8), size), 0)[:rows_here]

    window = turned.shape[0]
    data = data_ref[...].astype(jnp.float32)
    wide[:, :order_rows] = data
    begin = pl.multiple_of(first // RUN * RUN, RUN)
    turned[...] = wide[:, pl.ds(begin, window)].T
    for fetch, copy in zip(fetches, copies):
        fetch.wait()
        copy.start()
    right = rows_from(turned, first - begin)
    low[:rows_here] = jnp.zeros((rows_here, K), jnp.float32)
    rest = low.shape[0] - rows_here - data_rows
    low[rows_here + data_rows :] = jnp.zeros((rest, K), jnp.float32)
    low[rows_here : rows_here + data_rows] = data[:, :K]
    below = rows_from(low, jnp.maximum(first - K + rows_here, 0))

    half = data_rows // 2
    scales = scale_ref[:, :1]

    def scale_of(index):
        return jnp.where(
            index < K, 1.0, jnp.where(index < K + half, scales[0:1], scales[1:2])
        )

    row = scale_of(lax.broadcasted_iota(jnp.int32, (rows_here, 1), 0) + first)
    row = row * (1.0 / masked)
    column = scale_of(lax.broadcasted_iota(jnp.int32, (1, data_rows), 1) + K)
    cut = a_ref.shape[1]
    gram_ref[:, :cut] = (a_ref[...].astype(jnp.float32)[:rows_here] + below[:, :cut]) * row
    gram_ref[:, cut:K] = (b_ref[...].astype(jnp.float32)[:rows_here] + below[:, cut:]) * row
    gram_ref[:, K:] = right * (row * column)
    for copy in copies:
        copy.wait()


def close_up(rows_a, rows_b, data, scales, new_subspace, rows_here, masked):
    vmem = pl.BlockSpec(memory_space=pltpu.VMEM)
    hbm = pl.BlockSpec(memory_space=pl.ANY)
    data_rows, order_rows = data.shape
    window = -(-(rows_here + RUN) // RUN) * RUN
    wide = (order_rows // RUN) * RUN + window
    return pl.pallas_call(
        functools.partial(close_kernel, rows_here, masked),
        out_shape=(
            jax.ShapeDtypeStruct((rows_here, order_rows), jnp.float32),
            jax.ShapeDtypeStruct(new_subspace.shape, new_subspace.dtype),
        ),
        in_specs=[hbm] * 5,
        out_specs=(vmem, hbm),
        scratch_shapes=[
            pltpu.VMEM((5, K // 5, new_subspace.shape[1]), new_subspace.dtype),
            pltpu.VMEM(rows_a.shape, rows_a.dtype),
            pltpu.VMEM(rows_b.shape, rows_b.dtype),
            pltpu.VMEM(data.shape, data.dtype),
            pltpu.VMEM(scales.shape, scales.dtype),
            pltpu.VMEM((data_rows, wide), jnp.float32),
            pltpu.VMEM((window, data_rows), jnp.float32),
            pltpu.VMEM((2 * rows_here + data_rows + 16, K), jnp.float32),
            pltpu.SemaphoreType.DMA((14,)),
        ],
        compiler_params=pltpu.CompilerParams(vmem_limit_bytes=62 * 1024 * 1024),
    )(rows_a, rows_b, data, scales, new_subspace)


def body(raw_frames, mask_index, subspace, rotation):
    frames_here, slab_depth, extent = raw_frames.shape
    per_device = subspace.shape[1]
    group_count = lax.axis_size("grp")
    slab_count = lax.axis_size("slab")
    sizes = axes_of(group_count, slab_count)
    masked = per_device * slab_count * group_count
    frame_count = frames_here * group_count
    order_rows = K + frame_count
    rows_here = order_rows // group_count
    share = -(-rows_here // (16 * slab_count)) * 16

    rows_a, rows_b, data, scales, new_subspace = run_group(
        raw_frames.transpose(1, 0, 2), mask_index.reshape(-1, RUN), subspace, rotation.T,
        jnp.asarray(plane_weights()), sizes, masked, rows_here, share,
    )
    return close_up(
        rows_a.reshape(share * slab_count, -1), rows_b.reshape(share * slab_count, -1),
        data.reshape(frame_count, order_rows), scales, new_subspace, rows_here, masked,
    )


def solution(mesh):
    placed = (P("grp", "slab", None), P(("slab", "grp")), P(None, ("slab", "grp")), P())
    return jax.shard_map(
        body,
        mesh=mesh,
        in_specs=placed,
        out_specs=(P("grp", None), P(None, ("slab", "grp"))),
        check_vma=False,
    )
```

```python
import functools
import math

import jax
import jax.numpy as jnp
import numpy as np
from jax import lax
from jax.experimental import pallas as pl
from jax.experimental.pallas import tpu as pltpu
from jax.sharding import PartitionSpec as P

NX = 96
RUN = 128
RAD = 3
K = 1200
MESH = pl.DeviceIdType.MESH

smooth_sigma = 1.0617
epsilon = 1e-06

WIDE = 2 * RUN
LEFT = 3 * RUN
SPAN = 8 * RUN


def tap_weights():
    unscaled = [
        math.exp(-offset * offset / (2.0 * smooth_sigma * smooth_sigma))
        for offset in range(-RAD, RAD + 1)
    ]
    summed = sum(unscaled)
    return [weight / summed for weight in unscaled]


def plane_weights():
    taps = np.array(tap_weights())
    kinds = NX // math.gcd(WIDE, NX)
    out = np.zeros((kinds, SPAN, WIDE))
    for kind in range(kinds):
        target = np.arange(WIDE)
        column = (kind * WIDE + target) % NX
        for dy in range(-RAD, RAD + 1):
            for dx in range(-RAD, RAD + 1):
                inside = (column + dx >= 0) & (column + dx < NX)
                source = target + LEFT + dy * NX + dx
                out[kind, source[inside], target[inside]] = taps[dy + RAD] * taps[dx + RAD]
    return out.astype(jnp.bfloat16)


def axes_of(groups, slabs):
    outer = 4 if groups % 4 == 0 else 1
    cores = 2 if slabs % 2 == 0 else 1
    return outer, groups // outer, slabs // cores, cores


class Grid:
    def __init__(self, sizes, planes):
        self.full, self.planes = sizes, planes
        z, y, x, cores = sizes
        self.sizes = (z, y * x, cores) if planes else tuple(sizes)

    def here(self):
        _, ys, xs, cores = self.full
        slab, grp = lax.axis_index("slab"), lax.axis_index("grp")
        z, y, x, core = grp // ys, lax.rem(grp, ys), slab // cores, lax.rem(slab, cores)
        return [z, y * xs + x, core] if self.planes else [z, y, x, core]

    def device(self, at):
        _, ys, xs, cores = self.full
        if self.planes:
            at = [at[0], at[1] // xs, lax.rem(at[1], xs), at[2]]
        return (at[2] * cores + at[3], at[0] * ys + at[1])

    def moved(self, at, axis, step):
        other = lax.rem(at[axis] + step, self.sizes[axis])
        return at[:axis] + [other] + at[axis + 1 :], other


class Scatter:
    def __init__(self, grid, axis, left, src, landed, out, sems):
        self.grid, self.axis, self.src, self.landed, self.out = grid, axis, src, landed, out
        self.sizes = grid.sizes
        self.dim = left.index(axis)
        self.left = [other for other in left if other != axis]
        self.send_sem, self.recv_sem = sems
        self.at = grid.here()

    def part(self, where):
        return self.src.at[(slice(None),) * self.dim + (where,)]

    def copy(self, step):
        there, other = self.grid.moved(self.at, self.axis, step)
        return pltpu.make_async_remote_copy(
            src_ref=self.part(other),
            dst_ref=self.landed.at[step - 1],
            send_sem=self.send_sem.at[self.axis, step],
            recv_sem=self.recv_sem.at[self.axis, step],
            device_id=self.grid.device(there),
            device_id_type=MESH,
        )

    def start(self):
        for step in range(1, self.sizes[self.axis]):
            self.copy(step).start()

    def finish(self):
        for step in range(1, self.sizes[self.axis]):
            self.copy(step).wait()
        mine = self.part(self.at[self.axis])
        lead = [self.sizes[axis] for axis in self.left]
        total = math.prod(lead)

        def add(index, _):
            where = []
            for size in reversed(lead):
                where.insert(0, lax.rem(index, size))
                index = index // size
            where = tuple(where)
            value = mine[where].astype(jnp.float32)
            for step in range(self.sizes[self.axis] - 1):
                value = value + self.landed[(step,) + where].astype(jnp.float32)
            self.out[where] = value.astype(self.out.dtype)
            return 0

        lax.fori_loop(0, total, add, 0)


class Gather:
    def __init__(self, grid, axis, done, full, first, sems):
        self.grid, self.sizes, self.axis, self.full = grid, grid.sizes, axis, full
        self.send_sem, self.recv_sem = sems
        self.at = grid.here()
        self.where = tuple(
            slice(None) if other in done else self.at[other] for other in range(first, len(self.sizes))
        )

    def copy(self, step):
        there, _ = self.grid.moved(self.at, self.axis, step)
        return pltpu.make_async_remote_copy(
            src_ref=self.full.at[self.where],
            dst_ref=self.full.at[self.where],
            send_sem=self.send_sem.at[self.axis, step],
            recv_sem=self.recv_sem.at[self.axis, step],
            device_id=self.grid.device(there),
            device_id_type=MESH,
        )

    def start(self):
        for step in range(1, self.sizes[self.axis]):
            self.copy(step).start()

    def finish(self):
        for step in range(1, self.sizes[self.axis]):
            self.copy(step).wait()


def gather_stages(grid, order, full, first, sems):
    stages, done = [], []
    for axis in order:
        if grid.sizes[axis] > 1:
            stages.append(Gather(grid, axis, list(done), full, first, sems))
        done.append(axis)
    return stages


def stage_scratch(sizes, order, piece):
    out = []
    left = [axis for axis in range(len(sizes)) if sizes[axis] > 1]
    for axis in order:
        if sizes[axis] == 1:
            continue
        left.remove(axis)
        shape = tuple(sizes[other] for other in left) + piece
        out.append(pltpu.VMEM((sizes[axis] - 1,) + shape, jnp.bfloat16))
        if left:
            out.append(pltpu.VMEM(shape, jnp.bfloat16))
    return out


def stage_sems(sizes):
    most = max(sizes)
    return [pltpu.SemaphoreType.DMA((4, most)) for _ in range(4)]


def scatter_stages(grid, order, src, bufs, result, sems):
    stages, sizes = [], grid.sizes
    left = list(range(len(sizes)))
    for axis in order:
        if sizes[axis] == 1:
            src = src.at[(slice(None),) * left.index(axis) + (0,)]
            left = [other for other in left if other != axis]
    order = [axis for axis in order if sizes[axis] > 1]
    for number, axis in enumerate(order):
        last = number == len(order) - 1
        out = result if last else bufs[2 * number + 1]
        stages.append(Scatter(grid, axis, left, src, bufs[2 * number], out, sems))
        left = stages[-1].left
        src = out
    return stages


def place(peer, groups):
    return (peer // groups, lax.rem(peer, groups))


def group_kernel(dims, x_hbm, mask_ref, s_hbm, r_hbm, w_hbm,
                 rows_a, rows_b, data_ref, scale_ref, new_hbm,
                 stacked, gram_a, gram_b, dpart, up_ref, down_ref, below, above, picked_ref,
                 regrouped, starts, starts_at, power_at, power_sum, w_ref,
                 load_sem, mask_send, mask_recv, rim_send, rim_recv, halo_send, halo_recv,
                 all_send, all_recv, p_send, p_recv, *bufs):
    sizes, cut, depth, frames, extent, runs, share, masked, rows_here = dims
    groups, slabs = sizes[0] * sizes[1], sizes[2] * sizes[3]
    total = groups * slabs
    slab, grp = lax.axis_index("slab"), lax.axis_index("grp")
    me = slab * groups + grp
    grid, planes = Grid(sizes, False), Grid(sizes, True)
    at, plane_at = grid.here(), planes.here()
    bufs = list(bufs)
    upper = lax.rem(slab + 1, slabs)
    lower = lax.rem(slab + slabs - 1, slabs)
    own = runs * groups
    rim_groups = groups * RAD // depth
    rim = rim_groups * runs
    places = extent // RUN
    padded = depth + RAD
    taps = tap_weights()
    data_rows = frames * groups
    order_rows = K + data_rows
    half_rows = data_rows // 2
    some = frames // HALVES
    across = (((1,), (1,)), ((), ()))

    load_s = pltpu.make_async_copy(s_hbm, stacked.at[pl.ds(0, K)], load_sem.at[1])
    load_w = pltpu.make_async_copy(w_hbm, w_ref, load_sem.at[2])

    barrier = pltpu.get_barrier_semaphore()

    def greet(step, _):
        pl.semaphore_signal(
            barrier, inc=1, device_id=place(lax.rem(me + step, total), groups),
            device_id_type=MESH,
        )
        return 0

    def trade_starts(step):
        return pltpu.make_async_remote_copy(
            src_ref=starts.at[grp], dst_ref=starts.at[grp],
            send_sem=mask_send.at[step], recv_sem=mask_recv.at[step],
            device_id=(slab, lax.rem(grp + step, groups)), device_id_type=MESH,
        )

    def rim_starts(side, there, number, to):
        slot = groups + side * rim_groups + number
        return pltpu.make_async_remote_copy(
            src_ref=starts.at[grp], dst_ref=starts.at[slot],
            send_sem=rim_send.at[to], recv_sem=rim_recv.at[side * rim_groups + number],
            device_id=(there, to), device_id_type=MESH,
        )

    def for_peers(action):
        def one(step, _):
            action(step)
            return 0

        lax.fori_loop(1, groups, one, 0)

    def for_rim(action):
        def one(to, _):
            @pl.when(grp < rim_groups)
            def _():
                action(rim_starts(0, lower, grp, to))

            @pl.when(grp >= groups - rim_groups)
            def _():
                action(rim_starts(1, upper, grp - (groups - rim_groups), to))

            return 0

        lax.fori_loop(0, groups, one, 0)

    def send_starts():
        lane = lax.broadcasted_iota(jnp.int32, (1, RUN), 1)
        first = jnp.zeros((1, RUN), jnp.int32)
        for run in range(runs):
            first = jnp.where(lane == run, mask_ref[run : run + 1, :] - run, first)
        cell = lax.shift_right_arithmetic(first, 7) - slab * (depth * places)
        plane = jnp.zeros((1, RUN), jnp.int32)
        for number in range(1, depth):
            plane = plane + jnp.where(cell >= number * places, 1, 0)
        row = (cell - plane * places) * padded + plane
        row = jnp.minimum(jnp.maximum(row, 0), (places - 1) * padded + depth - 1)
        starts[grp] = jnp.where(lane < runs, row, 0)
        for_peers(lambda step: trade_starts(step).start())
        for_rim(lambda copy: copy.start())

    def await_starts():
        for_peers(lambda step: trade_starts(step).wait())
        for_rim(lambda copy: copy.wait_send())
        for number in range(rim_groups):
            rim_starts(0, lower, number, grp).wait_recv()
            rim_starts(1, upper, number, grp).wait_recv()
        copy = pltpu.make_async_copy(starts, starts_at, load_sem.at[0])
        copy.start()
        copy.wait()

    def halo(src, dst, number, other):
        return pltpu.make_async_remote_copy(
            src_ref=src, dst_ref=dst, send_sem=halo_send.at[number], recv_sem=halo_recv.at[number],
            device_id=(other, grp), device_id_type=MESH,
        )

    halos_up = [halo(up_ref.at[h], below.at[h], h, upper) for h in range(HALVES)]
    halos_down = [halo(down_ref.at[h], above.at[h], HALVES + h, lower) for h in range(HALVES)]

    def trade(h, step):
        other = lax.rem(grp + step, groups)
        return pltpu.make_async_remote_copy(
            src_ref=picked_ref.at[h, pl.ds(other * runs, runs)], dst_ref=regrouped.at[grp, h],
            send_sem=all_send.at[h, step], recv_sem=all_recv.at[h, step],
            device_id=(slab, other), device_id_type=MESH,
        )

    def start_trades(h, at_rim):
        for step in range(1, groups):
            other = lax.rem(grp + step, groups)
            inside = (other >= rim_groups) & (other < groups - rim_groups)
            pl.when(jnp.logical_not(inside) if at_rim else inside)(trade(h, step).start)

    def take(count):
        taken = bufs[:count]
        del bufs[:count]
        return taken

    def chain(grid, order, back, src, full, first, piece):
        sems = take(4)
        scratch = take(len(stage_scratch(grid.sizes, order, piece)))
        where = tuple((plane_at if grid.planes else at)[first:])
        return scatter_stages(grid, order, src, scratch, full.at[where], sems[:2]) + gather_stages(
            grid, back, full, first, sems[2:]
        )

    a_steps = chain(grid, ORDER_A, (2, 3), gram_a, rows_a, 2, (share, cut))
    b_steps = chain(grid, ORDER_B, (2, 3), gram_b, rows_b, 2, (share, K - cut))
    d_steps = chain(planes, ORDER_D, (0, 1, 2), dpart, data_ref, 0, dpart.shape[3:])

    def advance(steps):
        if steps:
            steps.pop(0).finish()
        if steps:
            steps[0].start()

    def basis_gram(gram, low_column, high_column):
        width = high_column - low_column
        used = [group for group in range(groups) if group * rows_here < K]
        top = -(-(used[-1] * rows_here + slabs * share) // 16) * 16
        found = lax.dot_general(
            stacked[:top], stacked[low_column:high_column], across,
            preferred_element_type=jnp.float32,
        )
        for group in range(groups):
            where = (group // sizes[1], group % sizes[1])
            for number in range(slabs):
                begin = group * rows_here + number * share
                gram[where + (number // sizes[3], number % sizes[3])] = (
                    found[begin : begin + share]
                    if group in used
                    else jnp.zeros((share, width), jnp.float32)
                ).astype(gram.dtype)

    def smooth(x_ref, y_ref):
        load_x = pltpu.make_async_copy(
            x_hbm, x_ref.at[:, :, pl.ds(LEFT, extent)], load_sem.at[3]
        )
        load_s.start()
        load_x.start()
        load_w.start()
        lax.fori_loop(1, total, greet, 0)
        right = x_ref.shape[2] - LEFT - extent
        x_ref[:, :, :LEFT] = jnp.zeros((depth, frames, LEFT), x_ref.dtype)
        x_ref[:, :, LEFT + extent :] = jnp.zeros((depth, frames, right), x_ref.dtype)
        rest = stacked.shape[0] - K
        stacked[K:] = jnp.zeros((rest, stacked.shape[1]), stacked.dtype)

        def blank(number, _):
            for h in range(HALVES):
                y_ref[h, pl.ds(number * padded, RAD)] = jnp.zeros((RAD, some, RUN), jnp.float32)
            return 0

        lax.fori_loop(0, places + 1, blank, 0)
        load_s.wait()
        basis_gram(gram_a, 0, cut)
        pl.semaphore_wait(barrier, total - 1)
        a_steps[0].start()
        send_starts()
        load_w.wait()
        load_x.wait()
        kinds = w_ref.shape[0]

        blocks = 2
        steps = extent // (WIDE * kinds * blocks)

        def planar(h, block):
            def one(kind, _):
                numbers = [(block * steps + step) * kinds + kind for step in range(steps)]
                cells = [
                    x_ref[
                        :, h * some : (h + 1) * some, pl.ds(pl.multiple_of(at * WIDE, WIDE), SPAN)
                    ].reshape(depth * some, SPAN)
                    for at in numbers
                ]
                found = jnp.dot(
                    jnp.concatenate(cells, 0), w_ref[kind], preferred_element_type=jnp.float32
                )
                found = found.reshape(steps, depth, some, WIDE)
                for step, number in enumerate(numbers):
                    for side in range(2):
                        y_ref[h, pl.ds((2 * number + side) * padded + RAD, depth)] = found[
                            step, :, :, side * RUN : (side + 1) * RUN
                        ]
                return 0

            lax.fori_loop(0, kinds, one, 0)

        def pick(h, slot, run, shift, used):
            row = starts_at[slot, 0, run]
            if shift > 0:
                row = jnp.minimum(row + shift, places * padded)
            if shift < 0:
                row = jnp.maximum(row + shift, -(RAD + 1))
            found = None
            for tap in used:
                term = taps[tap] * y_ref[h, row + tap]
                found = term if found is None else found + term
            return found

        def over(count, action):
            def one(number, _):
                for run in range(runs):
                    action(number, run)
                return 0

            lax.fori_loop(0, count, one, 0)

        every = range(2 * RAD + 1)
        low_part = jnp.where(slab > 0, 1.0, 0.0)
        high_part = jnp.where(slab < slabs - 1, 1.0, 0.0)

        def pick_halos(h):
            def one_up(number, run):
                up_ref[h, number * runs + run] = pick(
                    h, groups + number, run, depth, range(RAD)
                ).astype(up_ref.dtype)

            def one_down(number, run):
                down_ref[h, number * runs + run] = pick(
                    h, groups + rim_groups + number, run, -depth, range(RAD + 1, 2 * RAD + 1)
                ).astype(down_ref.dtype)

            over(rim_groups, one_up)
            halos_up[h].start()
            over(rim_groups, one_down)
            halos_down[h].start()

        def pick_inner(h):
            def one(number, run):
                slot = number + rim_groups
                picked_ref[h, slot * runs + run] = pick(h, slot, run, 0, every).astype(
                    picked_ref.dtype
                )

            over(groups - 2 * rim_groups, one)
            start_trades(h, False)

        def pick_edges(h):
            halos_up[h].wait()
            halos_down[h].wait()

            def one(number, run):
                where = number * runs + run
                picked_ref[h, where] = (
                    pick(h, number, run, 0, every)
                    + low_part * below[h, where].astype(jnp.float32)
                ).astype(picked_ref.dtype)
                slot = number + groups - rim_groups
                picked_ref[h, slot * runs + run] = (
                    pick(h, slot, run, 0, every)
                    + high_part * above[h, where].astype(jnp.float32)
                ).astype(picked_ref.dtype)

            over(rim_groups, one)
            start_trades(h, True)

        planar(0, 0)
        advance(a_steps)
        planar(0, 1)
        await_starts()
        pick_halos(0)
        pick_inner(0)
        planar(1, 0)
        pick_edges(0)
        planar(1, 1)
        pick_halos(1)
        pick_inner(1)
        pick_edges(1)

    pl.run_scoped(
        smooth,
        pltpu.VMEM((depth, frames, extent + SPAN - WIDE), jnp.bfloat16),
        pltpu.VMEM((HALVES, places * padded + RAD, some, RUN), jnp.float32),
    )

    def finish(regrouped_rows):
        r_ref, out_ref = regrouped_rows
        load_r = pltpu.make_async_copy(r_hbm, r_ref, load_sem.at[4])
        load_r.start()
        for h in range(HALVES):
            regrouped[grp, h] = picked_ref[h, pl.ds(grp * runs, runs)]
        advance(a_steps)
        basis_gram(gram_b, cut, K)
        b_steps[0].start()
        advance(a_steps)
        advance(b_steps)
        for h in range(HALVES):
            for_peers(lambda step, h=h: trade(h, step).wait())

        half = groups // 2
        squares = [jnp.zeros((1, RUN), jnp.float32) for _ in range(2)]
        for run in range(runs):
            lanes = slice(run * RUN, (run + 1) * RUN)
            for subject in range(2):
                block = regrouped[subject * half : (subject + 1) * half, :, run]
                block = block.astype(jnp.float32)
                block = block.reshape(half * frames, RUN)
                mean = jnp.sum(block, axis=0, keepdims=True) * (1.0 / (half * frames))
                rounded = (block - mean).astype(stacked.dtype)
                begin = K + subject * half_rows
                stacked[begin : begin + half_rows, lanes] = rounded
                wide = rounded.astype(jnp.float32)
                squares[subject] = squares[subject] + jnp.sum(wide * wide, axis=0, keepdims=True)
        power_sum[0:1, :] = squares[0]
        power_sum[1:2, :] = squares[1]

        def share_power(axis, count, other):
            first = 0 if axis == 0 else groups

            def copy(step):
                return pltpu.make_async_remote_copy(
                    src_ref=power_sum, dst_ref=power_at.at[first + step],
                    send_sem=p_send.at[first + step], recv_sem=p_recv.at[first + step],
                    device_id=other(step), device_id_type=MESH,
                )

            def start():
                for step in range(1, count):
                    copy(step).start()

            def wait():
                found = power_sum[...]
                for step in range(1, count):
                    copy(step).wait()
                for step in range(1, count):
                    found = found + power_at[first + step]
                power_sum[...] = found

            return start, wait

        start_p, wait_p = share_power(0, groups, lambda step: (slab, lax.rem(grp + step, groups)))
        start_q, wait_q = share_power(1, slabs, lambda step: (lax.rem(slab + step, slabs), grp))
        start_p()

        found = lax.dot_general(
            stacked[K:order_rows], stacked[:order_rows], across,
            preferred_element_type=jnp.float32,
        )
        piece = data_rows // total
        for number in range(total):
            line, core = number // sizes[3], number % sizes[3]
            dpart[line // planes.sizes[1], line % planes.sizes[1], core] = found[
                number * piece : (number + 1) * piece
            ].astype(dpart.dtype)
        d_steps[0].start()
        wait_p()
        start_q()
        advance(d_steps)
        advance(a_steps)
        wait_q()
        power = jnp.sum(power_sum[...], axis=1, keepdims=True)
        scales = lax.rsqrt(power * (1.0 / (masked * half_rows)) + epsilon)
        scale_ref[...] = jnp.broadcast_to(scales, scale_ref.shape)

        load_r.wait()
        edge = K // RUN * RUN
        lane = lax.broadcasted_iota(jnp.int32, (1, order_rows - edge), 1) + edge
        factor = jnp.where(
            lane < K, 1.0, jnp.where(lane < K + half_rows, scales[0:1], scales[1:2])
        )
        r_ref[:, edge:] = (r_ref[:, edge:].astype(jnp.float32) * factor).astype(r_ref.dtype)

        chunk = out_ref.shape[1]
        copies = []

        def rotate(number):
            slot = number % 2
            if number >= 2:
                copies[number - 2].wait()
            rows = slice(number * chunk, (number + 1) * chunk)
            out_ref[slot] = jnp.dot(
                r_ref[rows], stacked[:order_rows], preferred_element_type=jnp.float32
            ).astype(out_ref.dtype)
            copy = pltpu.make_async_copy(
                out_ref.at[slot], new_hbm.at[pl.ds(number * chunk, chunk)], load_sem.at[5 + slot]
            )
            copy.start()
            copies.append(copy)

        count = K // chunk
        rotate(0)
        todo = list(range(1, count))
        while d_steps or a_steps or b_steps:
            for steps in (d_steps, a_steps, b_steps):
                advance(steps)
            if todo:
                rotate(todo.pop(0))
        while todo:
            rotate(todo.pop(0))
        for copy in copies[-2:]:
            copy.wait()

    pl.run_scoped(
        lambda r_ref, out_ref: finish((r_ref, out_ref)),
        pltpu.VMEM((K, order_rows), jnp.bfloat16),
        pltpu.VMEM((2, K // 5, runs * RUN), jnp.bfloat16),
    )


HALVES = 2
ORDER_A, ORDER_B, ORDER_D = (3, 1, 2, 0), (3, 2, 1, 0), (2, 1, 0)


def run_group(cells, mask, subspace, turned, weights, sizes, masked, rows_here, share):
    depth, frames, extent = cells.shape
    vmem = pl.BlockSpec(memory_space=pltpu.VMEM)
    hbm = pl.BlockSpec(memory_space=pl.ANY)
    groups, slabs = sizes[0] * sizes[1], sizes[2] * sizes[3]
    total = groups * slabs
    runs = mask.shape[0]
    own = groups * runs
    rim_groups = groups * RAD // depth
    rim = rim_groups * runs
    data_rows = frames * groups
    order_rows = K + data_rows
    cut = -(-K * 3 // (5 * RUN)) * RUN
    planes = Grid(sizes, True)
    flat = planes.sizes
    d_piece = (data_rows // total, order_rows)
    last = (groups - 1) * rows_here // 16 * 16 + slabs * share + 16
    stacked_rows = max(order_rows, last)
    some = frames // HALVES
    rim_shape = pltpu.VMEM((HALVES, rim, some, RUN), jnp.bfloat16)
    dma = pltpu.SemaphoreType.DMA
    dims = (sizes, cut, depth, frames, extent, runs, share, masked, rows_here)
    slots = groups + 2 * rim_groups
    return pl.pallas_call(
        functools.partial(group_kernel, dims),
        out_shape=(
            jax.ShapeDtypeStruct(tuple(sizes[2:]) + (share, cut), jnp.bfloat16),
            jax.ShapeDtypeStruct(tuple(sizes[2:]) + (share, K - cut), jnp.bfloat16),
            jax.ShapeDtypeStruct(tuple(flat) + d_piece, jnp.bfloat16),
            jax.ShapeDtypeStruct((2, RUN), jnp.float32),
            jax.ShapeDtypeStruct(subspace.shape, jnp.bfloat16),
        ),
        in_specs=[hbm, vmem, hbm, hbm, hbm],
        out_specs=(vmem, vmem, vmem, vmem, hbm),
        scratch_shapes=[
            pltpu.VMEM((stacked_rows, runs * RUN), jnp.bfloat16),
            pltpu.VMEM(tuple(sizes) + (share, cut), jnp.bfloat16),
            pltpu.VMEM(tuple(sizes) + (share, K - cut), jnp.bfloat16),
            pltpu.VMEM(tuple(flat) + d_piece, jnp.bfloat16),
            rim_shape, rim_shape, rim_shape, rim_shape,
            pltpu.VMEM((HALVES, own, some, RUN), jnp.bfloat16),
            pltpu.VMEM((groups, HALVES, runs, some, RUN), jnp.bfloat16),
            pltpu.VMEM((slots, 1, RUN), jnp.int32),
            pltpu.SMEM((slots, 1, RUN), jnp.int32),
            pltpu.VMEM((groups + slabs, 2, RUN), jnp.float32),
            pltpu.VMEM((2, RUN), jnp.float32),
            pltpu.VMEM(weights.shape, jnp.bfloat16),
            dma((7,)),
            dma((groups,)), dma((groups,)),
            dma((groups,)), dma((2 * rim_groups,)),
            dma((2 * HALVES,)), dma((2 * HALVES,)),
            dma((HALVES, groups)), dma((HALVES, groups)),
            dma((groups + slabs,)), dma((groups + slabs,)),
        ]
        + stage_sems(sizes)
        + stage_scratch(sizes, ORDER_A, (share, cut))
        + stage_sems(sizes)
        + stage_scratch(sizes, ORDER_B, (share, K - cut))
        + stage_sems(flat)
        + stage_scratch(flat, ORDER_D, d_piece),
        compiler_params=pltpu.CompilerParams(
            collective_id=1, has_side_effects=True, vmem_limit_bytes=63 * 1024 * 1024
        ),
    )(cells, mask, subspace, turned, weights)


def close_kernel(rows_here, masked, a_hbm, b_hbm, data_hbm, scale_hbm, new_hbm, gram_ref,
                 out_hbm, held, a_ref, b_ref, data_ref, scale_ref, wide, turned, low, sem):
    first = lax.axis_index("grp") * rows_here
    data_rows, order_rows = data_ref.shape
    parts = 5
    chunk = K // parts
    fetches = [
        pltpu.make_async_copy(
            new_hbm.at[pl.ds(part * chunk, chunk)], held.at[part], sem.at[part]
        )
        for part in range(parts)
    ]
    copies = [
        pltpu.make_async_copy(
            held.at[part], out_hbm.at[pl.ds(part * chunk, chunk)], sem.at[parts + part]
        )
        for part in range(parts)
    ]
    loads = [
        pltpu.make_async_copy(source, target, sem.at[2 * parts + number])
        for number, (source, target) in enumerate(
            ((data_hbm, data_ref), (scale_hbm, scale_ref), (a_hbm, a_ref), (b_hbm, b_ref))
        )
    ]
    for copy in loads + fetches:
        copy.start()
    for copy in loads:
        copy.wait()

    def rows_from(ref, start):
        size = -(-rows_here // 8) * 8 + 8
        held = ref[pl.ds(pl.multiple_of(start // 8 * 8, 8), size)]
        return pltpu.roll(held, lax.rem(size - lax.rem(start, 8), size), 0)[:rows_here]

    window = turned.shape[0]
    data = data_ref[...].astype(jnp.float32)
    wide[:, :order_rows] = data
    begin = pl.multiple_of(first // RUN * RUN, RUN)
    turned[...] = wide[:, pl.ds(begin, window)].T
    for fetch, copy in zip(fetches, copies):
        fetch.wait()
        copy.start()
    right = rows_from(turned, first - begin)
    low[:rows_here] = jnp.zeros((rows_here, K), jnp.float32)
    rest = low.shape[0] - rows_here - data_rows
    low[rows_here + data_rows :] = jnp.zeros((rest, K), jnp.float32)
    low[rows_here : rows_here + data_rows] = data[:, :K]
    below = rows_from(low, jnp.maximum(first - K + rows_here, 0))

    half = data_rows // 2
    scales = scale_ref[:, :1]

    def scale_of(index):
        return jnp.where(
            index < K, 1.0, jnp.where(index < K + half, scales[0:1], scales[1:2])
        )

    row = scale_of(lax.broadcasted_iota(jnp.int32, (rows_here, 1), 0) + first)
    row = row * (1.0 / masked)
    column = scale_of(lax.broadcasted_iota(jnp.int32, (1, data_rows), 1) + K)
    cut = a_ref.shape[1]
    gram_ref[:, :cut] = (a_ref[...].astype(jnp.float32)[:rows_here] + below[:, :cut]) * row
    gram_ref[:, cut:K] = (b_ref[...].astype(jnp.float32)[:rows_here] + below[:, cut:]) * row
    gram_ref[:, K:] = right * (row * column)
    for copy in copies:
        copy.wait()


def close_up(rows_a, rows_b, data, scales, new_subspace, rows_here, masked):
    vmem = pl.BlockSpec(memory_space=pltpu.VMEM)
    hbm = pl.BlockSpec(memory_space=pl.ANY)
    data_rows, order_rows = data.shape
    window = -(-(rows_here + RUN) // RUN) * RUN
    wide = (order_rows // RUN) * RUN + window
    return pl.pallas_call(
        functools.partial(close_kernel, rows_here, masked),
        out_shape=(
            jax.ShapeDtypeStruct((rows_here, order_rows), jnp.float32),
            jax.ShapeDtypeStruct(new_subspace.shape, new_subspace.dtype),
        ),
        in_specs=[hbm] * 5,
        out_specs=(vmem, hbm),
        scratch_shapes=[
            pltpu.VMEM((5, K // 5, new_subspace.shape[1]), new_subspace.dtype),
            pltpu.VMEM(rows_a.shape, rows_a.dtype),
            pltpu.VMEM(rows_b.shape, rows_b.dtype),
            pltpu.VMEM(data.shape, data.dtype),
            pltpu.VMEM(scales.shape, scales.dtype),
            pltpu.VMEM((data_rows, wide), jnp.float32),
            pltpu.VMEM((window, data_rows), jnp.float32),
            pltpu.VMEM((2 * rows_here + data_rows + 16, K), jnp.float32),
            pltpu.SemaphoreType.DMA((14,)),
        ],
        compiler_params=pltpu.CompilerParams(vmem_limit_bytes=62 * 1024 * 1024),
    )(rows_a, rows_b, data, scales, new_subspace)


def body(raw_frames, mask_index, subspace, rotation):
    frames_here, slab_depth, extent = raw_frames.shape
    per_device = subspace.shape[1]
    group_count = lax.axis_size("grp")
    slab_count = lax.axis_size("slab")
    sizes = axes_of(group_count, slab_count)
    masked = per_device * slab_count * group_count
    frame_count = frames_here * group_count
    order_rows = K + frame_count
    rows_here = order_rows // group_count
    share = -(-rows_here // (16 * slab_count)) * 16

    rows_a, rows_b, data, scales, new_subspace = run_group(
        raw_frames.transpose(1, 0, 2), mask_index.reshape(-1, RUN), subspace, rotation.T,
        jnp.asarray(plane_weights()), sizes, masked, rows_here, share,
    )
    return close_up(
        rows_a.reshape(share * slab_count, -1), rows_b.reshape(share * slab_count, -1),
        data.reshape(frame_count, order_rows), scales, new_subspace, rows_here, masked,
    )


def solution(mesh):
    placed = (P("grp", "slab", None), P(("slab", "grp")), P(None, ("slab", "grp")), P())
    return jax.shard_map(
        body,
        mesh=mesh,
        in_specs=placed,
        out_specs=(P("grp", None), P(None, ("slab", "grp"))),
        check_vma=False,
    )
```

```python
import functools
import math

import jax
import jax.numpy as jnp
import numpy as np
from jax import lax
from jax.experimental import pallas as pl
from jax.experimental.pallas import tpu as pltpu
from jax.sharding import PartitionSpec as P

NX = 96
RUN = 128
RAD = 3
K = 1200
MESH = pl.DeviceIdType.MESH

smooth_sigma = 1.0617
epsilon = 1e-06

WIDE = 2 * RUN
LEFT = 3 * RUN
SPAN = 8 * RUN


def tap_weights():
    unscaled = [
        math.exp(-offset * offset / (2.0 * smooth_sigma * smooth_sigma))
        for offset in range(-RAD, RAD + 1)
    ]
    summed = sum(unscaled)
    return [weight / summed for weight in unscaled]


def plane_weights():
    taps = np.array(tap_weights())
    kinds = NX // math.gcd(WIDE, NX)
    out = np.zeros((kinds, SPAN, WIDE))
    for kind in range(kinds):
        target = np.arange(WIDE)
        column = (kind * WIDE + target) % NX
        for dy in range(-RAD, RAD + 1):
            for dx in range(-RAD, RAD + 1):
                inside = (column + dx >= 0) & (column + dx < NX)
                source = target + LEFT + dy * NX + dx
                out[kind, source[inside], target[inside]] = taps[dy + RAD] * taps[dx + RAD]
    return out.astype(jnp.bfloat16)


def axes_of(groups, slabs):
    outer = 4 if groups % 4 == 0 else 1
    cores = 2 if slabs % 2 == 0 else 1
    return outer, groups // outer, slabs // cores, cores


class Grid:
    def __init__(self, sizes, planes):
        self.full, self.planes = sizes, planes
        z, y, x, cores = sizes
        self.sizes = (z, y * x, cores) if planes else tuple(sizes)

    def here(self):
        _, ys, xs, cores = self.full
        slab, grp = lax.axis_index("slab"), lax.axis_index("grp")
        z, y, x, core = grp // ys, lax.rem(grp, ys), slab // cores, lax.rem(slab, cores)
        return [z, y * xs + x, core] if self.planes else [z, y, x, core]

    def device(self, at):
        _, ys, xs, cores = self.full
        if self.planes:
            at = [at[0], at[1] // xs, lax.rem(at[1], xs), at[2]]
        return (at[2] * cores + at[3], at[0] * ys + at[1])

    def moved(self, at, axis, step):
        other = lax.rem(at[axis] + step, self.sizes[axis])
        return at[:axis] + [other] + at[axis + 1 :], other


class Scatter:
    def __init__(self, grid, axis, left, src, landed, out, sems):
        self.grid, self.axis, self.src, self.landed, self.out = grid, axis, src, landed, out
        self.sizes = grid.sizes
        self.dim = left.index(axis)
        self.left = [other for other in left if other != axis]
        self.send_sem, self.recv_sem = sems
        self.at = grid.here()

    def part(self, where):
        return self.src.at[(slice(None),) * self.dim + (where,)]

    def copy(self, step):
        there, other = self.grid.moved(self.at, self.axis, step)
        return pltpu.make_async_remote_copy(
            src_ref=self.part(other),
            dst_ref=self.landed.at[step - 1],
            send_sem=self.send_sem.at[self.axis, step],
            recv_sem=self.recv_sem.at[self.axis, step],
            device_id=self.grid.device(there),
            device_id_type=MESH,
        )

    def start(self):
        for step in range(1, self.sizes[self.axis]):
            self.copy(step).start()

    def finish(self):
        for step in range(1, self.sizes[self.axis]):
            self.copy(step).wait()
        mine = self.part(self.at[self.axis])
        lead = [self.sizes[axis] for axis in self.left]
        total = math.prod(lead)

        def add(index, _):
            where = []
            for size in reversed(lead):
                where.insert(0, lax.rem(index, size))
                index = index // size
            where = tuple(where)
            value = mine[where].astype(jnp.float32)
            for step in range(self.sizes[self.axis] - 1):
                value = value + self.landed[(step,) + where].astype(jnp.float32)
            self.out[where] = value.astype(self.out.dtype)
            return 0

        lax.fori_loop(0, total, add, 0)


class Gather:
    def __init__(self, grid, axis, done, full, first, sems):
        self.grid, self.sizes, self.axis, self.full = grid, grid.sizes, axis, full
        self.send_sem, self.recv_sem = sems
        self.at = grid.here()
        self.where = tuple(
            slice(None) if other in done else self.at[other] for other in range(first, len(self.sizes))
        )

    def copy(self, step):
        there, _ = self.grid.moved(self.at, self.axis, step)
        return pltpu.make_async_remote_copy(
            src_ref=self.full.at[self.where],
            dst_ref=self.full.at[self.where],
            send_sem=self.send_sem.at[self.axis, step],
            recv_sem=self.recv_sem.at[self.axis, step],
            device_id=self.grid.device(there),
            device_id_type=MESH,
        )

    def start(self):
        for step in range(1, self.sizes[self.axis]):
            self.copy(step).start()

    def finish(self):
        for step in range(1, self.sizes[self.axis]):
            self.copy(step).wait()


def gather_stages(grid, order, full, first, sems):
    stages, done = [], []
    for axis in order:
        if grid.sizes[axis] > 1:
            stages.append(Gather(grid, axis, list(done), full, first, sems))
        done.append(axis)
    return stages


def stage_scratch(sizes, order, piece):
    out = []
    left = [axis for axis in range(len(sizes)) if sizes[axis] > 1]
    for axis in order:
        if sizes[axis] == 1:
            continue
        left.remove(axis)
        shape = tuple(sizes[other] for other in left) + piece
        out.append(pltpu.VMEM((sizes[axis] - 1,) + shape, jnp.bfloat16))
        if left:
            out.append(pltpu.VMEM(shape, jnp.bfloat16))
    return out


def stage_sems(sizes):
    most = max(sizes)
    return [pltpu.SemaphoreType.DMA((4, most)) for _ in range(4)]


def scatter_stages(grid, order, src, bufs, result, sems):
    stages, sizes = [], grid.sizes
    left = list(range(len(sizes)))
    for axis in order:
        if sizes[axis] == 1:
            src = src.at[(slice(None),) * left.index(axis) + (0,)]
            left = [other for other in left if other != axis]
    order = [axis for axis in order if sizes[axis] > 1]
    for number, axis in enumerate(order):
        last = number == len(order) - 1
        out = result if last else bufs[2 * number + 1]
        stages.append(Scatter(grid, axis, left, src, bufs[2 * number], out, sems))
        left = stages[-1].left
        src = out
    return stages


def place(peer, groups):
    return (peer // groups, lax.rem(peer, groups))


def group_kernel(dims, x_hbm, mask_ref, s_hbm, r_hbm, w_hbm,
                 rows_a, rows_b, data_ref, scale_ref, new_hbm,
                 stacked, gram_a, gram_b, dpart, up_ref, down_ref, below, above, picked_ref,
                 regrouped, starts, starts_at, power_at, power_sum, w_ref,
                 load_sem, mask_send, mask_recv, rim_send, rim_recv, halo_send, halo_recv,
                 all_send, all_recv, p_send, p_recv, *bufs):
    sizes, cut, depth, frames, extent, runs, share, masked, rows_here = dims
    groups, slabs = sizes[0] * sizes[1], sizes[2] * sizes[3]
    total = groups * slabs
    slab, grp = lax.axis_index("slab"), lax.axis_index("grp")
    me = slab * groups + grp
    grid, planes = Grid(sizes, False), Grid(sizes, True)
    at, plane_at = grid.here(), planes.here()
    bufs = list(bufs)
    upper = lax.rem(slab + 1, slabs)
    lower = lax.rem(slab + slabs - 1, slabs)
    own = runs * groups
    rim_groups = groups * RAD // depth
    rim = rim_groups * runs
    places = extent // RUN
    padded = depth + RAD
    taps = tap_weights()
    data_rows = frames * groups
    order_rows = K + data_rows
    half_rows = data_rows // 2
    some = frames // HALVES
    across = (((1,), (1,)), ((), ()))

    load_s = pltpu.make_async_copy(s_hbm, stacked.at[pl.ds(0, K)], load_sem.at[1])
    load_w = pltpu.make_async_copy(w_hbm, w_ref, load_sem.at[2])

    barrier = pltpu.get_barrier_semaphore()

    def greet(step, _):
        pl.semaphore_signal(
            barrier, inc=1, device_id=place(lax.rem(me + step, total), groups),
            device_id_type=MESH,
        )
        return 0

    def trade_starts(step):
        return pltpu.make_async_remote_copy(
            src_ref=starts.at[grp], dst_ref=starts.at[grp],
            send_sem=mask_send.at[step], recv_sem=mask_recv.at[step],
            device_id=(slab, lax.rem(grp + step, groups)), device_id_type=MESH,
        )

    def rim_starts(side, there, number, to):
        slot = groups + side * rim_groups + number
        return pltpu.make_async_remote_copy(
            src_ref=starts.at[grp], dst_ref=starts.at[slot],
            send_sem=rim_send.at[to], recv_sem=rim_recv.at[side * rim_groups + number],
            device_id=(there, to), device_id_type=MESH,
        )

    def for_peers(action):
        def one(step, _):
            action(step)
            return 0

        lax.fori_loop(1, groups, one, 0)

    def for_rim(action):
        def one(to, _):
            @pl.when(grp < rim_groups)
            def _():
                action(rim_starts(0, lower, grp, to))

            @pl.when(grp >= groups - rim_groups)
            def _():
                action(rim_starts(1, upper, grp - (groups - rim_groups), to))

            return 0

        lax.fori_loop(0, groups, one, 0)

    def send_starts():
        lane = lax.broadcasted_iota(jnp.int32, (1, RUN), 1)
        first = jnp.zeros((1, RUN), jnp.int32)
        for run in range(runs):
            first = jnp.where(lane == run, mask_ref[run : run + 1, :] - run, first)
        cell = lax.shift_right_arithmetic(first, 7) - slab * (depth * places)
        plane = jnp.zeros((1, RUN), jnp.int32)
        for number in range(1, depth):
            plane = plane + jnp.where(cell >= number * places, 1, 0)
        row = (cell - plane * places) * padded + plane
        row = jnp.minimum(jnp.maximum(row, 0), (places - 1) * padded + depth - 1)
        starts[grp] = jnp.where(lane < runs, row, 0)
        for_peers(lambda step: trade_starts(step).start())
        for_rim(lambda copy: copy.start())

    def await_starts():
        for_peers(lambda step: trade_starts(step).wait())
        for_rim(lambda copy: copy.wait_send())
        for number in range(rim_groups):
            rim_starts(0, lower, number, grp).wait_recv()
            rim_starts(1, upper, number, grp).wait_recv()
        copy = pltpu.make_async_copy(starts, starts_at, load_sem.at[0])
        copy.start()
        copy.wait()

    def halo(src, dst, number, other):
        return pltpu.make_async_remote_copy(
            src_ref=src, dst_ref=dst, send_sem=halo_send.at[number], recv_sem=halo_recv.at[number],
            device_id=(other, grp), device_id_type=MESH,
        )

    halos_up = [halo(up_ref.at[h], below.at[h], h, upper) for h in range(HALVES)]
    halos_down = [halo(down_ref.at[h], above.at[h], HALVES + h, lower) for h in range(HALVES)]

    def trade(h, step):
        other = lax.rem(grp + step, groups)
        return pltpu.make_async_remote_copy(
            src_ref=picked_ref.at[h, pl.ds(other * runs, runs)], dst_ref=regrouped.at[grp, h],
            send_sem=all_send.at[h, step], recv_sem=all_recv.at[h, step],
            device_id=(slab, other), device_id_type=MESH,
        )

    def start_trades(h, at_rim):
        for step in range(1, groups):
            other = lax.rem(grp + step, groups)
            inside = (other >= rim_groups) & (other < groups - rim_groups)
            pl.when(jnp.logical_not(inside) if at_rim else inside)(trade(h, step).start)

    def take(count):
        taken = bufs[:count]
        del bufs[:count]
        return taken

    def chain(grid, order, back, src, full, first, piece):
        sems = take(4)
        scratch = take(len(stage_scratch(grid.sizes, order, piece)))
        where = tuple((plane_at if grid.planes else at)[first:])
        return scatter_stages(grid, order, src, scratch, full.at[where], sems[:2]) + gather_stages(
            grid, back, full, first, sems[2:]
        )

    a_steps = chain(grid, ORDER_A, (2, 3), gram_a, rows_a, 2, (share, cut))
    b_steps = chain(grid, ORDER_B, (2, 3), gram_b, rows_b, 2, (share, K - cut))
    d_steps = chain(planes, ORDER_D, (0, 1, 2), dpart, data_ref, 0, dpart.shape[3:])

    def advance(steps):
        if steps:
            steps.pop(0).finish()
        if steps:
            steps[0].start()

    def basis_gram(gram, low_column, high_column):
        width = high_column - low_column
        used = [group for group in range(groups) if group * rows_here < K]
        top = -(-(used[-1] * rows_here + slabs * share) // 16) * 16
        found = lax.dot_general(
            stacked[:top], stacked[low_column:high_column], across,
            preferred_element_type=jnp.float32,
        )
        for group in range(groups):
            where = (group // sizes[1], group % sizes[1])
            for number in range(slabs):
                begin = group * rows_here + number * share
                gram[where + (number // sizes[3], number % sizes[3])] = (
                    found[begin : begin + share]
                    if group in used
                    else jnp.zeros((share, width), jnp.float32)
                ).astype(gram.dtype)

    def smooth(x_ref, y_ref):
        load_x = pltpu.make_async_copy(
            x_hbm, x_ref.at[:, :, pl.ds(LEFT, extent)], load_sem.at[3]
        )
        load_s.start()
        load_x.start()
        load_w.start()
        lax.fori_loop(1, total, greet, 0)
        right = x_ref.shape[2] - LEFT - extent
        x_ref[:, :, :LEFT] = jnp.zeros((depth, frames, LEFT), x_ref.dtype)
        x_ref[:, :, LEFT + extent :] = jnp.zeros((depth, frames, right), x_ref.dtype)
        rest = stacked.shape[0] - K
        stacked[K:] = jnp.zeros((rest, stacked.shape[1]), stacked.dtype)

        def blank(number, _):
            for h in range(HALVES):
                y_ref[h, pl.ds(number * padded, RAD)] = jnp.zeros((RAD, some, RUN), jnp.float32)
            return 0

        lax.fori_loop(0, places + 1, blank, 0)
        load_s.wait()
        basis_gram(gram_a, 0, cut)
        pl.semaphore_wait(barrier, total - 1)
        a_steps[0].start()
        send_starts()
        load_w.wait()
        load_x.wait()
        kinds = w_ref.shape[0]

        blocks = 2
        steps = extent // (WIDE * kinds * blocks)

        def planar(h, block):
            def one(kind, _):
                numbers = [(block * steps + step) * kinds + kind for step in range(steps)]
                cells = [
                    x_ref[
                        :, h * some : (h + 1) * some, pl.ds(pl.multiple_of(at * WIDE, WIDE), SPAN)
                    ].reshape(depth * some, SPAN)
                    for at in numbers
                ]
                found = jnp.dot(
                    jnp.concatenate(cells, 0), w_ref[kind], preferred_element_type=jnp.float32
                )
                found = found.reshape(steps, depth, some, WIDE)
                for step, number in enumerate(numbers):
                    for side in range(2):
                        y_ref[h, pl.ds((2 * number + side) * padded + RAD, depth)] = found[
                            step, :, :, side * RUN : (side + 1) * RUN
                        ]
                return 0

            lax.fori_loop(0, kinds, one, 0)

        def pick(h, slot, run, shift, used):
            row = starts_at[slot, 0, run]
            if shift > 0:
                row = jnp.minimum(row + shift, places * padded)
            if shift < 0:
                row = jnp.maximum(row + shift, -(RAD + 1))
            found = None
            for tap in used:
                term = taps[tap] * y_ref[h, row + tap]
                found = term if found is None else found + term
            return found

        def over(count, action):
            def one(number, _):
                for run in range(runs):
                    action(number, run)
                return 0

            lax.fori_loop(0, count, one, 0)

        every = range(2 * RAD + 1)
        low_part = jnp.where(slab > 0, 1.0, 0.0)
        high_part = jnp.where(slab < slabs - 1, 1.0, 0.0)

        def pick_halos(h):
            def one_up(number, run):
                up_ref[h, number * runs + run] = pick(
                    h, groups + number, run, depth, range(RAD)
                ).astype(up_ref.dtype)

            def one_down(number, run):
                down_ref[h, number * runs + run] = pick(
                    h, groups + rim_groups + number, run, -depth, range(RAD + 1, 2 * RAD + 1)
                ).astype(down_ref.dtype)

            over(rim_groups, one_up)
            halos_up[h].start()
            over(rim_groups, one_down)
            halos_down[h].start()

        def pick_inner(h):
            def one(number, run):
                slot = number + rim_groups
                picked_ref[h, slot * runs + run] = pick(h, slot, run, 0, every).astype(
                    picked_ref.dtype
                )

            over(groups - 2 * rim_groups, one)
            start_trades(h, False)

        def pick_edges(h):
            halos_up[h].wait()
            halos_down[h].wait()

            def one(number, run):
                where = number * runs + run
                picked_ref[h, where] = (
                    pick(h, number, run, 0, every)
                    + low_part * below[h, where].astype(jnp.float32)
                ).astype(picked_ref.dtype)
                slot = number + groups - rim_groups
                picked_ref[h, slot * runs + run] = (
                    pick(h, slot, run, 0, every)
                    + high_part * above[h, where].astype(jnp.float32)
                ).astype(picked_ref.dtype)

            over(rim_groups, one)
            start_trades(h, True)

        planar(0, 0)
        advance(a_steps)
        planar(0, 1)
        await_starts()
        pick_halos(0)
        pick_inner(0)
        planar(1, 0)
        pick_edges(0)
        planar(1, 1)
        pick_halos(1)
        pick_inner(1)
        pick_edges(1)

    pl.run_scoped(
        smooth,
        pltpu.VMEM((depth, frames, extent + SPAN - WIDE), jnp.bfloat16),
        pltpu.VMEM((HALVES, places * padded + RAD, some, RUN), jnp.float32),
    )

    def finish(regrouped_rows):
        r_ref, out_ref = regrouped_rows
        load_r = pltpu.make_async_copy(r_hbm, r_ref, load_sem.at[4])
        load_r.start()
        for h in range(HALVES):
            regrouped[grp, h] = picked_ref[h, pl.ds(grp * runs, runs)]
        advance(a_steps)
        basis_gram(gram_b, cut, K)
        b_steps[0].start()
        advance(b_steps)
        advance(a_steps)
        for h in range(HALVES):
            for_peers(lambda step, h=h: trade(h, step).wait())

        half = groups // 2
        squares = [jnp.zeros((1, RUN), jnp.float32) for _ in range(2)]
        for run in range(runs):
            lanes = slice(run * RUN, (run + 1) * RUN)
            for subject in range(2):
                block = regrouped[subject * half : (subject + 1) * half, :, run]
                block = block.astype(jnp.float32)
                block = block.reshape(half * frames, RUN)
                mean = jnp.sum(block, axis=0, keepdims=True) * (1.0 / (half * frames))
                rounded = (block - mean).astype(stacked.dtype)
                begin = K + subject * half_rows
                stacked[begin : begin + half_rows, lanes] = rounded
                wide = rounded.astype(jnp.float32)
                squares[subject] = squares[subject] + jnp.sum(wide * wide, axis=0, keepdims=True)
        power_sum[0:1, :] = squares[0]
        power_sum[1:2, :] = squares[1]

        def share_power(axis, count, other):
            first = 0 if axis == 0 else groups

            def copy(step):
                return pltpu.make_async_remote_copy(
                    src_ref=power_sum, dst_ref=power_at.at[first + step],
                    send_sem=p_send.at[first + step], recv_sem=p_recv.at[first + step],
                    device_id=other(step), device_id_type=MESH,
                )

            def start():
                for step in range(1, count):
                    copy(step).start()

            def wait():
                found = power_sum[...]
                for step in range(1, count):
                    copy(step).wait()
                for step in range(1, count):
                    found = found + power_at[first + step]
                power_sum[...] = found

            return start, wait

        start_p, wait_p = share_power(0, groups, lambda step: (slab, lax.rem(grp + step, groups)))
        start_q, wait_q = share_power(1, slabs, lambda step: (lax.rem(slab + step, slabs), grp))
        start_p()

        found = lax.dot_general(
            stacked[K:order_rows], stacked[:order_rows], across,
            preferred_element_type=jnp.float32,
        )
        piece = data_rows // total
        for number in range(total):
            line, core = number // sizes[3], number % sizes[3]
            dpart[line // planes.sizes[1], line % planes.sizes[1], core] = found[
                number * piece : (number + 1) * piece
            ].astype(dpart.dtype)
        d_steps[0].start()
        wait_p()
        start_q()
        advance(d_steps)
        advance(a_steps)
        wait_q()
        power = jnp.sum(power_sum[...], axis=1, keepdims=True)
        scales = lax.rsqrt(power * (1.0 / (masked * half_rows)) + epsilon)
        scale_ref[...] = jnp.broadcast_to(scales, scale_ref.shape)

        load_r.wait()
        edge = K // RUN * RUN
        lane = lax.broadcasted_iota(jnp.int32, (1, order_rows - edge), 1) + edge
        factor = jnp.where(
            lane < K, 1.0, jnp.where(lane < K + half_rows, scales[0:1], scales[1:2])
        )
        r_ref[:, edge:] = (r_ref[:, edge:].astype(jnp.float32) * factor).astype(r_ref.dtype)

        chunk = out_ref.shape[1]
        copies = []

        def rotate(number):
            slot = number % 2
            if number >= 2:
                copies[number - 2].wait()
            rows = slice(number * chunk, (number + 1) * chunk)
            out_ref[slot] = jnp.dot(
                r_ref[rows], stacked[:order_rows], preferred_element_type=jnp.float32
            ).astype(out_ref.dtype)
            copy = pltpu.make_async_copy(
                out_ref.at[slot], new_hbm.at[pl.ds(number * chunk, chunk)], load_sem.at[5 + slot]
            )
            copy.start()
            copies.append(copy)

        count = K // chunk
        rotate(0)
        todo = list(range(1, count))
        while d_steps or a_steps or b_steps:
            for steps in (d_steps, a_steps, b_steps):
                advance(steps)
            if todo:
                rotate(todo.pop(0))
        while todo:
            rotate(todo.pop(0))
        for copy in copies[-2:]:
            copy.wait()

    pl.run_scoped(
        lambda r_ref, out_ref: finish((r_ref, out_ref)),
        pltpu.VMEM((K, order_rows), jnp.bfloat16),
        pltpu.VMEM((2, K // 5, runs * RUN), jnp.bfloat16),
    )


HALVES = 2
ORDER_A, ORDER_B, ORDER_D = (3, 1, 2, 0), (3, 2, 1, 0), (2, 1, 0)


def run_group(cells, mask, subspace, turned, weights, sizes, masked, rows_here, share):
    depth, frames, extent = cells.shape
    vmem = pl.BlockSpec(memory_space=pltpu.VMEM)
    hbm = pl.BlockSpec(memory_space=pl.ANY)
    groups, slabs = sizes[0] * sizes[1], sizes[2] * sizes[3]
    total = groups * slabs
    runs = mask.shape[0]
    own = groups * runs
    rim_groups = groups * RAD // depth
    rim = rim_groups * runs
    data_rows = frames * groups
    order_rows = K + data_rows
    cut = -(-K * 3 // (5 * RUN)) * RUN
    planes = Grid(sizes, True)
    flat = planes.sizes
    d_piece = (data_rows // total, order_rows)
    last = (groups - 1) * rows_here // 16 * 16 + slabs * share + 16
    stacked_rows = max(order_rows, last)
    some = frames // HALVES
    rim_shape = pltpu.VMEM((HALVES, rim, some, RUN), jnp.bfloat16)
    dma = pltpu.SemaphoreType.DMA
    dims = (sizes, cut, depth, frames, extent, runs, share, masked, rows_here)
    slots = groups + 2 * rim_groups
    return pl.pallas_call(
        functools.partial(group_kernel, dims),
        out_shape=(
            jax.ShapeDtypeStruct(tuple(sizes[2:]) + (share, cut), jnp.bfloat16),
            jax.ShapeDtypeStruct(tuple(sizes[2:]) + (share, K - cut), jnp.bfloat16),
            jax.ShapeDtypeStruct(tuple(flat) + d_piece, jnp.bfloat16),
            jax.ShapeDtypeStruct((2, RUN), jnp.float32),
            jax.ShapeDtypeStruct(subspace.shape, jnp.bfloat16),
        ),
        in_specs=[hbm, vmem, hbm, hbm, hbm],
        out_specs=(vmem, vmem, vmem, vmem, hbm),
        scratch_shapes=[
            pltpu.VMEM((stacked_rows, runs * RUN), jnp.bfloat16),
            pltpu.VMEM(tuple(sizes) + (share, cut), jnp.bfloat16),
            pltpu.VMEM(tuple(sizes) + (share, K - cut), jnp.bfloat16),
            pltpu.VMEM(tuple(flat) + d_piece, jnp.bfloat16),
            rim_shape, rim_shape, rim_shape, rim_shape,
            pltpu.VMEM((HALVES, own, some, RUN), jnp.bfloat16),
            pltpu.VMEM((groups, HALVES, runs, some, RUN), jnp.bfloat16),
            pltpu.VMEM((slots, 1, RUN), jnp.int32),
            pltpu.SMEM((slots, 1, RUN), jnp.int32),
            pltpu.VMEM((groups + slabs, 2, RUN), jnp.float32),
            pltpu.VMEM((2, RUN), jnp.float32),
            pltpu.VMEM(weights.shape, jnp.bfloat16),
            dma((7,)),
            dma((groups,)), dma((groups,)),
            dma((groups,)), dma((2 * rim_groups,)),
            dma((2 * HALVES,)), dma((2 * HALVES,)),
            dma((HALVES, groups)), dma((HALVES, groups)),
            dma((groups + slabs,)), dma((groups + slabs,)),
        ]
        + stage_sems(sizes)
        + stage_scratch(sizes, ORDER_A, (share, cut))
        + stage_sems(sizes)
        + stage_scratch(sizes, ORDER_B, (share, K - cut))
        + stage_sems(flat)
        + stage_scratch(flat, ORDER_D, d_piece),
        compiler_params=pltpu.CompilerParams(
            collective_id=1, has_side_effects=True, vmem_limit_bytes=63 * 1024 * 1024
        ),
    )(cells, mask, subspace, turned, weights)


def close_kernel(rows_here, masked, a_hbm, b_hbm, data_hbm, scale_hbm, new_hbm, gram_ref,
                 out_hbm, held, a_ref, b_ref, data_ref, scale_ref, wide, turned, low, sem):
    first = lax.axis_index("grp") * rows_here
    data_rows, order_rows = data_ref.shape
    parts = 5
    chunk = K // parts
    fetches = [
        pltpu.make_async_copy(
            new_hbm.at[pl.ds(part * chunk, chunk)], held.at[part], sem.at[part]
        )
        for part in range(parts)
    ]
    copies = [
        pltpu.make_async_copy(
            held.at[part], out_hbm.at[pl.ds(part * chunk, chunk)], sem.at[parts + part]
        )
        for part in range(parts)
    ]
    loads = [
        pltpu.make_async_copy(source, target, sem.at[2 * parts + number])
        for number, (source, target) in enumerate(
            ((data_hbm, data_ref), (scale_hbm, scale_ref), (a_hbm, a_ref), (b_hbm, b_ref))
        )
    ]
    for copy in loads + fetches:
        copy.start()
    for copy in loads:
        copy.wait()

    def rows_from(ref, start):
        size = -(-rows_here // 8) * 8 + 8
        held = ref[pl.ds(pl.multiple_of(start // 8 * 8, 8), size)]
        return pltpu.roll(held, lax.rem(size - lax.rem(start, 8), size), 0)[:rows_here]

    window = turned.shape[0]
    data = data_ref[...].astype(jnp.float32)
    wide[:, :order_rows] = data
    begin = pl.multiple_of(first // RUN * RUN, RUN)
    turned[...] = wide[:, pl.ds(begin, window)].T
    for fetch, copy in zip(fetches, copies):
        fetch.wait()
        copy.start()
    right = rows_from(turned, first - begin)
    low[:rows_here] = jnp.zeros((rows_here, K), jnp.float32)
    rest = low.shape[0] - rows_here - data_rows
    low[rows_here + data_rows :] = jnp.zeros((rest, K), jnp.float32)
    low[rows_here : rows_here + data_rows] = data[:, :K]
    below = rows_from(low, jnp.maximum(first - K + rows_here, 0))

    half = data_rows // 2
    scales = scale_ref[:, :1]

    def scale_of(index):
        return jnp.where(
            index < K, 1.0, jnp.where(index < K + half, scales[0:1], scales[1:2])
        )

    row = scale_of(lax.broadcasted_iota(jnp.int32, (rows_here, 1), 0) + first)
    row = row * (1.0 / masked)
    column = scale_of(lax.broadcasted_iota(jnp.int32, (1, data_rows), 1) + K)
    cut = a_ref.shape[1]
    gram_ref[:, :cut] = (a_ref[...].astype(jnp.float32)[:rows_here] + below[:, :cut]) * row
    gram_ref[:, cut:K] = (b_ref[...].astype(jnp.float32)[:rows_here] + below[:, cut:]) * row
    gram_ref[:, K:] = right * (row * column)
    for copy in copies:
        copy.wait()


def close_up(rows_a, rows_b, data, scales, new_subspace, rows_here, masked):
    vmem = pl.BlockSpec(memory_space=pltpu.VMEM)
    hbm = pl.BlockSpec(memory_space=pl.ANY)
    data_rows, order_rows = data.shape
    window = -(-(rows_here + RUN) // RUN) * RUN
    wide = (order_rows // RUN) * RUN + window
    return pl.pallas_call(
        functools.partial(close_kernel, rows_here, masked),
        out_shape=(
            jax.ShapeDtypeStruct((rows_here, order_rows), jnp.float32),
            jax.ShapeDtypeStruct(new_subspace.shape, new_subspace.dtype),
        ),
        in_specs=[hbm] * 5,
        out_specs=(vmem, hbm),
        scratch_shapes=[
            pltpu.VMEM((5, K // 5, new_subspace.shape[1]), new_subspace.dtype),
            pltpu.VMEM(rows_a.shape, rows_a.dtype),
            pltpu.VMEM(rows_b.shape, rows_b.dtype),
            pltpu.VMEM(data.shape, data.dtype),
            pltpu.VMEM(scales.shape, scales.dtype),
            pltpu.VMEM((data_rows, wide), jnp.float32),
            pltpu.VMEM((window, data_rows), jnp.float32),
            pltpu.VMEM((2 * rows_here + data_rows + 16, K), jnp.float32),
            pltpu.SemaphoreType.DMA((14,)),
        ],
        compiler_params=pltpu.CompilerParams(vmem_limit_bytes=62 * 1024 * 1024),
    )(rows_a, rows_b, data, scales, new_subspace)


def body(raw_frames, mask_index, subspace, rotation):
    frames_here, slab_depth, extent = raw_frames.shape
    per_device = subspace.shape[1]
    group_count = lax.axis_size("grp")
    slab_count = lax.axis_size("slab")
    sizes = axes_of(group_count, slab_count)
    masked = per_device * slab_count * group_count
    frame_count = frames_here * group_count
    order_rows = K + frame_count
    rows_here = order_rows // group_count
    share = -(-rows_here // (16 * slab_count)) * 16

    rows_a, rows_b, data, scales, new_subspace = run_group(
        raw_frames.transpose(1, 0, 2), mask_index.reshape(-1, RUN), subspace, rotation.T,
        jnp.asarray(plane_weights()), sizes, masked, rows_here, share,
    )
    return close_up(
        rows_a.reshape(share * slab_count, -1), rows_b.reshape(share * slab_count, -1),
        data.reshape(frame_count, order_rows), scales, new_subspace, rows_here, masked,
    )


def solution(mesh):
    placed = (P("grp", "slab", None), P(("slab", "grp")), P(None, ("slab", "grp")), P())
    return jax.shard_map(
        body,
        mesh=mesh,
        in_specs=placed,
        out_specs=(P("grp", None), P(None, ("slab", "grp"))),
        check_vma=False,
    )
```
